32 devices in a mesh: crop: 1, res: 32 (over z, y, x, core).
Axes of the slice: x: 2, y: 2, z: 4, core: 2. Of those that a mesh axis runs over, the one named last changes fastest.
Arguments:
- homolog_symbol_ids: int32 [64, 128], P(('crop', 'res')), may hold values from 0 to 22
- residue_attend_mask: int32 [128], P('crop'), may hold values 0 or 1
- alignment_state: bfloat16 [64, 128, 256], P(('crop', 'res')), may hold values from -6 to 6
- pair: bfloat16 [128, 128, 128], P(('crop', 'res')), may hold values from -6 to 6
- symbol_lookup_matrix: bfloat16 [23, 256], replicated, may hold values from -3 to 3
- pair_bias_weight: bfloat16 [128, 8], replicated, may hold values from -0.5 to 0.5
- row_projection_weight: bfloat16 [256, 1024], replicated, may hold values from -8 to 8
- horizontal_readout_matrix: bfloat16 [256, 256], replicated, may hold values from -0.375 to 0.375
- column_projection_weight: bfloat16 [256, 1024], replicated, may hold values from -8 to 8
- vertical_readout_matrix: bfloat16 [256, 256], replicated, may hold values from -0.375 to 0.375
- product_factor_matrices: bfloat16 [256, 64], replicated, may hold values from -0.375 to 0.375
- outer_output_weight: bfloat16 [1024, 128], replicated, may hold values from -1.5 to 1.5
- triangle_input_weight: bfloat16 [128, 640], replicated, may hold values from -0.5 to 0.5
- triangle_output_weight: bfloat16 [128, 128], replicated, may hold values from -0.5 to 0.5
Outputs:
- alignment_output: bfloat16 [64, 128, 256], P('crop', 'res')
- pair_output: bfloat16 [128, 128, 128], P(('crop', 'res'))
The draws below stay inside these ranges and needn't reach their ends.
All inputs are finite; a program needn't handle non-finite values.
Results may differ from the reference program's by a relative error of at most 0.013.
Values may be sent and summed in bfloat16 or wider, within the bound.
A program may use at most 64 MiB of HBM per device.

```python
import jax
import jax.numpy as jnp
from jax import lax

FEATURE_DEPTH = 256
CZ = 128
HEAD_NUMBER = 8
PRODUCT_WIDTH = 32
AMINO_VOCAB = 23
HOMOLOG_NUMBER = 64
CHAIN_LENGTH = 128


def draw_alignment_state(key, part):
    random_seed_primary = jax.random.fold_in(jax.random.fold_in(key, 3), 0)
    lower_bound_index = jax.random.normal(random_seed_primary, (HOMOLOG_NUMBER, CHAIN_LENGTH, FEATURE_DEPTH), jnp.float32)
    return jnp.clip(lower_bound_index, -6.0, 6.0).astype(jnp.bfloat16)


def draw_projection(key, channels):
    weight = jnp.clip(jax.random.normal(key, (channels, 4 * channels), jnp.float32), -4.0, 4.0) * channels ** (-0.5)
    return weight.astype(jnp.bfloat16)


def draw_row_projection_weight(key, part):
    return draw_projection(jax.random.fold_in(key, 11), FEATURE_DEPTH)


def draw_column_projection_weight(key, part):
    return draw_projection(jax.random.fold_in(key, 29), FEATURE_DEPTH)


def touch_ends(result, key, smallest, high):
    extent = result.shape
    place = [jax.random.randint(jax.random.fold_in(key, axis), (), 0, extent[axis]) for axis in range(len(extent))]
    result = result.at[tuple(place)].set(smallest)
    longest = extent.index(max(extent))
    place[longest] = (place[longest] + 1) % extent[longest]
    return result.at[tuple(place)].set(high)


def shard_levels(key, shape, pieces, smallest, largest):
    factor_of, own = 1.0, jax.random.fold_in(key, 6)
    for position, blocks in pieces:
        heights = jnp.exp(jax.random.uniform(jax.random.fold_in(own, position), (blocks,), jnp.float32, smallest / len(pieces), largest / len(pieces)))
        factor_of = factor_of * jnp.repeat(heights, shape[position] // blocks).reshape([-1 if axis == position else 1 for axis in range(len(shape))])
    return factor_of


def bell_draw(key, extent, scale, reach, cuts=(), kind=jnp.bfloat16):
    loudness = shard_levels(key, extent, cuts, -0.22, 0.18) if cuts else 1.0
    entries = jax.random.normal(key, extent, jnp.float32) * scale * loudness
    return jnp.minimum(jnp.maximum(entries, -reach), reach).astype(kind)


def setup_inputs(seed: int = 0, part: int = 0) -> dict:
    seeds = jax.random.split(jax.random.key(seed), 15)
    part_keys = jax.random.split(jax.random.fold_in(seeds[14], part), 15)
    homolog_symbol_ids = touch_ends(jax.random.randint(part_keys[0], (HOMOLOG_NUMBER, CHAIN_LENGTH), 0, AMINO_VOCAB), jax.random.fold_in(part_keys[0], 1), 0, AMINO_VOCAB - 1).astype(jnp.int32)
    residue_attend_mask = touch_ends((jax.random.randint(part_keys[1], (CHAIN_LENGTH,), 0, 8) < 7).astype(jnp.int32), jax.random.fold_in(part_keys[1], 1), 0, 1)
    alignment_state = draw_alignment_state(jax.random.fold_in(jax.random.fold_in(seeds[14], part), 71), part)
    pair = bell_draw(part_keys[3], (CHAIN_LENGTH, CHAIN_LENGTH, CZ), 1.0, 6.0, ((0, 32),))
    symbol_lookup_matrix = bell_draw(seeds[4], (AMINO_VOCAB, FEATURE_DEPTH), 0.5, 3.0)
    pair_bias_weight = bell_draw(seeds[5], (CZ, HEAD_NUMBER), CZ ** -0.5, 0.5)
    row_projection_weight = draw_row_projection_weight(jax.random.fold_in(seeds[14], 71), part)
    horizontal_readout_matrix = bell_draw(seeds[7], (FEATURE_DEPTH, FEATURE_DEPTH), FEATURE_DEPTH ** -0.5, 0.375)
    column_projection_weight = draw_column_projection_weight(jax.random.fold_in(seeds[14], 71), part)
    vertical_readout_matrix = bell_draw(seeds[9], (FEATURE_DEPTH, FEATURE_DEPTH), FEATURE_DEPTH ** -0.5, 0.375)
    product_factor_matrices = bell_draw(seeds[10], (FEATURE_DEPTH, 2 * PRODUCT_WIDTH), FEATURE_DEPTH ** -0.5, 0.375)
    outer_output_weight = bell_draw(seeds[11], (PRODUCT_WIDTH * PRODUCT_WIDTH, CZ), (PRODUCT_WIDTH * PRODUCT_WIDTH // 64) ** -0.5, 1.5)
    triangle_input_weight = bell_draw(seeds[12], (CZ, 5 * CZ), CZ ** -0.5, 0.5)
    triangle_output_weight = bell_draw(seeds[13], (CZ, CZ), CZ ** -0.5, 0.5)
    return dict(homolog_symbol_ids=homolog_symbol_ids, residue_attend_mask=residue_attend_mask, alignment_state=alignment_state, pair=pair, symbol_lookup_matrix=symbol_lookup_matrix, pair_bias_weight=pair_bias_weight, row_projection_weight=row_projection_weight, horizontal_readout_matrix=horizontal_readout_matrix, column_projection_weight=column_projection_weight, vertical_readout_matrix=vertical_readout_matrix, product_factor_matrices=product_factor_matrices, outer_output_weight=outer_output_weight, triangle_input_weight=triangle_input_weight, triangle_output_weight=triangle_output_weight)


EPSILON = 1e-05

def layer_normalized(input_rows, axis):
    average = lax.optimization_barrier(jnp.mean(input_rows, axis, keepdims=True))
    centred = input_rows - average
    spread = lax.optimization_barrier(jnp.mean(centred * centred, axis, keepdims=True))
    return centred * lax.rsqrt(spread + EPSILON)

def split_proj(input_rows, weight):
    channels = weight.shape[0]
    head_size = channels // HEAD_NUMBER
    projected = jnp.dot(input_rows, weight, preferred_element_type=jnp.float32)
    query_tensor = (projected[:, :channels] * head_size ** (-0.5)).astype(jnp.bfloat16).reshape(-1, HEAD_NUMBER, head_size)
    key_tensor = projected[:, channels:2 * channels].astype(jnp.bfloat16).reshape(-1, HEAD_NUMBER, head_size)
    value_tensor = projected[:, 2 * channels:3 * channels].astype(jnp.bfloat16).reshape(-1, HEAD_NUMBER, head_size)
    gate_values = projected[:, 3 * channels:]
    return (query_tensor, key_tensor, value_tensor, gate_values)

def gated_attention(query_tensor, key_tensor, value_tensor, gate_values, extra_bias, out_weight):
    scores = jnp.einsum('qhd,khd->hqk', query_tensor.astype(jnp.float32), key_tensor.astype(jnp.float32)) + extra_bias
    row_top = lax.optimization_barrier(jnp.max(scores, -1, keepdims=True))
    exp_scores = jnp.exp(scores - row_top)
    weights = (exp_scores / lax.optimization_barrier(jnp.sum(exp_scores, -1, keepdims=True))).astype(jnp.bfloat16)
    mixed = jnp.einsum('hqk,khd->qhd', weights.astype(jnp.float32), value_tensor.astype(jnp.float32))
    gated = (jax.nn.sigmoid(gate_values) * mixed.reshape(gate_values.shape)).astype(jnp.bfloat16)
    return jnp.dot(gated, out_weight, preferred_element_type=jnp.float32)

def reference(homolog_symbol_ids, residue_attend_mask, alignment_state, pair, symbol_lookup_matrix, pair_bias_weight, row_projection_weight, horizontal_readout_matrix, column_projection_weight, vertical_readout_matrix, product_factor_matrices, outer_output_weight, triangle_input_weight, triangle_output_weight):
    one_hot_tokens = (homolog_symbol_ids[:, :, None] == jnp.arange(AMINO_VOCAB, dtype=jnp.int32)[None, None, :]).astype(jnp.float32)
    alignment_initial = alignment_state.astype(jnp.float32) + jnp.einsum('kly,yb->klb', one_hot_tokens, symbol_lookup_matrix.astype(jnp.float32))
    pair_normed = layer_normalized(pair.astype(jnp.float32), -1).astype(jnp.bfloat16)
    bias_full = jnp.einsum('ijc,ch->hij', pair_normed.astype(jnp.float32), pair_bias_weight.astype(jnp.float32)).astype(jnp.bfloat16)
    mask_bias = (residue_attend_mask.astype(jnp.float32) - 1.0) * 10000.0
    extra_bias = bias_full.astype(jnp.float32) + mask_bias[None, None, :]

    def row_update_one(alignment_row):
        input_rows = layer_normalized(alignment_row, -1).astype(jnp.bfloat16)
        query_tensor, key_tensor, value_tensor, gate_values = split_proj(input_rows, row_projection_weight)
        return (alignment_row + gated_attention(query_tensor, key_tensor, value_tensor, gate_values, extra_bias, horizontal_readout_matrix)).astype(jnp.bfloat16)
    alignment_after_rows = lax.map(row_update_one, alignment_initial)

    def column_update_one(column):
        column_start = column.astype(jnp.float32)
        input_rows = layer_normalized(column_start, -1).astype(jnp.bfloat16)
        query_tensor, key_tensor, value_tensor, gate_values = split_proj(input_rows, column_projection_weight)
        return column_start + gated_attention(query_tensor, key_tensor, value_tensor, gate_values, jnp.float32(0.0), vertical_readout_matrix)
    alignment_after_columns = lax.map(column_update_one, jnp.swapaxes(alignment_after_rows, 0, 1))
    alignment_output = jnp.swapaxes(alignment_after_columns, 0, 1).astype(jnp.bfloat16)
    outer_input = layer_normalized(alignment_after_columns, -1).astype(jnp.bfloat16)
    factor_ab = jnp.einsum('rsc,ce->rse', outer_input.astype(jnp.float32), product_factor_matrices.astype(jnp.float32))
    left = factor_ab[..., :PRODUCT_WIDTH].astype(jnp.bfloat16)
    latter_factor = factor_ab[..., PRODUCT_WIDTH:].astype(jnp.bfloat16)

    def opm_one(former_factor_vector):
        cross_product_result = (jnp.einsum('vf,avt->aft', former_factor_vector.astype(jnp.float32), latter_factor.astype(jnp.float32)) / HOMOLOG_NUMBER).astype(jnp.bfloat16)
        return jnp.dot(cross_product_result.reshape(CHAIN_LENGTH, PRODUCT_WIDTH * PRODUCT_WIDTH), outer_output_weight, preferred_element_type=jnp.float32)
    update = lax.map(opm_one, left)
    pair_one = pair.astype(jnp.float32) + update
    tri_normed = layer_normalized(pair_one, -1).astype(jnp.bfloat16)
    projected = jnp.einsum('ijc,ce->ije', tri_normed.astype(jnp.float32), triangle_input_weight.astype(jnp.float32))
    left_f = (jax.nn.sigmoid(projected[..., CZ:2 * CZ]) * projected[..., :CZ]).astype(jnp.bfloat16)
    right_f = (jax.nn.sigmoid(projected[..., 3 * CZ:4 * CZ]) * projected[..., 2 * CZ:3 * CZ]).astype(jnp.bfloat16)
    gate_out = projected[..., 4 * CZ:]
    combined = jnp.einsum('ikc,jkc->ijc', left_f.astype(jnp.float32), right_f.astype(jnp.float32)).astype(jnp.bfloat16)
    comb_normed = layer_normalized(combined.astype(jnp.float32), -1).astype(jnp.bfloat16)
    tri_update = jnp.dot(comb_normed, triangle_output_weight, preferred_element_type=jnp.float32)
    pair_output = (pair_one + jax.nn.sigmoid(gate_out) * tri_update).astype(jnp.bfloat16)
    return (alignment_output, pair_output)
```

```python
import functools

import jax
import jax.numpy as jnp
from jax import lax
from jax.experimental import pallas as pl
from jax.experimental.pallas import tpu as pltpu
from jax.sharding import PartitionSpec as P

EPSILON = 1e-05
MESH = pl.DeviceIdType.MESH
F32 = jnp.float32
BF16 = jnp.bfloat16

NN = (((1,), (0,)), ((), ()))
NT = (((1,), (1,)), ((), ()))
TN = (((0,), (0,)), ((), ()))


def dot(a, b, dims=NN):
    return lax.dot_general(a, b, dims, preferred_element_type=F32)


def layer_normalized(rows, axis=-1):
    average = jnp.mean(rows, axis, keepdims=True)
    centred = rows - average
    spread = jnp.mean(centred * centred, axis, keepdims=True)
    return centred * lax.rsqrt(spread + EPSILON)


def split_index(index, size):
    if size & (size - 1) == 0:
        return lax.shift_right_logical(index, jnp.int32(size.bit_length() - 1)), index & (size - 1)
    return lax.div(index, size), lax.rem(index, size)


def selection(size, source):
    row = lax.broadcasted_iota(jnp.int32, (size, size), 0)
    column = lax.broadcasted_iota(jnp.int32, (size, size), 1)
    return jnp.where(column == source(row), 1.0, 0.0).astype(BF16)


def head_mask(head, head_size, channels):
    lane = lax.broadcasted_iota(jnp.int32, (1, channels), 1)
    inside = (lane >= head * head_size) & (lane < (head + 1) * head_size)
    return jnp.where(inside, 1.0, 0.0).astype(BF16)


def fill(buffer, values):
    for k in range(buffer.shape[0]):
        buffer[k] = values[:, k * 128 : (k + 1) * 128]


def pick(buffer, start, size, stride):
    return jnp.concatenate(
        [buffer[k, pl.ds(start, size, stride=stride), :] for k in range(buffer.shape[0])], 1
    )


def landed(landing):
    blocks = landing[...].astype(F32)
    return blocks.reshape(blocks.shape[0] * blocks.shape[1], blocks.shape[2])


def softmax_rows(scores):
    top = jnp.max(scores, -1, keepdims=True)
    powers = jnp.exp(scores - top)
    return (powers / jnp.sum(powers, -1, keepdims=True)).astype(BF16)


def block_kernel(
    sizes,
    ids_h, mask_h, align_h, pair_h, table_h, bias_w_h, row_w_h, row_o_h, col_w_h, col_o_h,
    factor_w_h, outer_w_h, tri_w_h, tri_o_h,
    align_out_h, pair_out_h,
    ids, mask, align, pair, table, bias_w, row_w, row_o, col_w, col_o,
    factor_w, outer_w, tri_w, tri_o,
    bias_src, bias_land, msa_src, msa_land, right_src, right_land, tri_src, tri_land,
    back_src, back_land,
    bias_f, msa_f, outer_f, outer_w2, left_t, right_f, right_m, pair_one_v, tri_t, tri_f,
    land_f, comb_f, back_f, gate_v, align_v, pair_v,
    in_sem, out_sem, send_sem, recv_sem,
):
    count, seqs, rows, length, channels, heads, width, pair_chan, total = sizes
    own = pair_chan // count
    head_size = channels // heads
    me = lax.axis_index("res")
    barrier = pltpu.get_barrier_semaphore()

    @pl.loop(1, count)
    def _(step):
        pl.semaphore_signal(
            barrier, inc=1, device_id={"res": lax.rem(me + step, count)}, device_id_type=MESH
        )

    staged = [
        (pair_h, pair), (bias_w_h, bias_w), (align_h, align), (ids_h, ids), (table_h, table),
        (row_w_h, row_w), (mask_h, mask), (row_o_h, row_o), (col_w_h, col_w), (col_o_h, col_o),
        (factor_w_h, factor_w), (outer_w_h, outer_w), (tri_w_h, tri_w), (tri_o_h, tri_o),
    ]
    loads = [
        pltpu.make_async_copy(source, target, in_sem.at[k])
        for k, (source, target) in enumerate(staged)
    ]
    for load in loads:
        load.start()

    def send(number, source, landing, gather):
        @pl.loop(1, count)
        def _(step):
            peer = lax.rem(me + step, count)
            pltpu.make_async_remote_copy(
                src_ref=source if gather else source.at[peer],
                dst_ref=landing.at[me],
                send_sem=send_sem.at[number],
                recv_sem=recv_sem.at[number],
                device_id={"res": peer},
                device_id_type=MESH,
            ).start()

    def received(number, landing):
        others = landing.at[pl.ds(0, count - 1)]
        pltpu.make_async_copy(others, others, recv_sem.at[number]).wait()

    loads[0].wait()
    loads[1].wait()
    pieces = []
    for i in range(rows):
        normed = layer_normalized(pair[i].astype(F32)).astype(BF16)
        pieces.append(dot(bias_w[...], normed, (((0,), (1,)), ((), ()))))
    slab = jnp.concatenate(pieces, 0).astype(BF16)
    bias_src[...] = slab
    bias_land[me] = slab
    pl.semaphore_wait(barrier, count - 1)
    send(0, bias_src, bias_land, True)

    for load in loads[2:6]:
        load.wait()
    token = lax.broadcasted_iota(jnp.int32, (table.shape[0], length), 0)
    zero_rows = []
    for s in range(seqs):
        one_hot = jnp.where(ids[pl.ds(s, 1), :] == token, 1.0, 0.0).astype(BF16)
        zero_rows.append(align[s].astype(F32) + dot(one_hot, table[...], TN))
    msa_zero = jnp.concatenate(zero_rows, 0)
    projected = dot(layer_normalized(msa_zero).astype(BF16), row_w[...])
    masks = [head_mask(h, head_size, channels) for h in range(heads)]
    scale = head_size ** (-0.5)

    loads[6].wait()
    loads[7].wait()
    raw_scores, spread_values = [], []
    for s in range(seqs):
        part = projected[s * length : (s + 1) * length]
        query = (part[:, :channels] * scale).astype(BF16)
        key = part[:, channels : 2 * channels].astype(BF16)
        value = part[:, 2 * channels : 3 * channels].astype(BF16)
        stacked = jnp.concatenate([query * m for m in masks], 0)
        raw_scores.append(dot(stacked, key, NT))
        spread_values.append(jnp.concatenate([value * m for m in masks], 0))
    to_owner = selection(
        seqs * length,
        lambda o: (
            split_index(split_index(o, rows)[0], seqs)[1] * length
            + split_index(o, seqs * rows)[0] * rows
            + split_index(o, rows)[1]
        ),
    )
    for load in loads[8:]:
        load.wait()
    tri_t[...] = jnp.transpose(tri_w[:, : 4 * pair_chan].astype(F32), (1, 0)).astype(BF16)
    fill(outer_f, outer_w[...].astype(F32))
    for d in range(width):
        outer_w2[:, d * pair_chan : (d + 1) * pair_chan] = pick(
            outer_f, d, width, width
        ).astype(BF16)

    received(0, bias_land)
    fill(bias_f, landed(bias_land))
    mask_bias = (mask[...].astype(F32) - 1.0) * 10000.0
    extra = jnp.concatenate(
        [pick(bias_f, h, length, heads) for h in range(heads)], 0
    ) + mask_bias
    one_rows = []
    for s in range(seqs):
        weights = softmax_rows(raw_scores[s] + extra)
        side = jnp.concatenate(
            [weights[h * length : (h + 1) * length] for h in range(heads)], 1
        )
        mixed = dot(side, spread_values[s])
        gate = projected[s * length : (s + 1) * length, 3 * channels :]
        gated = (jax.nn.sigmoid(gate) * mixed).astype(BF16)
        zero = msa_zero[s * length : (s + 1) * length]
        one_rows.append((zero + dot(gated, row_o[...])).astype(BF16))
    ordered = dot(to_owner, jnp.concatenate(one_rows, 0))
    ordered = ordered.reshape(count, seqs * rows, channels)
    lane_parts = channels // 128
    slabs = jnp.concatenate(
        [ordered[:, :, k * 128 : (k + 1) * 128] for k in range(lane_parts)], 1
    ).astype(BF16)
    msa_src[...] = slabs
    msa_land[me] = msa_src[me]
    send(1, msa_src, msa_land, False)

    to_output = selection(
        total * rows,
        lambda o: (
            split_index(o, rows)[1] * total
            + split_index(split_index(o, rows)[0], seqs)[1] * count
            + split_index(o, seqs * rows)[0]
        ),
    )
    received(1, msa_land)
    fill(msa_f, landed(msa_land))
    step = lane_parts * seqs * rows
    column = jnp.concatenate(
        [
            jnp.concatenate(
                [
                    pick(msa_f, (k * seqs + s) * rows + i, count, step)
                    for i in range(rows)
                    for s in range(seqs)
                ],
                0,
            )
            for k in range(lane_parts)
        ],
        1,
    )
    projected = dot(layer_normalized(column).astype(BF16), col_w[...])
    gated_rows = []
    for i in range(rows):
        part = projected[i * total : (i + 1) * total]
        query = (part[:, :channels] * scale).astype(BF16)
        key = part[:, channels : 2 * channels].astype(BF16)
        value = part[:, 2 * channels : 3 * channels].astype(BF16)
        stacked = jnp.concatenate([query * m for m in masks], 0)
        weights = softmax_rows(dot(stacked, key, NT))
        every = dot(weights, value)
        mixed = every[:total] * masks[0].astype(F32)
        for h in range(1, heads):
            mixed = mixed + every[h * total : (h + 1) * total] * masks[h].astype(F32)
        gated_rows.append((jax.nn.sigmoid(part[:, 3 * channels :]) * mixed).astype(BF16))
    msa_two = column + dot(jnp.concatenate(gated_rows, 0), col_o[...])

    outer_input = layer_normalized(msa_two).astype(BF16)
    right_t = dot(factor_w[:, width:], outer_input, (((0,), (1,)), ((), ())))
    pack = max(1, 128 // total)
    groups = width // pack
    lanes = pack * total
    slabs = []
    if pack == 1:
        for i in range(rows):
            slabs.append(right_t[:, i * total : (i + 1) * total])
    else:
        lane = lax.broadcasted_iota(jnp.int32, (groups, lanes), 1)
        for i in range(rows):
            base, place = i // pack, i % pack
            joined = None
            for k in range(pack):
                piece = right_t[k * groups : (k + 1) * groups, base * lanes : (base + 1) * lanes]
                shift = ((k - place) * total) % lanes
                if shift:
                    piece = pltpu.roll(piece, shift, 1)
                joined = piece if joined is None else jnp.where(lane >= k * total, piece, joined)
            slabs.append(joined)
    slab = jnp.concatenate(slabs, 0).astype(BF16)
    right_src[...] = slab
    right_land[me] = slab
    send(2, right_src, right_land, True)

    ordered = dot(to_output, msa_two.astype(BF16)).astype(BF16)
    align_v[...] = ordered
    store_align = pltpu.make_async_copy(align_v, align_out_h, out_sem.at[0])
    store_align.start()
    left = dot(outer_input, factor_w[:, :width]).astype(BF16)
    chunk = 8
    for start in range(0, width, chunk):
        product = dot(left, outer_w2[:, start * pair_chan : (start + chunk) * pair_chan])
        for d in range(start, start + chunk):
            at = ((d % groups) * pack + d // groups) * total
            for i in range(rows):
                left_t[at : at + total, i * pair_chan : (i + 1) * pair_chan] = product[
                    i * total : (i + 1) * total,
                    (d - start) * pair_chan : (d - start + 1) * pair_chan,
                ].astype(BF16)

    received(2, right_land)
    fill(right_f, landed(right_land))
    for k in range(groups):
        right_m[:, k * lanes : (k + 1) * lanes] = pick(
            right_f, k, length, groups
        ).astype(BF16)
    update = dot(right_m[...], left_t[...]) * (1.0 / total)

    normed = []
    for i in range(rows):
        one = pair[i].astype(F32) + update[:, i * pair_chan : (i + 1) * pair_chan]
        pair_one_v[i] = one
        normed.append(layer_normalized(one).astype(BF16))
        factors = dot(tri_t[...], normed[i], NT)
        for k in range(2):
            low = 2 * k * pair_chan
            factor = (
                jax.nn.sigmoid(factors[low + pair_chan : low + 2 * pair_chan])
                * factors[low : low + pair_chan]
            )
            fill(tri_f.at[:, pl.ds((2 * i + k) * pair_chan, pair_chan), :], factor)
    for p in range(count):
        tri_src[p] = jnp.concatenate(
            [pick(tri_f, p * own + c, 2 * rows, pair_chan) for c in range(own)], 0
        ).astype(BF16)
    tri_land[me] = tri_src[me]
    send(3, tri_src, tri_land, False)

    for i in range(rows):
        gate_v[i] = jax.nn.sigmoid(dot(normed[i], tri_w[:, 4 * pair_chan :]))
    to_natural = selection(
        length, lambda o: split_index(o, rows)[1] * count + split_index(o, rows)[0]
    )

    received(3, tri_land)
    fill(land_f, landed(tri_land))
    stride = 2 * own * rows
    for c in range(own):
        sides = [
            jnp.concatenate(
                [
                    pick(land_f, (c * rows + i) * 2 + k, count, stride)
                    for i in range(rows)
                ],
                0,
            ).astype(BF16)
            for k in range(2)
        ]
        fill(comb_f.at[:, pl.ds(c * length, length), :], dot(sides[0], sides[1], NT))
    for p in range(count):
        back_src[p] = pick(comb_f, p, own * rows, count).astype(BF16)
    back_land[me] = back_src[me]
    send(4, back_src, back_land, False)

    received(4, back_land)
    fill(back_f, landed(back_land))
    for i in range(rows):
        combined = layer_normalized(pick(back_f, i, pair_chan, rows), 0).astype(BF16)
        turned = dot(to_natural, combined, NT).astype(BF16)
        result = pair_one_v[i] + gate_v[i] * dot(turned, tri_o[...])
        pair_v[i] = result.astype(BF16)
    store_pair = pltpu.make_async_copy(pair_v, pair_out_h, out_sem.at[1])
    store_pair.start()
    for number, landing in enumerate((bias_land, msa_land, right_land, tri_land, back_land)):
        others = landing.at[pl.ds(0, count - 1)]
        pltpu.make_async_copy(others, others, send_sem.at[number]).wait()
    store_align.wait()
    store_pair.wait()


def shards(
    homolog_symbol_ids,
    residue_attend_mask,
    alignment_state,
    pair,
    symbol_lookup_matrix,
    pair_bias_weight,
    row_projection_weight,
    horizontal_readout_matrix,
    column_projection_weight,
    vertical_readout_matrix,
    product_factor_matrices,
    outer_output_weight,
    triangle_input_weight,
    triangle_output_weight,
):
    count = lax.axis_size("res")
    seqs, length, channels = alignment_state.shape
    rows, _, pair_chan = pair.shape
    heads = pair_bias_weight.shape[1]
    width = product_factor_matrices.shape[1] // 2
    total = seqs * count
    own = pair_chan // count
    pack = max(1, 128 // total)
    groups, lanes = width // pack, pack * total
    operands = [
        homolog_symbol_ids,
        residue_attend_mask.reshape(1, length),
        alignment_state,
        pair,
        symbol_lookup_matrix,
        pair_bias_weight,
        row_projection_weight,
        horizontal_readout_matrix,
        column_projection_weight,
        vertical_readout_matrix,
        product_factor_matrices,
        outer_output_weight,
        triangle_input_weight,
        triangle_output_weight,
    ]
    lane_parts = channels // 128
    slab_rows = (
        (heads * rows, length),
        (lane_parts * seqs * rows, 128),
        (groups * rows, lanes),
        (2 * own * rows, length),
        (own * rows, length),
    )
    vmem = pltpu.VMEM
    exchanges = []
    for number, extent in enumerate(slab_rows):
        gathers = number in (0, 2)
        exchanges.append(vmem(extent if gathers else (count,) + extent, BF16))
        exchanges.append(vmem((count,) + extent, BF16))
    flat = [(b // 128, count * a, 128) for a, b in slab_rows]
    scratch = (
        [vmem(x.shape, x.dtype) for x in operands]
        + exchanges
        + [
            vmem(flat[0], F32),
            vmem(flat[1], F32),
            vmem((pair_chan // 128, width * width, 128), F32),
            vmem((width, width * pair_chan), BF16),
            vmem((width * total, rows * pair_chan), BF16),
            vmem(flat[2], F32),
            vmem((length, width * total), BF16),
            vmem(pair.shape, F32),
            vmem((4 * pair_chan, pair_chan), BF16),
            vmem((length // 128, 2 * rows * pair_chan, 128), F32),
            vmem(flat[3], F32),
            vmem((length // 128, own * length, 128), F32),
            vmem(flat[4], F32),
            vmem(pair.shape, F32),
            vmem((total * rows, channels), BF16),
            vmem(pair.shape, BF16),
            pltpu.SemaphoreType.DMA((len(operands),)),
            pltpu.SemaphoreType.DMA((2,)),
            pltpu.SemaphoreType.DMA((5,)),
            pltpu.SemaphoreType.DMA((5,)),
        ]
    )
    sizes = (count, seqs, rows, length, channels, heads, width, pair_chan, total)
    anywhere = pl.BlockSpec(memory_space=pl.ANY)
    alignment_output, pair_output = pl.pallas_call(
        functools.partial(block_kernel, sizes),
        out_shape=(
            jax.ShapeDtypeStruct((total * rows, channels), BF16),
            jax.ShapeDtypeStruct(pair.shape, BF16),
        ),
        in_specs=[anywhere] * len(operands),
        out_specs=(anywhere, anywhere),
        scratch_shapes=scratch,
        compiler_params=pltpu.CompilerParams(
            collective_id=0, has_side_effects=True, vmem_limit_bytes=60 * 1024 * 1024
        ),
    )(*operands)
    return (alignment_output.reshape(total, rows, channels), pair_output)


def solution(mesh):
    placed = (
        P(("crop", "res"), None),
        P("crop"),
        P(("crop", "res"), None, None),
        P(("crop", "res"), None, None),
        P(),
        P(),
        P(),
        P(),
        P(),
        P(),
        P(),
        P(),
        P(),
        P(),
    )
    return jax.shard_map(
        shards,
        mesh=mesh,
        in_specs=placed,
        out_specs=(P("crop", "res", None), P(("crop", "res"), None, None)),
        check_vma=False,
    )
```

```python
import functools

import jax
import jax.numpy as jnp
from jax import lax
from jax.experimental import pallas as pl
from jax.experimental.pallas import tpu as pltpu
from jax.sharding import PartitionSpec as P

EPSILON = 1e-05
MESH = pl.DeviceIdType.MESH
F32 = jnp.float32
BF16 = jnp.bfloat16

NN = (((1,), (0,)), ((), ()))
NT = (((1,), (1,)), ((), ()))
TN = (((0,), (0,)), ((), ()))


def dot(a, b, dims=NN):
    return lax.dot_general(a, b, dims, preferred_element_type=F32)


def layer_normalized(rows, axis=-1):
    average = jnp.mean(rows, axis, keepdims=True)
    centred = rows - average
    spread = jnp.mean(centred * centred, axis, keepdims=True)
    return centred * lax.rsqrt(spread + EPSILON)


def split_index(index, size):
    if size & (size - 1) == 0:
        return lax.shift_right_logical(index, jnp.int32(size.bit_length() - 1)), index & (size - 1)
    return lax.div(index, size), lax.rem(index, size)


def selection(size, source):
    row = lax.broadcasted_iota(jnp.int32, (size, size), 0)
    column = lax.broadcasted_iota(jnp.int32, (size, size), 1)
    return jnp.where(column == source(row), 1.0, 0.0).astype(BF16)


def head_mask(head, head_size, channels):
    lane = lax.broadcasted_iota(jnp.int32, (1, channels), 1)
    inside = (lane >= head * head_size) & (lane < (head + 1) * head_size)
    return jnp.where(inside, 1.0, 0.0).astype(BF16)


def fill(buffer, values):
    for k in range(buffer.shape[0]):
        buffer[k] = values[:, k * 128 : (k + 1) * 128]


def pick(buffer, start, size, stride):
    return jnp.concatenate(
        [buffer[k, pl.ds(start, size, stride=stride), :] for k in range(buffer.shape[0])], 1
    )


def landed(landing):
    blocks = landing[...].astype(F32)
    return blocks.reshape(-1, blocks.shape[-1])


def by_group(blocks, groups):
    size = blocks[0].shape[0] // groups
    if size % 8 == 0:
        return jnp.concatenate([b.reshape(groups, size, b.shape[1]) for b in blocks], 1)
    return jnp.stack(
        [
            jnp.concatenate([b[g * size : (g + 1) * size] for b in blocks], 0)
            for g in range(groups)
        ],
        0,
    )


def softmax_rows(scores):
    top = jnp.max(scores, -1, keepdims=True)
    powers = jnp.exp(scores - top)
    return (powers / jnp.sum(powers, -1, keepdims=True)).astype(BF16)


def block_kernel(
    sizes,
    ids_h, mask_h, align_h, pair_h, table_h, bias_w_h, row_w_h, row_o_h, col_w_h, col_o_h,
    factor_w_h, outer_w_h, tri_w_h, tri_o_h,
    align_out, pair_out,
    ids, mask, align, pair, table, bias_w, row_w, row_o, col_w, col_o,
    factor_w, outer_w, tri_w, tri_o,
    bias_src, bias_land, msa_src, msa_land, right_src, right_land, tri_left, left_land,
    tri_right, tri_land, back_src, back_land,
    bias_f, msa_f, outer_f, outer_w2, left_t, right_f, right_m, pair_one_v, tri_t,
    land_f, left_f, comb_f, back_f, gate_v,
    in_sem, send_sem, recv_sem, bias_sem, right_sem,
):
    count, seqs, rows, length, channels, heads, width, pair_chan, total = sizes
    head_size = channels // heads
    me = lax.axis_index("res")
    barrier = pltpu.get_barrier_semaphore()

    @pl.loop(1, count)
    def _(step):
        pl.semaphore_signal(
            barrier, inc=1, device_id={"res": lax.rem(me + step, count)}, device_id_type=MESH
        )

    staged = [
        (pair_h, pair), (bias_w_h, bias_w), (align_h, align), (ids_h, ids), (table_h, table),
        (row_w_h, row_w), (mask_h, mask), (row_o_h, row_o), (col_w_h, col_w), (col_o_h, col_o),
        (factor_w_h, factor_w), (outer_w_h, outer_w), (tri_w_h, tri_w), (tri_o_h, tri_o),
    ]
    loads = [
        pltpu.make_async_copy(source, target, in_sem.at[k])
        for k, (source, target) in enumerate(staged)
    ]
    for load in loads:
        load.start()

    def remote(source, target, number, received_by, peer):
        pltpu.make_async_remote_copy(
            src_ref=source,
            dst_ref=target,
            send_sem=send_sem.at[number],
            recv_sem=received_by,
            device_id={"res": peer},
            device_id_type=MESH,
        ).start()

    def taken(landing, semaphore):
        pltpu.make_async_copy(landing, landing, semaphore).wait()

    chips = count // 2
    partner = me + 1 - 2 * lax.rem(me, 2)
    flips = [
        (1 - 2 * lax.rem(lax.div(me, 2 << j), 2)) * (2 << j) for j in range(chips.bit_length() - 1)
    ]
    others = [me + sum(flips[j] for j in range(len(flips)) if (k >> j) & 1) for k in range(1, chips)]

    def gather_start(number, arrivals, source, landing, part):
        for k in reversed(range(chips - 1)):
            remote(
                source, landing.at[(me,) + part], number, arrivals.at[part + (k,)], others[k]
            )
        remote(source, landing.at[(me,) + part], number, recv_sem.at[number], partner)

    def gather_relay(number, arrivals, landing, part):
        for k in range(chips - 1):
            block = landing.at[(others[k],) + part]
            taken(block, arrivals.at[part + (k,)])
            remote(block, block, number, recv_sem.at[number], partner)

    def gather_finish(number, landing):
        taken(landing.at[pl.ds(0, chips)], recv_sem.at[number])

    half = count // 2
    group, first = lax.rem(me, half), lax.div(me, half) * half

    def spread(number, source, landing, size):
        @pl.loop(1, size)
        def _(step):
            if size == count:
                peer = lax.rem(me + step, count)
            else:
                peer = first + lax.rem(group + step, size)
            remote(source(peer), landing, number, recv_sem.at[number], peer)

    loads[0].wait()
    loads[1].wait()
    pieces = []
    for i in range(rows):
        normed = layer_normalized(pair[i].astype(F32)).astype(BF16)
        pieces.append(dot(bias_w[...], normed, NT))
    slab = jnp.concatenate(pieces, 0).astype(BF16)
    bias_src[...] = slab
    bias_land[me] = slab
    pl.semaphore_wait(barrier, count - 1)
    gather_start(0, bias_sem, bias_src, bias_land, ())

    for load in loads[2:6]:
        load.wait()
    token = lax.broadcasted_iota(jnp.int32, (table.shape[0], length), 0)
    zero_rows = []
    for s in range(seqs):
        one_hot = jnp.where(ids[pl.ds(s, 1), :] == token, 1.0, 0.0).astype(BF16)
        zero_rows.append(align[s].astype(F32) + dot(one_hot, table[...], TN))
    msa_zero = jnp.concatenate(zero_rows, 0)
    projected = dot(layer_normalized(msa_zero).astype(BF16), row_w[...])
    masks = [head_mask(h, head_size, channels) for h in range(heads)]
    scale = head_size ** (-0.5)

    loads[6].wait()
    loads[7].wait()
    raw_scores, spread_values = [], []
    for s in range(seqs):
        part = projected[s * length : (s + 1) * length]
        query = (part[:, :channels] * scale).astype(BF16)
        key = part[:, channels : 2 * channels].astype(BF16)
        value = part[:, 2 * channels : 3 * channels].astype(BF16)
        stacked = jnp.concatenate([query * m for m in masks], 0)
        raw_scores.append(dot(stacked, key, NT))
        spread_values.append(jnp.concatenate([value * m for m in masks], 0))
    to_owner = selection(
        seqs * length,
        lambda o: (
            split_index(split_index(o, rows)[0], seqs)[1] * length
            + split_index(o, seqs * rows)[0] * rows
            + split_index(o, rows)[1]
        ),
    )
    for load in loads[8:]:
        load.wait()
    tri_t[...] = jnp.transpose(tri_w[:, : 4 * pair_chan].astype(F32), (1, 0)).astype(BF16)
    fill(outer_f, outer_w[...].astype(F32))
    for d in range(width):
        outer_w2[:, d * pair_chan : (d + 1) * pair_chan] = pick(
            outer_f, d, width, width
        ).astype(BF16)

    gather_relay(0, bias_sem, bias_land, ())
    gather_finish(0, bias_land)
    fill(bias_f, landed(bias_land))
    mask_bias = (mask[...].astype(F32) - 1.0) * 10000.0
    extra = jnp.concatenate(
        [pick(bias_f, h, length, heads) for h in range(heads)], 0
    ) + mask_bias
    one_rows = []
    for s in range(seqs):
        weights = softmax_rows(raw_scores[s] + extra)
        side = jnp.concatenate(
            [weights[h * length : (h + 1) * length] for h in range(heads)], 1
        )
        mixed = dot(side, spread_values[s])
        gate = projected[s * length : (s + 1) * length, 3 * channels :]
        gated = (jax.nn.sigmoid(gate) * mixed).astype(BF16)
        zero = msa_zero[s * length : (s + 1) * length]
        one_rows.append((zero + dot(gated, row_o[...])).astype(BF16))
    ordered = dot(to_owner, jnp.concatenate(one_rows, 0))
    ordered = ordered.reshape(count, seqs * rows, channels)
    lane_parts = channels // 128
    slabs = jnp.concatenate(
        [ordered[:, :, k * 128 : (k + 1) * 128] for k in range(lane_parts)], 1
    ).astype(BF16)
    msa_src[...] = slabs
    msa_land[me] = msa_src[me]
    spread(1, lambda peer: msa_src.at[peer], msa_land.at[me], count)

    to_output = selection(
        total * rows,
        lambda o: (
            split_index(o, rows)[1] * total
            + split_index(split_index(o, rows)[0], seqs)[1] * count
            + split_index(o, seqs * rows)[0]
        ),
    )
    taken(msa_land.at[pl.ds(0, count - 1)], recv_sem.at[1])
    fill(msa_f, landed(msa_land))
    step = lane_parts * seqs * rows
    column = jnp.concatenate(
        [
            jnp.concatenate(
                [
                    pick(msa_f, (k * seqs + s) * rows + i, count, step)
                    for i in range(rows)
                    for s in range(seqs)
                ],
                0,
            )
            for k in range(lane_parts)
        ],
        1,
    )
    pack = max(1, 128 // total)
    groups = width // pack
    lanes = pack * total
    lane = lax.broadcasted_iota(jnp.int32, (groups, lanes), 1)
    two_rows, inputs = [], []
    for start in range(0, rows, pack):
        block = column[start * total : (start + pack) * total]
        projected = dot(layer_normalized(block).astype(BF16), col_w[...])
        gated_rows = []
        for i in range(pack):
            part = projected[i * total : (i + 1) * total]
            query = (part[:, :channels] * scale).astype(BF16)
            key = part[:, channels : 2 * channels].astype(BF16)
            value = part[:, 2 * channels : 3 * channels].astype(BF16)
            stacked = jnp.concatenate([query * m for m in masks], 0)
            weights = softmax_rows(dot(stacked, key, NT))
            every = dot(weights, value)
            mixed = every[:total] * masks[0].astype(F32)
            for h in range(1, heads):
                mixed = mixed + every[h * total : (h + 1) * total] * masks[h].astype(F32)
            gated_rows.append((jax.nn.sigmoid(part[:, 3 * channels :]) * mixed).astype(BF16))
        msa_two = block + dot(jnp.concatenate(gated_rows, 0), col_o[...])
        outer_input = layer_normalized(msa_two).astype(BF16)
        two_rows.append(msa_two.astype(BF16))
        inputs.append(outer_input)

        right_t = dot(factor_w[width:, :], outer_input, NT)
        slabs = []
        for place in range(pack):
            joined = None
            for k in range(pack):
                piece = right_t[k * groups : (k + 1) * groups]
                shift = ((k - place) * total) % lanes
                if shift:
                    piece = pltpu.roll(piece, shift, 1)
                joined = piece if joined is None else jnp.where(lane >= k * total, piece, joined)
            slabs.append(joined)
        slab = jnp.concatenate(slabs, 0).astype(BF16)
        part = (start // pack,)
        right_src[part[0]] = slab
        right_land[me, part[0]] = slab
        gather_start(2, right_sem, right_src.at[part[0]], right_land, part)

    ordered = dot(to_output, jnp.concatenate(two_rows, 0))
    align_out[...] = ordered.reshape(total, rows, channels).astype(BF16)
    left = dot(jnp.concatenate(inputs, 0), factor_w[:width, :], NT).astype(BF16)
    chunk = 8
    for start in range(0, width, chunk):
        product = dot(left, outer_w2[:, start * pair_chan : (start + chunk) * pair_chan])
        for d in range(start, start + chunk):
            at = ((d % groups) * pack + d // groups) * total
            for i in range(rows):
                left_t[at : at + total, i * pair_chan : (i + 1) * pair_chan] = product[
                    i * total : (i + 1) * total,
                    (d - start) * pair_chan : (d - start + 1) * pair_chan,
                ].astype(BF16)

    for k in range(rows // pack):
        gather_relay(2, right_sem, right_land, (k,))
    gather_finish(2, right_land)
    fill(right_f, landed(right_land))
    for k in range(groups):
        right_m[:, k * lanes : (k + 1) * lanes] = pick(right_f, k, length, groups).astype(BF16)

    own = pair_chan // half
    normed = []
    pairs = tri_left.shape[0]
    pair_rows = rows // pairs
    for q in range(pairs):
        columns = pl.ds(q * pair_rows * pair_chan, pair_rows * pair_chan)
        update = dot(right_m[...], left_t[:, columns]) * (1.0 / total)
        sides = [[], []]
        for k in range(pair_rows):
            i = q * pair_rows + k
            one = pair[i].astype(F32) + update[:, k * pair_chan : (k + 1) * pair_chan]
            pair_one_v[i] = one
            normed.append(layer_normalized(one).astype(BF16))
            factors = dot(tri_t[...], normed[i], NT)
            for side in range(2):
                low = 2 * side * pair_chan
                sides[side].append(
                    jax.nn.sigmoid(factors[low + pair_chan : low + 2 * pair_chan])
                    * factors[low : low + pair_chan]
                )
        tri_left[q] = by_group(sides[0], half).astype(BF16)
        tri_right[q] = by_group(sides[1], half).astype(BF16)
        left_land[group, q] = tri_left[q, group]
        tri_land[me, q] = tri_right[q, group]
        spread(
            3, lambda peer: tri_right.at[q, lax.rem(peer, half)], tri_land.at[me, q], count
        )
        spread(4, lambda peer: tri_left.at[q, lax.rem(peer, half)], left_land.at[group, q], half)

    for i in range(rows):
        gate_v[i] = jax.nn.sigmoid(dot(normed[i], tri_w[:, 4 * pair_chan :]))
    taken(tri_land.at[pl.ds(0, count - 1)], recv_sem.at[3])
    taken(left_land.at[pl.ds(0, half - 1)], recv_sem.at[4])
    fill(land_f, landed(tri_land))
    fill(left_f, landed(left_land))
    block = half * rows
    for c in range(own):
        left_side = jnp.concatenate(
            [pick(left_f, i * own + c, half, own * rows) for i in range(rows)], 0
        ).astype(BF16)
        right_side = pick(land_f, c, length, own).astype(BF16)
        fill(comb_f.at[:, pl.ds(c * block, block), :], dot(left_side, right_side, NT))
    for p in range(half):
        back_src[p] = pick(comb_f, p, own * rows, half).astype(BF16)
    back_land[group] = back_src[group]
    spread(5, lambda peer: back_src.at[lax.rem(peer, half)], back_land.at[group], half)

    taken(back_land.at[pl.ds(0, half - 1)], recv_sem.at[5])
    fill(back_f, landed(back_land))
    for i in range(rows):
        combined = layer_normalized(pick(back_f, i, pair_chan, rows), 0).astype(BF16)
        result = pair_one_v[i] + gate_v[i] * dot(combined, tri_o[...], TN)
        pair_out[i] = result.astype(BF16)
    for number, sent in enumerate((bias_land, msa_land, right_land, tri_land)):
        taken(sent.at[pl.ds(0, count - 1)], send_sem.at[number])
    taken(left_land.at[pl.ds(0, half - 1)], send_sem.at[4])
    taken(back_land.at[pl.ds(0, half - 1)], send_sem.at[5])


def shards(
    homolog_symbol_ids,
    residue_attend_mask,
    alignment_state,
    pair,
    symbol_lookup_matrix,
    pair_bias_weight,
    row_projection_weight,
    horizontal_readout_matrix,
    column_projection_weight,
    vertical_readout_matrix,
    product_factor_matrices,
    outer_output_weight,
    triangle_input_weight,
    triangle_output_weight,
):
    count = lax.axis_size("res")
    seqs, length, channels = alignment_state.shape
    rows, _, pair_chan = pair.shape
    heads = pair_bias_weight.shape[1]
    width = product_factor_matrices.shape[1] // 2
    total = seqs * count
    half = count // 2
    own = pair_chan // half
    pack = max(1, 128 // total)
    groups, lanes = width // pack, pack * total
    operands = [
        homolog_symbol_ids,
        residue_attend_mask.reshape(1, length),
        alignment_state,
        pair,
        symbol_lookup_matrix,
        pair_bias_weight.T,
        row_projection_weight,
        horizontal_readout_matrix,
        column_projection_weight,
        vertical_readout_matrix,
        product_factor_matrices.T,
        outer_output_weight,
        triangle_input_weight,
        triangle_output_weight,
    ]
    lane_parts = channels // 128
    vmem = pltpu.VMEM
    parts, pairs = rows // pack, 2
    tri_slab = (pairs, half, own * rows // pairs, length)
    exchanges = [
        vmem((heads * rows, length), BF16),
        vmem((count, heads * rows, length), BF16),
        vmem((count, lane_parts * seqs * rows, 128), BF16),
        vmem((count, lane_parts * seqs * rows, 128), BF16),
        vmem((parts, groups * pack, lanes), BF16),
        vmem((count, parts, groups * pack, lanes), BF16),
        vmem(tri_slab, BF16),
        vmem((half, pairs) + tri_slab[2:], BF16),
        vmem(tri_slab, BF16),
        vmem((count, pairs) + tri_slab[2:], BF16),
        vmem((half, own * rows, length), BF16),
        vmem((half, own * rows, length), BF16),
    ]

    def pieces(row_count, lane_count):
        return vmem((lane_count // 128, row_count, 128), F32)

    scratch = (
        [vmem(x.shape, x.dtype) for x in operands]
        + exchanges
        + [
            pieces(count * heads * rows, length),
            pieces(count * lane_parts * seqs * rows, 128),
            pieces(width * width, pair_chan),
            vmem((width, width * pair_chan), BF16),
            vmem((width * total, rows * pair_chan), BF16),
            pieces(length * groups, lanes),
            vmem((length, width * total), BF16),
            vmem(pair.shape, F32),
            vmem((4 * pair_chan, pair_chan), BF16),
            pieces(count * own * rows, length),
            pieces(half * own * rows, length),
            pieces(half * own * rows, length),
            pieces(half * own * rows, length),
            vmem(pair.shape, F32),
            pltpu.SemaphoreType.DMA((len(operands),)),
            pltpu.SemaphoreType.DMA((6,)),
            pltpu.SemaphoreType.DMA((6,)),
            pltpu.SemaphoreType.DMA((half - 1,)),
            pltpu.SemaphoreType.DMA((parts, half - 1)),
        ]
    )
    sizes = (count, seqs, rows, length, channels, heads, width, pair_chan, total)
    anywhere = pl.BlockSpec(memory_space=pl.ANY)
    inside = pl.BlockSpec(memory_space=pltpu.VMEM)
    alignment_output, pair_output = pl.pallas_call(
        functools.partial(block_kernel, sizes),
        out_shape=(
            jax.ShapeDtypeStruct((total, rows, channels), BF16),
            jax.ShapeDtypeStruct(pair.shape, BF16),
        ),
        in_specs=[anywhere] * len(operands),
        out_specs=(inside, inside),
        scratch_shapes=scratch,
        compiler_params=pltpu.CompilerParams(
            collective_id=0, has_side_effects=True, vmem_limit_bytes=60 * 1024 * 1024
        ),
    )(*operands)
    return (alignment_output, pair_output)


def solution(mesh):
    placed = (
        P(("crop", "res"), None),
        P("crop"),
        P(("crop", "res"), None, None),
        P(("crop", "res"), None, None),
        P(),
        P(),
        P(),
        P(),
        P(),
        P(),
        P(),
        P(),
        P(),
        P(),
    )
    return jax.shard_map(
        shards,
        mesh=mesh,
        in_specs=placed,
        out_specs=(P("crop", "res", None), P(("crop", "res"), None, None)),
        check_vma=False,
    )
```

```python
import functools

import jax
import jax.numpy as jnp
from jax import lax
from jax.experimental import pallas as pl
from jax.experimental.pallas import tpu as pltpu
from jax.sharding import PartitionSpec as P

EPSILON = 1e-05
MESH = pl.DeviceIdType.MESH
VMEM_BYTES = 40 * 1024 * 1024
F32 = jnp.float32
BF16 = jnp.bfloat16

NN = (((1,), (0,)), ((), ()))
NT = (((1,), (1,)), ((), ()))
TN = (((0,), (0,)), ((), ()))


def dot(a, b, dims=NN):
    return lax.dot_general(a, b, dims, preferred_element_type=F32)


def layer_normalized(rows, axis=-1):
    average = jnp.mean(rows, axis, keepdims=True)
    centred = rows - average
    spread = jnp.mean(centred * centred, axis, keepdims=True)
    return centred * lax.rsqrt(spread + EPSILON)


def split_index(index, size):
    if size & (size - 1) == 0:
        return lax.shift_right_logical(index, jnp.int32(size.bit_length() - 1)), index & (size - 1)
    return lax.div(index, size), lax.rem(index, size)


def selection(size, source):
    row = lax.broadcasted_iota(jnp.int32, (size, size), 0)
    column = lax.broadcasted_iota(jnp.int32, (size, size), 1)
    return jnp.where(column == source(row), 1.0, 0.0).astype(BF16)


def head_mask(head, head_size, channels):
    lane = lax.broadcasted_iota(jnp.int32, (1, channels), 1)
    inside = (lane >= head * head_size) & (lane < (head + 1) * head_size)
    return jnp.where(inside, 1.0, 0.0).astype(BF16)


def fill(buffer, values):
    for k in range(buffer.shape[0]):
        buffer[k] = values[:, k * 128 : (k + 1) * 128]


def pick(buffer, start, size, stride):
    return jnp.concatenate(
        [buffer[k, pl.ds(start, size, stride=stride), :] for k in range(buffer.shape[0])], 1
    )


def landed(landing):
    blocks = landing[...].astype(F32)
    return blocks.reshape(-1, blocks.shape[-1])


def by_group(blocks, groups):
    size = blocks[0].shape[0] // groups
    if size % 8 == 0:
        return jnp.concatenate([b.reshape(groups, size, b.shape[1]) for b in blocks], 1)
    return jnp.stack(
        [
            jnp.concatenate([b[g * size : (g + 1) * size] for b in blocks], 0)
            for g in range(groups)
        ],
        0,
    )


def softmax_rows(scores):
    top = jnp.max(scores, -1, keepdims=True)
    powers = jnp.exp(scores - top)
    return (powers / jnp.sum(powers, -1, keepdims=True)).astype(BF16)


def block_kernel(
    sizes,
    ids_h, mask_h, align_h, pair_h, table_h, bias_w_h, row_w_h, row_o_h, col_w_h, col_o_h,
    factor_w_h, outer_w_h, tri_w_h,
    align_out, back_land, pair_one_v, gate_v,
    ids, mask, align, pair, table, bias_w, row_w, row_o, col_w, col_o,
    factor_w, outer_w, tri_w,
    bias_src, bias_land, msa_src, msa_land, right_src, right_land, tri_left, left_land,
    tri_right, tri_land, back_src,
    bias_f, msa_f, outer_f, outer_w2, left_t, right_f, right_m, tri_t,
    land_f, left_f, comb_f,
    in_sem, send_sem, recv_sem, bias_sem, right_sem,
):
    count, seqs, rows, length, channels, heads, width, pair_chan, total = sizes
    head_size = channels // heads
    me = lax.axis_index("res")
    barrier = pltpu.get_barrier_semaphore()

    @pl.loop(1, count)
    def _(step):
        pl.semaphore_signal(
            barrier, inc=1, device_id={"res": lax.rem(me + step, count)}, device_id_type=MESH
        )

    staged = [
        (pair_h, pair), (bias_w_h, bias_w), (align_h, align), (ids_h, ids), (table_h, table),
        (row_w_h, row_w), (mask_h, mask), (row_o_h, row_o), (col_w_h, col_w), (col_o_h, col_o),
        (factor_w_h, factor_w), (outer_w_h, outer_w), (tri_w_h, tri_w),
    ]
    loads = [
        pltpu.make_async_copy(source, target, in_sem.at[k])
        for k, (source, target) in enumerate(staged)
    ]
    for load in loads:
        load.start()

    def remote(source, target, number, received_by, peer):
        pltpu.make_async_remote_copy(
            src_ref=source,
            dst_ref=target,
            send_sem=send_sem.at[number],
            recv_sem=received_by,
            device_id={"res": peer},
            device_id_type=MESH,
        ).start()

    def taken(landing, semaphore):
        pltpu.make_async_copy(landing, landing, semaphore).wait()

    chips = count // 2
    partner = me + 1 - 2 * lax.rem(me, 2)
    flips = [
        (1 - 2 * lax.rem(lax.div(me, 2 << j), 2)) * (2 << j) for j in range(chips.bit_length() - 1)
    ]
    others = [me + sum(flips[j] for j in range(len(flips)) if (k >> j) & 1) for k in range(1, chips)]

    def gather_start(number, arrivals, source, landing, part):
        for k in reversed(range(chips - 1)):
            remote(
                source, landing.at[(me,) + part], number, arrivals.at[part + (k,)], others[k]
            )
        remote(source, landing.at[(me,) + part], number, recv_sem.at[number], partner)

    def gather_relay(number, arrivals, landing, part):
        for k in range(chips - 1):
            block = landing.at[(others[k],) + part]
            taken(block, arrivals.at[part + (k,)])
            remote(block, block, number, recv_sem.at[number], partner)

    def gather_finish(number, landing):
        taken(landing.at[pl.ds(0, chips)], recv_sem.at[number])

    half = count // 2
    group, first = lax.rem(me, half), lax.div(me, half) * half

    def spread(number, source, landing, size):
        @pl.loop(1, size)
        def _(step):
            if size == count:
                peer = lax.rem(me + step, count)
            else:
                peer = first + lax.rem(group + step, size)
            remote(source(peer), landing, number, recv_sem.at[number], peer)

    loads[0].wait()
    loads[1].wait()
    pieces = []
    for i in range(rows):
        normed = layer_normalized(pair[i].astype(F32)).astype(BF16)
        pieces.append(dot(bias_w[...], normed, NT))
    slab = jnp.concatenate(pieces, 0).astype(BF16)
    bias_src[...] = slab
    bias_land[me] = slab
    pl.semaphore_wait(barrier, count - 1)
    gather_start(0, bias_sem, bias_src, bias_land, ())

    for load in loads[2:6]:
        load.wait()
    token = lax.broadcasted_iota(jnp.int32, (table.shape[0], length), 0)
    zero_rows = []
    for s in range(seqs):
        one_hot = jnp.where(ids[pl.ds(s, 1), :] == token, 1.0, 0.0).astype(BF16)
        zero_rows.append(align[s].astype(F32) + dot(one_hot, table[...], TN))
    msa_zero = jnp.concatenate(zero_rows, 0)
    projected = dot(layer_normalized(msa_zero).astype(BF16), row_w[...])
    masks = [head_mask(h, head_size, channels) for h in range(heads)]
    scale = head_size ** (-0.5)

    loads[6].wait()
    loads[7].wait()
    raw_scores, spread_values = [], []
    for s in range(seqs):
        part = projected[s * length : (s + 1) * length]
        query = (part[:, :channels] * scale).astype(BF16)
        key = part[:, channels : 2 * channels].astype(BF16)
        value = part[:, 2 * channels : 3 * channels].astype(BF16)
        stacked = jnp.concatenate([query * m for m in masks], 0)
        raw_scores.append(dot(stacked, key, NT))
        spread_values.append(jnp.concatenate([value * m for m in masks], 0))
    to_owner = selection(
        seqs * length,
        lambda o: (
            split_index(split_index(o, rows)[0], seqs)[1] * length
            + split_index(o, seqs * rows)[0] * rows
            + split_index(o, rows)[1]
        ),
    )
    for load in loads[8:]:
        load.wait()
    tri_t[...] = jnp.transpose(tri_w[:, : 4 * pair_chan].astype(F32), (1, 0)).astype(BF16)
    fill(outer_f, outer_w[...].astype(F32))
    for d in range(width):
        outer_w2[:, d * pair_chan : (d + 1) * pair_chan] = pick(
            outer_f, d, width, width
        ).astype(BF16)

    gather_relay(0, bias_sem, bias_land, ())
    gather_finish(0, bias_land)
    fill(bias_f, landed(bias_land))
    mask_bias = (mask[...].astype(F32) - 1.0) * 10000.0
    extra = jnp.concatenate(
        [pick(bias_f, h, length, heads) for h in range(heads)], 0
    ) + mask_bias
    one_rows = []
    for s in range(seqs):
        weights = softmax_rows(raw_scores[s] + extra)
        side = jnp.concatenate(
            [weights[h * length : (h + 1) * length] for h in range(heads)], 1
        )
        mixed = dot(side, spread_values[s])
        gate = projected[s * length : (s + 1) * length, 3 * channels :]
        gated = (jax.nn.sigmoid(gate) * mixed).astype(BF16)
        zero = msa_zero[s * length : (s + 1) * length]
        one_rows.append((zero + dot(gated, row_o[...])).astype(BF16))
    ordered = dot(to_owner, jnp.concatenate(one_rows, 0))
    ordered = ordered.reshape(count, seqs * rows, channels)
    lane_parts = channels // 128
    slabs = jnp.concatenate(
        [ordered[:, :, k * 128 : (k + 1) * 128] for k in range(lane_parts)], 1
    ).astype(BF16)
    msa_src[...] = slabs
    msa_land[me] = msa_src[me]
    spread(1, lambda peer: msa_src.at[peer], msa_land.at[me], count)

    to_output = selection(
        total * rows,
        lambda o: (
            split_index(o, rows)[1] * total
            + split_index(split_index(o, rows)[0], seqs)[1] * count
            + split_index(o, seqs * rows)[0]
        ),
    )
    taken(msa_land.at[pl.ds(0, count - 1)], recv_sem.at[1])
    fill(msa_f, landed(msa_land))
    step = lane_parts * seqs * rows
    column = jnp.concatenate(
        [
            jnp.concatenate(
                [
                    pick(msa_f, (k * seqs + s) * rows + i, count, step)
                    for i in range(rows)
                    for s in range(seqs)
                ],
                0,
            )
            for k in range(lane_parts)
        ],
        1,
    )
    pack = max(1, 128 // total)
    groups = width // pack
    lanes = pack * total
    lane = lax.broadcasted_iota(jnp.int32, (groups, lanes), 1)
    two_rows, inputs = [], []
    for start in range(0, rows, pack):
        block = column[start * total : (start + pack) * total]
        projected = dot(layer_normalized(block).astype(BF16), col_w[...])
        gated_rows = []
        for i in range(pack):
            part = projected[i * total : (i + 1) * total]
            query = (part[:, :channels] * scale).astype(BF16)
            key = part[:, channels : 2 * channels].astype(BF16)
            value = part[:, 2 * channels : 3 * channels].astype(BF16)
            stacked = jnp.concatenate([query * m for m in masks], 0)
            weights = softmax_rows(dot(stacked, key, NT))
            every = dot(weights, value)
            mixed = every[:total] * masks[0].astype(F32)
            for h in range(1, heads):
                mixed = mixed + every[h * total : (h + 1) * total] * masks[h].astype(F32)
            gated_rows.append((jax.nn.sigmoid(part[:, 3 * channels :]) * mixed).astype(BF16))
        msa_two = block + dot(jnp.concatenate(gated_rows, 0), col_o[...])
        outer_input = layer_normalized(msa_two).astype(BF16)
        two_rows.append(msa_two.astype(BF16))
        inputs.append(outer_input)

        right_t = dot(factor_w[width:, :], outer_input, NT)
        slabs = []
        for place in range(pack):
            joined = None
            for k in range(pack):
                piece = right_t[k * groups : (k + 1) * groups]
                shift = ((k - place) * total) % lanes
                if shift:
                    piece = pltpu.roll(piece, shift, 1)
                joined = piece if joined is None else jnp.where(lane >= k * total, piece, joined)
            slabs.append(joined)
        slab = jnp.concatenate(slabs, 0).astype(BF16)
        part = (start // pack,)
        right_src[part[0]] = slab
        right_land[me, part[0]] = slab
        gather_start(2, right_sem, right_src.at[part[0]], right_land, part)

    left = dot(jnp.concatenate(inputs, 0), factor_w[:width, :], NT).astype(BF16)
    chunk = 8
    for start in range(0, width, chunk):
        product = dot(left, outer_w2[:, start * pair_chan : (start + chunk) * pair_chan])
        for d in range(start, start + chunk):
            at = ((d % groups) * pack + d // groups) * total
            for i in range(rows):
                left_t[at : at + total, i * pair_chan : (i + 1) * pair_chan] = product[
                    i * total : (i + 1) * total,
                    (d - start) * pair_chan : (d - start + 1) * pair_chan,
                ].astype(BF16)

    for k in range(rows // pack):
        gather_relay(2, right_sem, right_land, (k,))
    gather_finish(2, right_land)
    fill(right_f, landed(right_land))
    for k in range(groups):
        right_m[:, k * lanes : (k + 1) * lanes] = pick(right_f, k, length, groups).astype(BF16)

    own = pair_chan // half
    normed = []
    pairs = tri_left.shape[0]
    pair_rows = rows // pairs
    for q in range(pairs):
        columns = pl.ds(q * pair_rows * pair_chan, pair_rows * pair_chan)
        update = dot(right_m[...], left_t[:, columns]) * (1.0 / total)
        sides = [[], []]
        for k in range(pair_rows):
            i = q * pair_rows + k
            one = pair[i].astype(F32) + update[:, k * pair_chan : (k + 1) * pair_chan]
            pair_one_v[i] = one
            normed.append(layer_normalized(one).astype(BF16))
            factors = dot(tri_t[...], normed[i], NT)
            for side in range(2):
                low = 2 * side * pair_chan
                sides[side].append(
                    jax.nn.sigmoid(factors[low + pair_chan : low + 2 * pair_chan])
                    * factors[low : low + pair_chan]
                )
        tri_left[q] = by_group(sides[0], half).astype(BF16)
        tri_right[q] = by_group(sides[1], half).astype(BF16)
        left_land[group, q] = tri_left[q, group]
        tri_land[me, q] = tri_right[q, group]
        spread(
            3, lambda peer: tri_right.at[q, lax.rem(peer, half)], tri_land.at[me, q], count
        )
        spread(4, lambda peer: tri_left.at[q, lax.rem(peer, half)], left_land.at[group, q], half)

    ordered = dot(to_output, jnp.concatenate(two_rows, 0))
    align_out[...] = ordered.reshape(total, rows, channels).astype(BF16)
    for i in range(rows):
        gate_v[i] = jax.nn.sigmoid(dot(normed[i], tri_w[:, 4 * pair_chan :]))
    taken(tri_land.at[pl.ds(0, count - 1)], recv_sem.at[3])
    taken(left_land.at[pl.ds(0, half - 1)], recv_sem.at[4])
    fill(land_f, landed(tri_land))
    fill(left_f, landed(left_land))
    block = half * rows
    for c in range(own):
        left_side = jnp.concatenate(
            [pick(left_f, i * own + c, half, own * rows) for i in range(rows)], 0
        ).astype(BF16)
        right_side = pick(land_f, c, length, own).astype(BF16)
        fill(comb_f.at[:, pl.ds(c * block, block), :], dot(left_side, right_side, NT))
    for p in range(half):
        back_src[p] = pick(comb_f, p, own * rows, half).astype(BF16)
    back_land[group] = back_src[group]
    spread(5, lambda peer: back_src.at[lax.rem(peer, half)], back_land.at[group], half)

    taken(back_land.at[pl.ds(0, half - 1)], recv_sem.at[5])
    for number, sent in enumerate((bias_land, msa_land, right_land, tri_land)):
        taken(sent.at[pl.ds(0, count - 1)], send_sem.at[number])
    taken(left_land.at[pl.ds(0, half - 1)], send_sem.at[4])
    taken(back_land.at[pl.ds(0, half - 1)], send_sem.at[5])


def finish_kernel(rows, align, back_land, pair_one, gate, tri_o, align_out, pair_out, back_f, pair_v, sem):
    store_align = pltpu.make_async_copy(align, align_out, sem.at[0])
    store_align.start()
    fill(back_f, landed(back_land))
    for i in range(rows):
        combined = layer_normalized(pick(back_f, i, pair_one.shape[2], rows), 0).astype(BF16)
        result = pair_one[i] + gate[i] * dot(combined, tri_o[...], TN)
        pair_v[i] = result.astype(BF16)
    store_pair = pltpu.make_async_copy(pair_v, pair_out, sem.at[1])
    store_pair.start()
    store_align.wait()
    store_pair.wait()


def shards(
    homolog_symbol_ids,
    residue_attend_mask,
    alignment_state,
    pair,
    symbol_lookup_matrix,
    pair_bias_weight,
    row_projection_weight,
    horizontal_readout_matrix,
    column_projection_weight,
    vertical_readout_matrix,
    product_factor_matrices,
    outer_output_weight,
    triangle_input_weight,
    triangle_output_weight,
):
    count = lax.axis_size("res")
    seqs, length, channels = alignment_state.shape
    rows, _, pair_chan = pair.shape
    heads = pair_bias_weight.shape[1]
    width = product_factor_matrices.shape[1] // 2
    total = seqs * count
    half = count // 2
    own = pair_chan // half
    pack = max(1, 128 // total)
    groups, lanes = width // pack, pack * total
    operands = [
        homolog_symbol_ids,
        residue_attend_mask.reshape(1, length),
        alignment_state,
        pair,
        symbol_lookup_matrix,
        pair_bias_weight.T,
        row_projection_weight,
        horizontal_readout_matrix,
        column_projection_weight,
        vertical_readout_matrix,
        product_factor_matrices.T,
        outer_output_weight,
        triangle_input_weight,
    ]
    lane_parts = channels // 128
    vmem = pltpu.VMEM
    parts, pairs = rows // pack, 2
    tri_slab = (pairs, half, own * rows // pairs, length)
    exchanges = [
        vmem((heads * rows, length), BF16),
        vmem((count, heads * rows, length), BF16),
        vmem((count, lane_parts * seqs * rows, 128), BF16),
        vmem((count, lane_parts * seqs * rows, 128), BF16),
        vmem((parts, groups * pack, lanes), BF16),
        vmem((count, parts, groups * pack, lanes), BF16),
        vmem(tri_slab, BF16),
        vmem((half, pairs) + tri_slab[2:], BF16),
        vmem(tri_slab, BF16),
        vmem((count, pairs) + tri_slab[2:], BF16),
        vmem((half, own * rows, length), BF16),
    ]

    def pieces(row_count, lane_count):
        return vmem((lane_count // 128, row_count, 128), F32)

    scratch = (
        [vmem(x.shape, x.dtype) for x in operands]
        + exchanges
        + [
            pieces(count * heads * rows, length),
            pieces(count * lane_parts * seqs * rows, 128),
            pieces(width * width, pair_chan),
            vmem((width, width * pair_chan), BF16),
            vmem((width * total, rows * pair_chan), BF16),
            pieces(length * groups, lanes),
            vmem((length, width * total), BF16),
            vmem((4 * pair_chan, pair_chan), BF16),
            pieces(count * own * rows, length),
            pieces(half * own * rows, length),
            pieces(half * own * rows, length),
            pltpu.SemaphoreType.DMA((len(operands),)),
            pltpu.SemaphoreType.DMA((6,)),
            pltpu.SemaphoreType.DMA((6,)),
            pltpu.SemaphoreType.DMA((half - 1,)),
            pltpu.SemaphoreType.DMA((parts, half - 1)),
        ]
    )
    sizes = (count, seqs, rows, length, channels, heads, width, pair_chan, total)
    anywhere = pl.BlockSpec(memory_space=pltpu.HBM)
    inside = pl.BlockSpec(memory_space=pltpu.VMEM)
    aligned, back, pair_one, gate = pl.pallas_call(
        functools.partial(block_kernel, sizes),
        out_shape=(
            jax.ShapeDtypeStruct((total, rows, channels), BF16),
            jax.ShapeDtypeStruct((half, own * rows, length), BF16),
            jax.ShapeDtypeStruct(pair.shape, F32),
            jax.ShapeDtypeStruct(pair.shape, F32),
        ),
        in_specs=[anywhere] * len(operands),
        out_specs=(inside,) * 4,
        scratch_shapes=scratch,
        compiler_params=pltpu.CompilerParams(
            collective_id=0, has_side_effects=True, vmem_limit_bytes=VMEM_BYTES
        ),
    )(*[pltpu.with_memory_space_constraint(x, pltpu.HBM) for x in operands])
    return pl.pallas_call(
        functools.partial(finish_kernel, rows),
        out_shape=(
            jax.ShapeDtypeStruct((total, rows, channels), BF16),
            jax.ShapeDtypeStruct(pair.shape, BF16),
        ),
        in_specs=[inside] * 5,
        out_specs=(anywhere, anywhere),
        scratch_shapes=[
            pieces(half * own * rows, length),
            vmem(pair.shape, BF16),
            pltpu.SemaphoreType.DMA((2,)),
        ],
        compiler_params=pltpu.CompilerParams(vmem_limit_bytes=VMEM_BYTES // 4),
    )(aligned, back, pair_one, gate, triangle_output_weight)


def solution(mesh):
    placed = (
        P(("crop", "res"), None),
        P("crop"),
        P(("crop", "res"), None, None),
        P(("crop", "res"), None, None),
        P(),
        P(),
        P(),
        P(),
        P(),
        P(),
        P(),
        P(),
        P(),
        P(),
    )
    return jax.shard_map(
        shards,
        mesh=mesh,
        in_specs=placed,
        out_specs=(P("crop", "res", None), P(("crop", "res"), None, None)),
        check_vma=False,
    )
```

```python
import functools

import jax
import jax.numpy as jnp
from jax import lax
from jax.experimental import pallas as pl
from jax.experimental.pallas import tpu as pltpu
from jax.sharding import PartitionSpec as P

EPSILON = 1e-05
MESH = pl.DeviceIdType.MESH
VMEM_BYTES = 40 * 1024 * 1024
F32 = jnp.float32
BF16 = jnp.bfloat16

NN = (((1,), (0,)), ((), ()))
NT = (((1,), (1,)), ((), ()))
TN = (((0,), (0,)), ((), ()))


def dot(a, b, dims=NN):
    return lax.dot_general(a, b, dims, preferred_element_type=F32)


def layer_normalized(rows, axis=-1):
    average = jnp.mean(rows, axis, keepdims=True)
    centred = rows - average
    spread = jnp.mean(centred * centred, axis, keepdims=True)
    return centred * lax.rsqrt(spread + EPSILON)


def split_index(index, size):
    if size & (size - 1) == 0:
        return lax.shift_right_logical(index, jnp.int32(size.bit_length() - 1)), index & (size - 1)
    return lax.div(index, size), lax.rem(index, size)


def selection(size, source):
    row = lax.broadcasted_iota(jnp.int32, (size, size), 0)
    column = lax.broadcasted_iota(jnp.int32, (size, size), 1)
    return jnp.where(column == source(row), 1.0, 0.0).astype(BF16)


def head_mask(head, head_size, channels):
    lane = lax.broadcasted_iota(jnp.int32, (1, channels), 1)
    inside = (lane >= head * head_size) & (lane < (head + 1) * head_size)
    return jnp.where(inside, 1.0, 0.0).astype(BF16)


def fill(buffer, values):
    for k in range(buffer.shape[0]):
        buffer[k] = values[:, k * 128 : (k + 1) * 128]


def pick(buffer, start, size, stride):
    return jnp.concatenate(
        [buffer[k, pl.ds(start, size, stride=stride), :] for k in range(buffer.shape[0])], 1
    )


def landed(landing):
    blocks = landing[...].astype(F32)
    return blocks.reshape(-1, blocks.shape[-1])


def pack_lanes(block, pack, size):
    if pack == 1:
        return [block]
    height, lanes = block.shape[0] // pack, pack * size
    lane = lax.broadcasted_iota(jnp.int32, (height, lanes), 1)
    packed = []
    for place in range(pack):
        joined = None
        for k in range(pack):
            piece = block[k * height : (k + 1) * height]
            shift = ((k - place) * size) % lanes
            if shift:
                piece = pltpu.roll(piece, shift, 1)
            joined = piece if joined is None else jnp.where(lane >= k * size, piece, joined)
        packed.append(joined)
    return packed


def softmax_rows(scores):
    top = jnp.max(scores, -1, keepdims=True)
    powers = jnp.exp(scores - top)
    return (powers / jnp.sum(powers, -1, keepdims=True)).astype(BF16)


def block_kernel(
    sizes,
    ids_h, mask_h, align_h, pair_h, table_h, bias_w_h, row_w_h, row_o_h, col_w_h, col_o_h,
    factor_w_h, outer_w_h, tri_w_h,
    align_out, back_land, pair_one_v, gate_v,
    ids, mask, align, pair, table, bias_w, row_w, row_o, col_w, col_o,
    factor_w, outer_w, tri_w,
    bias_src, bias_land, msa_src, msa_land, right_src, right_land, tri_left, left_land,
    tri_right, tri_land, back_src,
    bias_f, msa_f, outer_f, outer_w2, left_t, right_f, right_m, tri_t,
    tri_f, land_f, left_f, comb_f,
    in_sem, send_sem, recv_sem, bias_sem, right_sem,
):
    count, seqs, rows, length, channels, heads, width, pair_chan, total = sizes
    head_size = channels // heads
    me = lax.axis_index("res")
    barrier = pltpu.get_barrier_semaphore()

    @pl.loop(1, count)
    def _(step):
        pl.semaphore_signal(
            barrier, inc=1, device_id={"res": lax.rem(me + step, count)}, device_id_type=MESH
        )

    staged = [
        (pair_h, pair), (bias_w_h, bias_w), (align_h, align), (ids_h, ids), (table_h, table),
        (row_w_h, row_w), (mask_h, mask), (row_o_h, row_o), (col_w_h, col_w), (col_o_h, col_o),
        (factor_w_h, factor_w), (outer_w_h, outer_w), (tri_w_h, tri_w),
    ]
    loads = [
        pltpu.make_async_copy(source, target, in_sem.at[k])
        for k, (source, target) in enumerate(staged)
    ]
    for load in loads:
        load.start()

    def remote(source, target, number, received_by, peer):
        pltpu.make_async_remote_copy(
            src_ref=source,
            dst_ref=target,
            send_sem=send_sem.at[number],
            recv_sem=received_by,
            device_id={"res": peer},
            device_id_type=MESH,
        ).start()

    def taken(landing, semaphore):
        pltpu.make_async_copy(landing, landing, semaphore).wait()

    chips = count // 2
    partner = me + 1 - 2 * lax.rem(me, 2)
    flips = [
        (1 - 2 * lax.rem(lax.div(me, 2 << j), 2)) * (2 << j) for j in range(chips.bit_length() - 1)
    ]
    others = [me + sum(flips[j] for j in range(len(flips)) if (k >> j) & 1) for k in range(1, chips)]

    def gather_start(number, arrivals, source, landing, part):
        for k in reversed(range(chips - 1)):
            remote(
                source, landing.at[(me,) + part], number, arrivals.at[part + (k,)], others[k]
            )
        remote(source, landing.at[(me,) + part], number, recv_sem.at[number], partner)

    def gather_relay(number, arrivals, landing, part, steps, handed):
        for k in steps:
            block = landing.at[(others[k],) + part]
            taken(block, arrivals.at[part + (k,)])
            remote(block, block, number, recv_sem.at[handed], partner)

    def gather_finish(handed, landing, blocks):
        taken(landing.at[pl.ds(0, blocks)], recv_sem.at[handed])

    half = count // 2
    group, first = lax.rem(me, half), lax.div(me, half) * half

    def spread(number, source, landing, size):
        @pl.loop(1, size)
        def _(step):
            if size == count:
                peer = lax.rem(me + step, count)
            else:
                peer = first + lax.rem(group + step, size)
            remote(source(peer), landing, number, recv_sem.at[number], peer)

    loads[0].wait()
    loads[1].wait()
    pieces = []
    for i in range(rows):
        normed = layer_normalized(pair[i].astype(F32)).astype(BF16)
        pieces.append(dot(bias_w[...], normed, NT))
    slab = jnp.concatenate(pieces, 0).astype(BF16)
    bias_src[...] = slab
    bias_land[me] = slab
    pl.semaphore_wait(barrier, count - 1)
    gather_start(0, bias_sem, bias_src, bias_land, ())

    for load in loads[2:6]:
        load.wait()
    token = lax.broadcasted_iota(jnp.int32, (table.shape[0], length), 0)
    zero_rows = []
    for s in range(seqs):
        one_hot = jnp.where(ids[pl.ds(s, 1), :] == token, 1.0, 0.0).astype(BF16)
        zero_rows.append(align[s].astype(F32) + dot(one_hot, table[...], TN))
    msa_zero = jnp.concatenate(zero_rows, 0)
    projected = dot(layer_normalized(msa_zero).astype(BF16), row_w[...])
    masks = [head_mask(h, head_size, channels) for h in range(heads)]
    scale = head_size ** (-0.5)

    loads[6].wait()
    loads[7].wait()
    raw_scores, spread_values = [], []
    for s in range(seqs):
        part = projected[s * length : (s + 1) * length]
        query = (part[:, :channels] * scale).astype(BF16)
        key = part[:, channels : 2 * channels].astype(BF16)
        value = part[:, 2 * channels : 3 * channels].astype(BF16)
        stacked = jnp.concatenate([query * m for m in masks], 0)
        raw_scores.append(dot(stacked, key, NT))
        spread_values.append(jnp.concatenate([value * m for m in masks], 0))
    to_owner = selection(
        seqs * length,
        lambda o: (
            split_index(split_index(o, rows)[0], seqs)[1] * length
            + split_index(o, seqs * rows)[0] * rows
            + split_index(o, rows)[1]
        ),
    )
    for load in loads[8:]:
        load.wait()
    tri_t[...] = jnp.transpose(tri_w[:, : 4 * pair_chan].astype(F32), (1, 0)).astype(BF16)
    fill(outer_f, outer_w[...].astype(F32))
    for d in range(width):
        outer_w2[:, d * pair_chan : (d + 1) * pair_chan] = pick(
            outer_f, d, width, width
        ).astype(BF16)

    gather_relay(0, bias_sem, bias_land, (), range(chips - 1), 0)
    gather_finish(0, bias_land, chips)
    fill(bias_f, landed(bias_land))
    mask_bias = (mask[...].astype(F32) - 1.0) * 10000.0
    extra = jnp.concatenate(
        [pick(bias_f, h, length, heads) for h in range(heads)], 0
    ) + mask_bias
    one_rows = []
    for s in range(seqs):
        weights = softmax_rows(raw_scores[s] + extra)
        side = jnp.concatenate(
            [weights[h * length : (h + 1) * length] for h in range(heads)], 1
        )
        mixed = dot(side, spread_values[s])
        gate = projected[s * length : (s + 1) * length, 3 * channels :]
        gated = (jax.nn.sigmoid(gate) * mixed).astype(BF16)
        zero = msa_zero[s * length : (s + 1) * length]
        one_rows.append((zero + dot(gated, row_o[...])).astype(BF16))
    ordered = dot(to_owner, jnp.concatenate(one_rows, 0))
    ordered = ordered.reshape(count, seqs * rows, channels)
    lane_parts = channels // 128
    slabs = jnp.concatenate(
        [ordered[:, :, k * 128 : (k + 1) * 128] for k in range(lane_parts)], 1
    ).astype(BF16)
    msa_src[...] = slabs
    msa_land[me] = msa_src[me]
    spread(1, lambda peer: msa_src.at[peer], msa_land.at[me], count)

    to_output = selection(
        total * rows,
        lambda o: (
            split_index(o, rows)[1] * total
            + split_index(split_index(o, rows)[0], seqs)[1] * count
            + split_index(o, seqs * rows)[0]
        ),
    )
    taken(msa_land.at[pl.ds(0, count - 1)], recv_sem.at[1])
    fill(msa_f, landed(msa_land))
    step = lane_parts * seqs * rows
    column = jnp.concatenate(
        [
            jnp.concatenate(
                [
                    pick(msa_f, (k * seqs + s) * rows + i, count, step)
                    for i in range(rows)
                    for s in range(seqs)
                ],
                0,
            )
            for k in range(lane_parts)
        ],
        1,
    )
    pack = max(1, 128 // total)
    groups = width // pack
    lanes = pack * total
    two_rows, inputs = [], []
    for start in range(0, rows, pack):
        block = column[start * total : (start + pack) * total]
        projected = dot(layer_normalized(block).astype(BF16), col_w[...])
        gated_rows = []
        for i in range(pack):
            part = projected[i * total : (i + 1) * total]
            query = (part[:, :channels] * scale).astype(BF16)
            key = part[:, channels : 2 * channels].astype(BF16)
            value = part[:, 2 * channels : 3 * channels].astype(BF16)
            stacked = jnp.concatenate([query * m for m in masks], 0)
            weights = softmax_rows(dot(stacked, key, NT))
            every = dot(weights, value)
            mixed = every[:total] * masks[0].astype(F32)
            for h in range(1, heads):
                mixed = mixed + every[h * total : (h + 1) * total] * masks[h].astype(F32)
            gated_rows.append((jax.nn.sigmoid(part[:, 3 * channels :]) * mixed).astype(BF16))
        msa_two = block + dot(jnp.concatenate(gated_rows, 0), col_o[...])
        outer_input = layer_normalized(msa_two).astype(BF16)
        two_rows.append(msa_two.astype(BF16))
        inputs.append(outer_input)

        right_t = dot(factor_w[width:, :], outer_input, NT)
        slab = jnp.concatenate(pack_lanes(right_t, pack, total), 0).astype(BF16)
        part = (start // pack,)
        right_src[part[0]] = slab
        right_land[me, part[0]] = slab
        gather_start(2, right_sem, right_src.at[part[0]], right_land, part)

    left = dot(jnp.concatenate(inputs, 0), factor_w[:width, :], NT).astype(BF16)
    chunk = 8
    for start in range(0, width, chunk):
        product = dot(left, outer_w2[:, start * pair_chan : (start + chunk) * pair_chan])
        for d in range(start, start + chunk):
            at = ((d % groups) * pack + d // groups) * total
            for i in range(rows):
                left_t[at : at + total, i * pair_chan : (i + 1) * pair_chan] = product[
                    i * total : (i + 1) * total,
                    (d - start) * pair_chan : (d - start + 1) * pair_chan,
                ].astype(BF16)

    own = pair_chan // half
    near = chips // 2 - 1
    reach = half * rows
    fold = max(1, 128 // reach)
    height = pair_chan // fold
    normed, starts = [], []
    for turn in range(2):
        if turn == 0:
            steps, blocks, which = range(near), chips // 2, lax.div(me, half)
        else:
            steps, blocks, which = range(near, chips - 1), chips // 2, 1 - lax.div(me, half)
        for k in range(rows // pack):
            gather_relay(2, right_sem, right_land, (k,), steps, 2 + 4 * turn)
        gather_finish(2 + 4 * turn, right_land, blocks)
        fill(right_f, landed(right_land.at[pl.ds(which * half, half)]))
        for k in range(groups):
            right_m[:, k * lanes : (k + 1) * lanes] = pick(right_f, k, reach, groups).astype(BF16)
        update = dot(right_m[...], left_t[...]) * (1.0 / total)
        start = pl.multiple_of(which * reach, reach)
        stacked = []
        for i in range(rows):
            one = pair[i, pl.ds(start, reach), :].astype(F32) + update[
                :, i * pair_chan : (i + 1) * pair_chan
            ]
            pair_one_v[i, pl.ds(start, reach), :] = one
            stacked.append(one)
        normed.append(layer_normalized(jnp.concatenate(stacked, 0)).astype(BF16))
        starts.append(start)
        factors = dot(tri_t[...], normed[turn], NT)
        for side, target in enumerate((tri_left, tri_right)):
            low = 2 * side * pair_chan
            factor = (
                jax.nn.sigmoid(factors[low + pair_chan : low + 2 * pair_chan])
                * factors[low : low + pair_chan]
            )
            wide = fold * reach
            for base in range(rows // fold):
                packed = pack_lanes(factor[:, base * wide : (base + 1) * wide], fold, reach)
                for place in range(fold):
                    at = (base * fold + place) * height
                    fill(tri_f.at[:, pl.ds(at, height), :], packed[place])
            for g in range(half):
                target[turn, g] = pick(tri_f, g, rows * own // fold, half).astype(BF16)
        left_land[which, group] = tri_left[turn, group]
        tri_land[which, me] = tri_right[turn, group]
        spread(
            3,
            lambda peer: tri_right.at[turn, lax.rem(peer, half)],
            tri_land.at[which, me],
            count,
        )
        spread(
            4,
            lambda peer: tri_left.at[turn, lax.rem(peer, half)],
            left_land.at[which, group],
            half,
        )

    ordered = dot(to_output, jnp.concatenate(two_rows, 0))
    align_out[...] = ordered.reshape(total, rows, channels).astype(BF16)
    for turn in range(2):
        opened = jax.nn.sigmoid(dot(normed[turn], tri_w[:, 4 * pair_chan :]))
        for i in range(rows):
            gate_v[i, pl.ds(starts[turn], reach), :] = opened[i * reach : (i + 1) * reach]

    taken(tri_land.at[pl.ds(0, 2), pl.ds(0, count - 1)], recv_sem.at[3])
    taken(left_land.at[pl.ds(0, 2), pl.ds(0, half - 1)], recv_sem.at[4])
    fill(land_f, landed(tri_land))
    fill(left_f, landed(left_land))
    slab_rows = rows * own // fold
    block = half * rows
    lane = lax.broadcasted_iota(jnp.int32, (1, fold * reach), 1)
    folds = [
        jnp.where((lane >= k * reach) & (lane < (k + 1) * reach), 1.0, 0.0).astype(BF16)
        for k in range(fold)
    ]
    for c in range(own // fold):
        step = own // fold
        left_sides = [
            jnp.concatenate(
                [
                    pick(left_f, q * half * slab_rows + i * step + c, half, slab_rows)
                    for i in range(rows)
                ],
                0,
            ).astype(BF16)
            for q in range(2)
        ]
        right_side = jnp.concatenate(
            [pick(land_f, q * count * slab_rows + c, length, step) for q in range(2)], 1
        ).astype(BF16)
        left_side = jnp.concatenate(
            [jnp.concatenate([side * m for side in left_sides], 1) for m in folds], 0
        )
        product = dot(left_side, right_side, NT)
        for k in range(fold):
            fill(
                comb_f.at[:, pl.ds((k * step + c) * block, block), :],
                product[k * block : (k + 1) * block],
            )
    for p in range(half):
        back_src[p] = pick(comb_f, p, own * rows, half).astype(BF16)
    back_land[group] = back_src[group]
    spread(5, lambda peer: back_src.at[lax.rem(peer, half)], back_land.at[group], half)

    taken(back_land.at[pl.ds(0, half - 1)], recv_sem.at[5])
    for number, sent in enumerate((bias_land, msa_land, right_land)):
        taken(sent.at[pl.ds(0, count - 1)], send_sem.at[number])
    taken(tri_land.at[pl.ds(0, 2), pl.ds(0, count - 1)], send_sem.at[3])
    taken(left_land.at[pl.ds(0, 2), pl.ds(0, half - 1)], send_sem.at[4])
    taken(back_land.at[pl.ds(0, half - 1)], send_sem.at[5])


def finish_kernel(rows, align, back_land, pair_one, gate, tri_o, align_out, pair_out, back_f, pair_v, sem):
    store_align = pltpu.make_async_copy(align, align_out, sem.at[0])
    store_align.start()
    fill(back_f, landed(back_land))
    owners = back_land.shape[0]
    own = back_land.shape[1] // rows
    for i in range(rows):
        channels = [pick(back_f, c * rows + i, owners, own * rows) for c in range(own)]
        combined = layer_normalized(jnp.concatenate(channels, 0), 0).astype(BF16)
        result = pair_one[i] + gate[i] * dot(combined, tri_o[...], TN)
        pair_v[i] = result.astype(BF16)
    store_pair = pltpu.make_async_copy(pair_v, pair_out, sem.at[1])
    store_pair.start()
    store_align.wait()
    store_pair.wait()


def shards(
    homolog_symbol_ids,
    residue_attend_mask,
    alignment_state,
    pair,
    symbol_lookup_matrix,
    pair_bias_weight,
    row_projection_weight,
    horizontal_readout_matrix,
    column_projection_weight,
    vertical_readout_matrix,
    product_factor_matrices,
    outer_output_weight,
    triangle_input_weight,
    triangle_output_weight,
):
    count = lax.axis_size("res")
    seqs, length, channels = alignment_state.shape
    rows, _, pair_chan = pair.shape
    heads = pair_bias_weight.shape[1]
    width = product_factor_matrices.shape[1] // 2
    total = seqs * count
    half = count // 2
    own = pair_chan // half
    pack = max(1, 128 // total)
    groups, lanes = width // pack, pack * total
    operands = [
        homolog_symbol_ids,
        residue_attend_mask.reshape(1, length),
        alignment_state,
        pair,
        symbol_lookup_matrix,
        pair_bias_weight.T,
        row_projection_weight,
        horizontal_readout_matrix,
        column_projection_weight,
        vertical_readout_matrix,
        product_factor_matrices.T,
        outer_output_weight,
        triangle_input_weight,
    ]
    lane_parts = channels // 128
    vmem = pltpu.VMEM
    parts = rows // pack
    reach = half * rows
    fold = max(1, 128 // reach)
    tri_slab = (rows * own // fold, fold * reach)
    exchanges = [
        vmem((heads * rows, length), BF16),
        vmem((count, heads * rows, length), BF16),
        vmem((count, lane_parts * seqs * rows, 128), BF16),
        vmem((count, lane_parts * seqs * rows, 128), BF16),
        vmem((parts, groups * pack, lanes), BF16),
        vmem((count, parts, groups * pack, lanes), BF16),
        vmem((2, half) + tri_slab, BF16),
        vmem((2, half) + tri_slab, BF16),
        vmem((2, half) + tri_slab, BF16),
        vmem((2, count) + tri_slab, BF16),
        vmem((half, own * rows, length), BF16),
    ]

    def pieces(row_count, lane_count):
        return vmem((lane_count // 128, row_count, 128), F32)

    scratch = (
        [vmem(x.shape, x.dtype) for x in operands]
        + exchanges
        + [
            pieces(count * heads * rows, length),
            pieces(count * lane_parts * seqs * rows, 128),
            pieces(width * width, pair_chan),
            vmem((width, width * pair_chan), BF16),
            vmem((width * total, rows * pair_chan), BF16),
            pieces(reach * groups, lanes),
            vmem((reach, width * total), BF16),
            vmem((4 * pair_chan, pair_chan), BF16),
            pieces(rows * pair_chan // fold, fold * reach),
            pieces(2 * count * tri_slab[0], tri_slab[1]),
            pieces(2 * half * tri_slab[0], tri_slab[1]),
            pieces(half * own * rows, length),
            pltpu.SemaphoreType.DMA((len(operands),)),
            pltpu.SemaphoreType.DMA((6,)),
            pltpu.SemaphoreType.DMA((7,)),
            pltpu.SemaphoreType.DMA((half - 1,)),
            pltpu.SemaphoreType.DMA((parts, half - 1)),
        ]
    )
    sizes = (count, seqs, rows, length, channels, heads, width, pair_chan, total)
    anywhere = pl.BlockSpec(memory_space=pltpu.HBM)
    inside = pl.BlockSpec(memory_space=pltpu.VMEM)
    aligned, back, pair_one, gate = pl.pallas_call(
        functools.partial(block_kernel, sizes),
        out_shape=(
            jax.ShapeDtypeStruct((total, rows, channels), BF16),
            jax.ShapeDtypeStruct((half, own * rows, length), BF16),
            jax.ShapeDtypeStruct(pair.shape, F32),
            jax.ShapeDtypeStruct(pair.shape, F32),
        ),
        in_specs=[anywhere] * len(operands),
        out_specs=(inside,) * 4,
        scratch_shapes=scratch,
        compiler_params=pltpu.CompilerParams(
            collective_id=0, has_side_effects=True, vmem_limit_bytes=VMEM_BYTES
        ),
    )(*[pltpu.with_memory_space_constraint(x, pltpu.HBM) for x in operands])
    return pl.pallas_call(
        functools.partial(finish_kernel, rows),
        out_shape=(
            jax.ShapeDtypeStruct((total, rows, channels), BF16),
            jax.ShapeDtypeStruct(pair.shape, BF16),
        ),
        in_specs=[inside] * 5,
        out_specs=(anywhere, anywhere),
        scratch_shapes=[
            pieces(half * own * rows, length),
            vmem(pair.shape, BF16),
            pltpu.SemaphoreType.DMA((2,)),
        ],
        compiler_params=pltpu.CompilerParams(vmem_limit_bytes=VMEM_BYTES // 4),
    )(aligned, back, pair_one, gate, triangle_output_weight)


def solution(mesh):
    placed = (
        P(("crop", "res"), None),
        P("crop"),
        P(("crop", "res"), None, None),
        P(("crop", "res"), None, None),
        P(),
        P(),
        P(),
        P(),
        P(),
        P(),
        P(),
        P(),
        P(),
        P(),
    )
    return jax.shard_map(
        shards,
        mesh=mesh,
        in_specs=placed,
        out_specs=(P("crop", "res", None), P(("crop", "res"), None, None)),
        check_vma=False,
    )
```

```python
import functools

import jax
import jax.numpy as jnp
from jax import lax
from jax.experimental import pallas as pl
from jax.experimental.pallas import tpu as pltpu
from jax.sharding import PartitionSpec as P

EPSILON = 1e-05
MESH = pl.DeviceIdType.MESH
VMEM_BYTES = 40 * 1024 * 1024
F32 = jnp.float32
BF16 = jnp.bfloat16

NN = (((1,), (0,)), ((), ()))
NT = (((1,), (1,)), ((), ()))
TN = (((0,), (0,)), ((), ()))


def dot(a, b, dims=NN):
    return lax.dot_general(a, b, dims, preferred_element_type=F32)


def layer_normalized(rows, axis=-1):
    average = jnp.mean(rows, axis, keepdims=True)
    centred = rows - average
    spread = jnp.mean(centred * centred, axis, keepdims=True)
    return centred * lax.rsqrt(spread + EPSILON)


def split_index(index, size):
    if size & (size - 1) == 0:
        return lax.shift_right_logical(index, jnp.int32(size.bit_length() - 1)), index & (size - 1)
    return lax.div(index, size), lax.rem(index, size)


def selection(size, source):
    row = lax.broadcasted_iota(jnp.int32, (size, size), 0)
    column = lax.broadcasted_iota(jnp.int32, (size, size), 1)
    return jnp.where(column == source(row), 1.0, 0.0).astype(BF16)


def head_mask(head, head_size, channels):
    lane = lax.broadcasted_iota(jnp.int32, (1, channels), 1)
    inside = (lane >= head * head_size) & (lane < (head + 1) * head_size)
    return jnp.where(inside, 1.0, 0.0).astype(BF16)


def fill(buffer, values):
    for k in range(buffer.shape[0]):
        buffer[k] = values[:, k * 128 : (k + 1) * 128]


def pick(buffer, start, size, stride):
    return jnp.concatenate(
        [buffer[k, pl.ds(start, size, stride=stride), :] for k in range(buffer.shape[0])], 1
    )


def landed(landing):
    blocks = landing[...].astype(F32)
    return blocks.reshape(-1, blocks.shape[-1])


def pack_lanes(block, pack, size):
    if pack == 1:
        return [block]
    height, lanes = block.shape[0] // pack, pack * size
    lane = lax.broadcasted_iota(jnp.int32, (height, lanes), 1)
    packed = []
    for place in range(pack):
        joined = None
        for k in range(pack):
            piece = block[k * height : (k + 1) * height]
            shift = ((k - place) * size) % lanes
            if shift:
                piece = pltpu.roll(piece, shift, 1)
            joined = piece if joined is None else jnp.where(lane >= k * size, piece, joined)
        packed.append(joined)
    return packed


def attend(scores, values, ones):
    powers = jnp.exp(scores - jnp.max(scores, -1, keepdims=True)).astype(BF16)
    side = jnp.concatenate([powers[h] for h in range(powers.shape[0])], 1)
    return dot(side, values) / dot(side, ones)


def interleave(blocks, rows):
    owners, lanes = blocks[0].shape[0] // rows, blocks[0].shape[1]
    if len(blocks) == 2 and rows == 4:
        one, two = [b.reshape(owners // 2, 8, lanes) for b in blocks]
        low = lax.broadcasted_iota(jnp.int32, one.shape, 1) < rows
        even = jnp.where(low, one, pltpu.roll(two, rows, 1))
        odd = jnp.where(low, pltpu.roll(one, rows, 1), two)
        return jnp.stack([even, odd], 1).reshape(owners, 8, lanes)
    return jnp.stack(
        [
            jnp.concatenate([b[p * rows : (p + 1) * rows] for b in blocks], 0)
            for p in range(owners)
        ],
        0,
    )


def block_kernel(
    sizes,
    ids_h, mask_h, align_h, pair_h, table_h, bias_w_h, row_w_h, row_o_h, col_w_h, col_o_h,
    factor_w_h, outer_w_h, tri_w_h,
    align_out, back_land, pair_one_v, gate_v,
    ids, mask, align, pair, table, bias_w, row_w, row_o, col_w, col_o,
    factor_w, outer_w, tri_w,
    bias_src, bias_land, msa_src, msa_land, right_src, right_land, tri_left, left_land,
    tri_right, tri_land, back_src,
    bias_f, msa_f, outer_f, outer_w2, left_t, right_f, right_m, tri_t,
    tri_f, land_f, left_f, comb_f, zero_v, raw_v, value_v, open_v,
    in_sem, send_sem, recv_sem, bias_sem, right_sem,
):
    count, seqs, rows, length, channels, heads, width, pair_chan, total = sizes
    head_size = channels // heads
    me = lax.axis_index("res")
    barrier = pltpu.get_barrier_semaphore()

    @pl.loop(1, count)
    def _(step):
        pl.semaphore_signal(
            barrier, inc=1, device_id={"res": lax.rem(me + step, count)}, device_id_type=MESH
        )

    staged = [
        (pair_h, pair), (bias_w_h, bias_w), (align_h, align), (ids_h, ids), (table_h, table),
        (row_w_h, row_w), (mask_h, mask), (row_o_h, row_o), (col_w_h, col_w), (col_o_h, col_o),
        (factor_w_h, factor_w), (outer_w_h, outer_w), (tri_w_h, tri_w),
    ]
    loads = [
        pltpu.make_async_copy(source, target, in_sem.at[k])
        for k, (source, target) in enumerate(staged)
    ]
    for load in loads:
        load.start()

    def remote(source, target, number, received_by, peer):
        pltpu.make_async_remote_copy(
            src_ref=source,
            dst_ref=target,
            send_sem=send_sem.at[number],
            recv_sem=received_by,
            device_id={"res": peer},
            device_id_type=MESH,
        ).start()

    def taken(landing, semaphore):
        pltpu.make_async_copy(landing, landing, semaphore).wait()

    chips = count // 2
    partner = me + 1 - 2 * lax.rem(me, 2)
    flips = [
        (1 - 2 * lax.rem(lax.div(me, 2 << j), 2)) * (2 << j) for j in range(chips.bit_length() - 1)
    ]
    others = [me + sum(flips[j] for j in range(len(flips)) if (k >> j) & 1) for k in range(1, chips)]

    def gather_start(number, arrivals, source, landing, part):
        for k in reversed(range(chips - 1)):
            remote(
                source, landing.at[(me,) + part], number, arrivals.at[part + (k,)], others[k]
            )
        remote(source, landing.at[(me,) + part], number, recv_sem.at[number], partner)

    def gather_relay(number, arrivals, landing, part, steps, handed):
        for k in steps:
            block = landing.at[(others[k],) + part]
            taken(block, arrivals.at[part + (k,)])
            remote(block, block, number, recv_sem.at[handed], partner)

    def gather_finish(handed, landing, blocks):
        taken(landing.at[pl.ds(0, blocks)], recv_sem.at[handed])

    half = count // 2
    group, first = lax.rem(me, half), lax.div(me, half) * half

    def spread(number, source, landing, size, base=0, skip=1):
        place = me if size == count else group

        @pl.loop(skip, size)
        def _(step):
            peer = base + lax.rem(place + step, size)
            remote(source(peer), landing, number, recv_sem.at[number], peer)

    loads[0].wait()
    loads[1].wait()
    pieces = []
    for i in range(rows):
        normed = layer_normalized(pair[i].astype(F32)).astype(BF16)
        pieces.append(dot(bias_w[...], normed, NT))
    slab = jnp.concatenate(pieces, 0).astype(BF16)
    bias_src[...] = slab
    bias_land[me] = slab
    pl.semaphore_wait(barrier, count - 1)
    gather_start(0, bias_sem, bias_src, bias_land, ())

    for load in loads[2:6]:
        load.wait()
    token = lax.broadcasted_iota(jnp.int32, (table.shape[0], length), 0)
    zero_rows = []
    for s in range(seqs):
        one_hot = jnp.where(ids[pl.ds(s, 1), :] == token, 1.0, 0.0).astype(BF16)
        zero_rows.append(align[s].astype(F32) + dot(one_hot, table[...], TN))
    msa_zero = jnp.concatenate(zero_rows, 0)
    projected = dot(layer_normalized(msa_zero).astype(BF16), row_w[...])
    masks = [head_mask(h, head_size, channels) for h in range(heads)]
    scale = head_size ** (-0.5)

    loads[6].wait()
    loads[7].wait()
    def by_head(block):
        return jnp.concatenate([block * m for m in masks], 0)

    def split(part):
        query = (part[:, :channels] * scale).astype(BF16)
        key = part[:, channels : 2 * channels].astype(BF16)
        value = part[:, 2 * channels : 3 * channels].astype(BF16)
        scores = dot(by_head(query), key, NT).reshape(heads, query.shape[0], key.shape[0])
        return scores, by_head(value), jax.nn.sigmoid(part[:, 3 * channels :])

    zero_v[...] = msa_zero.reshape(zero_v.shape)
    for s in range(seqs):
        raw_v[s], value_v[s], open_v[s] = split(projected[s * length : (s + 1) * length])
    for load in loads[8:]:
        load.wait()
    tri_t[...] = jnp.transpose(tri_w[:, : 4 * pair_chan].astype(F32), (1, 0)).astype(BF16)
    fill(outer_f, outer_w[...].astype(F32))
    for d in range(width):
        outer_w2[:, d * pair_chan : (d + 1) * pair_chan] = pick(
            outer_f, d, width, width
        ).astype(BF16)

    near, reach = chips // 2 - 1, half * rows
    mine = lax.div(me, half)
    turns = (
        (range(near), mine, pl.multiple_of(mine * reach, reach)),
        (range(near, chips - 1), 1 - mine, pl.multiple_of((1 - mine) * reach, reach)),
    )
    mask_bias = (mask[...].astype(F32) - 1.0) * 10000.0
    row_ones = by_head(jnp.ones((length, channels), BF16))
    lane_parts = channels // 128
    for turn, (steps, which, start) in enumerate(turns):
        gather_relay(0, bias_sem, bias_land, (), steps, 7 * turn)
        gather_finish(7 * turn, bias_land, chips // 2)
        fill(bias_f, landed(bias_land.at[pl.ds(which * half, half)]))
        extra = jnp.stack([pick(bias_f, h, reach, heads) for h in range(heads)], 0) + mask_bias
        gated = []
        for s in range(seqs):
            mixed = attend(raw_v[s, :, pl.ds(start, reach), :] + extra, value_v[s], row_ones)
            gated.append((open_v[s, pl.ds(start, reach), :] * mixed).astype(BF16))
        added = dot(jnp.concatenate(gated, 0), row_o[...])
        blocks = [
            zero_v[s, pl.ds(start, reach), :] + added[s * reach : (s + 1) * reach]
            for s in range(seqs)
        ]
        ordered = interleave(blocks, rows)
        msa_src[pl.ds(which * half, half)] = jnp.concatenate(
            [ordered[:, :, k * 128 : (k + 1) * 128] for k in range(lane_parts)], 1
        ).astype(BF16)
        if turn == 0:
            msa_land[me] = msa_src[me]
        spread(
            1,
            lambda peer: msa_src.at[peer],
            msa_land.at[me],
            half,
            first if turn == 0 else half - first,
            1 - turn,
        )

    to_output = selection(
        total * rows,
        lambda o: (
            split_index(o, rows)[1] * total
            + split_index(split_index(o, rows)[0], seqs)[1] * count
            + split_index(o, seqs * rows)[0]
        ),
    )
    taken(msa_land.at[pl.ds(0, count - 1)], recv_sem.at[1])
    fill(msa_f, landed(msa_land))
    step = lane_parts * seqs * rows
    column = jnp.concatenate(
        [
            jnp.concatenate(
                [
                    pick(msa_f, (k * seqs + s) * rows + i, count, step)
                    for i in range(rows)
                    for s in range(seqs)
                ],
                0,
            )
            for k in range(lane_parts)
        ],
        1,
    )
    pack = max(1, 128 // total)
    groups = width // pack
    lanes = pack * total
    column_ones = by_head(jnp.ones((lanes, channels), BF16))
    together = (
        split_index(lax.broadcasted_iota(jnp.int32, (1, lanes, lanes), 1), total)[0]
        == split_index(lax.broadcasted_iota(jnp.int32, (1, lanes, lanes), 2), total)[0]
    )
    two_rows, inputs = [], []
    for start in range(0, rows, pack):
        block = column[start * total : (start + pack) * total]
        projected = dot(layer_normalized(block).astype(BF16), col_w[...])
        scores, value, opened = split(projected)
        if pack > 1:
            scores = jnp.where(together, scores, -1e30)
        gated = (opened * attend(scores, value, column_ones)).astype(BF16)
        msa_two = block + dot(gated, col_o[...])
        outer_input = layer_normalized(msa_two).astype(BF16)
        two_rows.append(msa_two.astype(BF16))
        inputs.append(outer_input)

        right_t = dot(factor_w[width:, :], outer_input, NT)
        slab = jnp.concatenate(pack_lanes(right_t, pack, total), 0).astype(BF16)
        part = (start // pack,)
        right_src[part[0]] = slab
        right_land[me, part[0]] = slab
        gather_start(2, right_sem, right_src.at[part[0]], right_land, part)

    left = dot(jnp.concatenate(inputs, 0), factor_w[:width, :], NT).astype(BF16)
    chunk = 8
    for start in range(0, width, chunk):
        product = dot(left, outer_w2[:, start * pair_chan : (start + chunk) * pair_chan])
        for d in range(start, start + chunk):
            at = ((d % groups) * pack + d // groups) * total
            for i in range(rows):
                left_t[at : at + total, i * pair_chan : (i + 1) * pair_chan] = product[
                    i * total : (i + 1) * total,
                    (d - start) * pair_chan : (d - start + 1) * pair_chan,
                ].astype(BF16)

    own = pair_chan // half
    fold = max(1, 128 // reach)
    height = pair_chan // fold
    normed = []
    for turn, (steps, which, start) in enumerate(turns):
        for k in range(rows // pack):
            gather_relay(2, right_sem, right_land, (k,), steps, 2 + 4 * turn)
        gather_finish(2 + 4 * turn, right_land, chips // 2)
        fill(right_f, landed(right_land.at[pl.ds(which * half, half)]))
        for k in range(groups):
            right_m[:, k * lanes : (k + 1) * lanes] = pick(right_f, k, reach, groups).astype(BF16)
        update = dot(right_m[...], left_t[...]) * (1.0 / total)
        stacked = []
        for i in range(rows):
            one = pair[i, pl.ds(start, reach), :].astype(F32) + update[
                :, i * pair_chan : (i + 1) * pair_chan
            ]
            pair_one_v[i, pl.ds(start, reach), :] = one
            stacked.append(one)
        normed.append(layer_normalized(jnp.concatenate(stacked, 0)).astype(BF16))
        factors = dot(tri_t[...], normed[turn], NT)
        for side, target in enumerate((tri_left, tri_right)):
            low = 2 * side * pair_chan
            factor = (
                jax.nn.sigmoid(factors[low + pair_chan : low + 2 * pair_chan])
                * factors[low : low + pair_chan]
            )
            wide = fold * reach
            for base in range(rows // fold):
                packed = pack_lanes(factor[:, base * wide : (base + 1) * wide], fold, reach)
                for place in range(fold):
                    at = (base * fold + place) * height
                    fill(tri_f.at[:, pl.ds(at, height), :], packed[place])
            for g in range(half):
                target[turn, g] = pick(tri_f, g, rows * own // fold, half).astype(BF16)
        left_land[which, group] = tri_left[turn, group]
        tri_land[which, me] = tri_right[turn, group]
        spread(
            3,
            lambda peer: tri_right.at[turn, lax.rem(peer, half)],
            tri_land.at[which, me],
            count,
        )
        spread(
            4,
            lambda peer: tri_left.at[turn, lax.rem(peer, half)],
            left_land.at[which, group],
            half,
            first,
        )

    ordered = dot(to_output, jnp.concatenate(two_rows, 0))
    align_out[...] = ordered.reshape(total, rows, channels).astype(BF16)
    for turn in range(2):
        opened = jax.nn.sigmoid(dot(normed[turn], tri_w[:, 4 * pair_chan :]))
        for i in range(rows):
            gate_v[i, pl.ds(turns[turn][2], reach), :] = opened[i * reach : (i + 1) * reach]

    taken(tri_land.at[pl.ds(0, 2), pl.ds(0, count - 1)], recv_sem.at[3])
    taken(left_land.at[pl.ds(0, 2), pl.ds(0, half - 1)], recv_sem.at[4])
    fill(land_f, landed(tri_land))
    fill(left_f, landed(left_land))
    slab_rows = rows * own // fold
    block = half * rows
    lane = lax.broadcasted_iota(jnp.int32, (1, fold * reach), 1)
    folds = [
        jnp.where((lane >= k * reach) & (lane < (k + 1) * reach), 1.0, 0.0).astype(BF16)
        for k in range(fold)
    ]
    for c in range(own // fold):
        step = own // fold
        left_sides = [
            jnp.concatenate(
                [
                    pick(left_f, q * half * slab_rows + i * step + c, half, slab_rows)
                    for i in range(rows)
                ],
                0,
            ).astype(BF16)
            for q in range(2)
        ]
        right_side = jnp.concatenate(
            [pick(land_f, q * count * slab_rows + c, length, step) for q in range(2)], 1
        ).astype(BF16)
        left_side = jnp.concatenate(
            [jnp.concatenate([side * m for side in left_sides], 1) for m in folds], 0
        )
        product = dot(left_side, right_side, NT)
        for k in range(fold):
            fill(
                comb_f.at[:, pl.ds((k * step + c) * block, block), :],
                product[k * block : (k + 1) * block],
            )
    for p in range(half):
        back_src[p] = pick(comb_f, p, own * rows, half).astype(BF16)
    back_land[group] = back_src[group]
    spread(5, lambda peer: back_src.at[lax.rem(peer, half)], back_land.at[group], half, first)

    taken(back_land.at[pl.ds(0, half - 1)], recv_sem.at[5])
    for number, sent in enumerate((bias_land, msa_land, right_land)):
        taken(sent.at[pl.ds(0, count - 1)], send_sem.at[number])
    taken(tri_land.at[pl.ds(0, 2), pl.ds(0, count - 1)], send_sem.at[3])
    taken(left_land.at[pl.ds(0, 2), pl.ds(0, half - 1)], send_sem.at[4])
    taken(back_land.at[pl.ds(0, half - 1)], send_sem.at[5])


def finish_kernel(rows, align, back_land, pair_one, gate, tri_o, align_out, pair_out, back_f, pair_v, sem):
    store_align = pltpu.make_async_copy(align, align_out, sem.at[0])
    store_align.start()
    fill(back_f, landed(back_land))
    owners = back_land.shape[0]
    own = back_land.shape[1] // rows
    for i in range(rows):
        channels = [pick(back_f, c * rows + i, owners, own * rows) for c in range(own)]
        combined = layer_normalized(jnp.concatenate(channels, 0), 0).astype(BF16)
        result = pair_one[i] + gate[i] * dot(combined, tri_o[...], TN)
        pair_v[i] = result.astype(BF16)
    store_pair = pltpu.make_async_copy(pair_v, pair_out, sem.at[1])
    store_pair.start()
    store_align.wait()
    store_pair.wait()


def shards(
    homolog_symbol_ids,
    residue_attend_mask,
    alignment_state,
    pair,
    symbol_lookup_matrix,
    pair_bias_weight,
    row_projection_weight,
    horizontal_readout_matrix,
    column_projection_weight,
    vertical_readout_matrix,
    product_factor_matrices,
    outer_output_weight,
    triangle_input_weight,
    triangle_output_weight,
):
    count = lax.axis_size("res")
    seqs, length, channels = alignment_state.shape
    rows, _, pair_chan = pair.shape
    heads = pair_bias_weight.shape[1]
    width = product_factor_matrices.shape[1] // 2
    total = seqs * count
    half = count // 2
    own = pair_chan // half
    pack = max(1, 128 // total)
    groups, lanes = width // pack, pack * total
    operands = [
        homolog_symbol_ids,
        residue_attend_mask.reshape(1, length),
        alignment_state,
        pair,
        symbol_lookup_matrix,
        pair_bias_weight.T,
        row_projection_weight,
        horizontal_readout_matrix,
        column_projection_weight,
        vertical_readout_matrix,
        product_factor_matrices.T,
        outer_output_weight,
        triangle_input_weight,
    ]
    lane_parts = channels // 128
    vmem = pltpu.VMEM
    parts = rows // pack
    reach = half * rows
    fold = max(1, 128 // reach)
    tri_slab = (rows * own // fold, fold * reach)
    exchanges = [
        vmem((heads * rows, length), BF16),
        vmem((count, heads * rows, length), BF16),
        vmem((count, lane_parts * seqs * rows, 128), BF16),
        vmem((count, lane_parts * seqs * rows, 128), BF16),
        vmem((parts, groups * pack, lanes), BF16),
        vmem((count, parts, groups * pack, lanes), BF16),
        vmem((2, half) + tri_slab, BF16),
        vmem((2, half) + tri_slab, BF16),
        vmem((2, half) + tri_slab, BF16),
        vmem((2, count) + tri_slab, BF16),
        vmem((half, own * rows, length), BF16),
    ]

    def pieces(row_count, lane_count):
        return vmem((lane_count // 128, row_count, 128), F32)

    scratch = (
        [vmem(x.shape, x.dtype) for x in operands]
        + exchanges
        + [
            pieces(half * heads * rows, length),
            pieces(count * lane_parts * seqs * rows, 128),
            pieces(width * width, pair_chan),
            vmem((width, width * pair_chan), BF16),
            vmem((width * total, rows * pair_chan), BF16),
            pieces(reach * groups, lanes),
            vmem((reach, width * total), BF16),
            vmem((4 * pair_chan, pair_chan), BF16),
            pieces(rows * pair_chan // fold, fold * reach),
            pieces(2 * count * tri_slab[0], tri_slab[1]),
            pieces(2 * half * tri_slab[0], tri_slab[1]),
            pieces(half * own * rows, length),
            vmem((seqs, length, channels), F32),
            vmem((seqs, heads, length, length), F32),
            vmem((seqs, heads * length, channels), BF16),
            vmem((seqs, length, channels), F32),
            pltpu.SemaphoreType.DMA((len(operands),)),
            pltpu.SemaphoreType.DMA((6,)),
            pltpu.SemaphoreType.DMA((8,)),
            pltpu.SemaphoreType.DMA((half - 1,)),
            pltpu.SemaphoreType.DMA((parts, half - 1)),
        ]
    )
    sizes = (count, seqs, rows, length, channels, heads, width, pair_chan, total)
    anywhere = pl.BlockSpec(memory_space=pltpu.HBM)
    inside = pl.BlockSpec(memory_space=pltpu.VMEM)
    aligned, back, pair_one, gate = pl.pallas_call(
        functools.partial(block_kernel, sizes),
        out_shape=(
            jax.ShapeDtypeStruct((total, rows, channels), BF16),
            jax.ShapeDtypeStruct((half, own * rows, length), BF16),
            jax.ShapeDtypeStruct(pair.shape, F32),
            jax.ShapeDtypeStruct(pair.shape, F32),
        ),
        in_specs=[anywhere] * len(operands),
        out_specs=(inside,) * 4,
        scratch_shapes=scratch,
        compiler_params=pltpu.CompilerParams(
            collective_id=0, has_side_effects=True, vmem_limit_bytes=VMEM_BYTES
        ),
    )(*[pltpu.with_memory_space_constraint(x, pltpu.HBM) for x in operands])
    return pl.pallas_call(
        functools.partial(finish_kernel, rows),
        out_shape=(
            jax.ShapeDtypeStruct((total, rows, channels), BF16),
            jax.ShapeDtypeStruct(pair.shape, BF16),
        ),
        in_specs=[inside] * 5,
        out_specs=(anywhere, anywhere),
        scratch_shapes=[
            pieces(half * own * rows, length),
            vmem(pair.shape, BF16),
            pltpu.SemaphoreType.DMA((2,)),
        ],
        compiler_params=pltpu.CompilerParams(vmem_limit_bytes=VMEM_BYTES // 4),
    )(aligned, back, pair_one, gate, triangle_output_weight)


def solution(mesh):
    placed = (
        P(("crop", "res"), None),
        P("crop"),
        P(("crop", "res"), None, None),
        P(("crop", "res"), None, None),
        P(),
        P(),
        P(),
        P(),
        P(),
        P(),
        P(),
        P(),
        P(),
        P(),
    )
    return jax.shard_map(
        shards,
        mesh=mesh,
        in_specs=placed,
        out_specs=(P("crop", "res", None), P(("crop", "res"), None, None)),
        check_vma=False,
    )
```

```python
import functools

import jax
import jax.numpy as jnp
from jax import lax
from jax.experimental import pallas as pl
from jax.experimental.pallas import tpu as pltpu
from jax.sharding import PartitionSpec as P

EPSILON = 1e-05
MESH = pl.DeviceIdType.MESH
VMEM_BYTES = 40 * 1024 * 1024
F32 = jnp.float32
BF16 = jnp.bfloat16

NN = (((1,), (0,)), ((), ()))
NT = (((1,), (1,)), ((), ()))
TN = (((0,), (0,)), ((), ()))


def dot(a, b, dims=NN):
    return lax.dot_general(a, b, dims, preferred_element_type=F32)


def layer_normalized(rows, axis=-1):
    average = jnp.mean(rows, axis, keepdims=True)
    centred = rows - average
    spread = jnp.mean(centred * centred, axis, keepdims=True)
    return centred * lax.rsqrt(spread + EPSILON)


def split_index(index, size):
    if size & (size - 1) == 0:
        return lax.shift_right_logical(index, jnp.int32(size.bit_length() - 1)), index & (size - 1)
    return lax.div(index, size), lax.rem(index, size)


def selection(size, source):
    row = lax.broadcasted_iota(jnp.int32, (size, size), 0)
    column = lax.broadcasted_iota(jnp.int32, (size, size), 1)
    return jnp.where(column == source(row), 1.0, 0.0).astype(BF16)


def head_mask(head, head_size, channels):
    lane = lax.broadcasted_iota(jnp.int32, (1, channels), 1)
    inside = (lane >= head * head_size) & (lane < (head + 1) * head_size)
    return jnp.where(inside, 1.0, 0.0).astype(BF16)


def fill(buffer, values):
    for k in range(buffer.shape[0]):
        buffer[k] = values[:, k * 128 : (k + 1) * 128]


def pick(buffer, start, size, stride):
    return jnp.concatenate(
        [buffer[k, pl.ds(start, size, stride=stride), :] for k in range(buffer.shape[0])], 1
    )


def landed(landing):
    blocks = landing[...].astype(F32)
    return blocks.reshape(-1, blocks.shape[-1])


def pack_lanes(block, pack, size):
    if pack == 1:
        return [block]
    height, lanes = block.shape[0] // pack, pack * size
    lane = lax.broadcasted_iota(jnp.int32, (height, lanes), 1)
    packed = []
    for place in range(pack):
        joined = None
        for k in range(pack):
            piece = block[k * height : (k + 1) * height]
            shift = ((k - place) * size) % lanes
            if shift:
                piece = pltpu.roll(piece, shift, 1)
            joined = piece if joined is None else jnp.where(lane >= k * size, piece, joined)
        packed.append(joined)
    return packed


def attend(scores, values, ones):
    powers = jnp.exp(scores - jnp.max(scores, -1, keepdims=True)).astype(BF16)
    side = jnp.concatenate([powers[h] for h in range(powers.shape[0])], 1)
    return dot(side, values) / dot(side, ones)


def interleave(blocks, rows):
    owners, lanes = blocks[0].shape[0] // rows, blocks[0].shape[1]
    if len(blocks) == 2 and rows == 4:
        one, two = [b.reshape(owners // 2, 8, lanes) for b in blocks]
        low = lax.broadcasted_iota(jnp.int32, one.shape, 1) < rows
        even = jnp.where(low, one, pltpu.roll(two, rows, 1))
        odd = jnp.where(low, pltpu.roll(one, rows, 1), two)
        return jnp.stack([even, odd], 1).reshape(owners, 8, lanes)
    return jnp.stack(
        [
            jnp.concatenate([b[p * rows : (p + 1) * rows] for b in blocks], 0)
            for p in range(owners)
        ],
        0,
    )


def block_kernel(
    sizes,
    ids_h, mask_h, align_h, pair_h, table_h, bias_w_h, row_w_h, row_o_h, col_w_h, col_o_h,
    factor_w_h, outer_w_h, tri_w_h,
    align_out, back_land, pair_one_v, gate_v,
    ids, mask, align, pair, table, bias_w, row_w, row_o, col_w, col_o,
    factor_w, outer_w, tri_w,
    bias_src, bias_land, msa_src, msa_land, right_src, right_land, tri_left, left_land,
    tri_right, tri_land, back_src,
    bias_f, msa_f, outer_f, outer_w2, left_t, right_f, right_m, tri_t,
    tri_f, land_f, left_f, comb_f, zero_v, raw_v, value_v, open_v,
    in_sem, send_sem, recv_sem, bias_sem, right_sem,
):
    count, seqs, rows, length, channels, heads, width, pair_chan, total = sizes
    head_size = channels // heads
    me = lax.axis_index("res")
    barrier = pltpu.get_barrier_semaphore()

    for step in range(1, count):
        pl.semaphore_signal(
            barrier, inc=1, device_id={"res": lax.rem(me + step, count)}, device_id_type=MESH
        )

    staged = [
        (pair_h, pair), (bias_w_h, bias_w), (align_h, align), (ids_h, ids), (table_h, table),
        (row_w_h, row_w), (mask_h, mask), (row_o_h, row_o), (col_w_h, col_w), (col_o_h, col_o),
        (factor_w_h, factor_w), (outer_w_h, outer_w), (tri_w_h, tri_w),
    ]
    loads = [
        pltpu.make_async_copy(source, target, in_sem.at[k])
        for k, (source, target) in enumerate(staged)
    ]
    for load in loads:
        load.start()

    def remote(source, target, number, received_by, peer):
        pltpu.make_async_remote_copy(
            src_ref=source,
            dst_ref=target,
            send_sem=send_sem.at[number],
            recv_sem=received_by,
            device_id={"res": peer},
            device_id_type=MESH,
        ).start()

    def taken(landing, semaphore):
        pltpu.make_async_copy(landing, landing, semaphore).wait()

    chips = count // 2
    partner = me + 1 - 2 * lax.rem(me, 2)
    flips = [
        (1 - 2 * lax.rem(lax.div(me, 1 << j), 2)) * (1 << j) for j in range(count.bit_length() - 1)
    ]

    def across(k):
        return me + sum(flips[j] for j in range(len(flips)) if (k >> j) & 1)

    others = [across(2 * k) for k in range(1, chips)]

    def gather_start(number, arrivals, source, landing, part, reached=None):
        for k in reversed(range(chips - 1 if reached is None else reached)):
            remote(
                source, landing.at[(me,) + part], number, arrivals.at[part + (k,)], others[k]
            )
        remote(source, landing.at[(me,) + part], number, recv_sem.at[number], partner)

    def gather_forward(number, arrivals, landing, part):
        last = chips // 2 - 1
        block = landing.at[(others[last],) + part]
        taken(block, arrivals.at[part + (last,)])
        for k in reversed(range(last)):
            remote(block, block, number, arrivals.at[part + (k + chips // 2,)], others[k])
        remote(block, block, number, recv_sem.at[6], partner)

    def gather_relay(number, arrivals, landing, part, steps, handed):
        for k in steps:
            block = landing.at[(others[k],) + part]
            taken(block, arrivals.at[part + (k,)])
            remote(block, block, number, recv_sem.at[handed], partner)

    def gather_finish(handed, landing, blocks):
        taken(landing.at[pl.ds(0, blocks)], recv_sem.at[handed])

    half = count // 2
    group = lax.rem(me, half)

    def spread(number, source, landing, distances):
        for k in reversed(distances):
            peer = across(k)
            remote(source(peer), landing, number, recv_sem.at[number], peer)

    everyone, own_half, other_half = range(1, count), range(1, half), range(half, count)

    loads[0].wait()
    loads[1].wait()
    pieces = []
    for i in range(rows):
        normed = layer_normalized(pair[i].astype(F32)).astype(BF16)
        pieces.append(dot(bias_w[...], normed, NT))
    slab = jnp.concatenate(pieces, 0).astype(BF16)
    bias_src[...] = slab
    bias_land[me] = slab
    pl.semaphore_wait(barrier, count - 1)
    gather_start(0, bias_sem, bias_src, bias_land, ())

    for load in loads[2:6]:
        load.wait()
    token = lax.broadcasted_iota(jnp.int32, (table.shape[0], length), 0)
    zero_rows = []
    for s in range(seqs):
        one_hot = jnp.where(ids[pl.ds(s, 1), :] == token, 1.0, 0.0).astype(BF16)
        zero_rows.append(align[s].astype(F32) + dot(one_hot, table[...], TN))
    msa_zero = jnp.concatenate(zero_rows, 0)
    projected = dot(layer_normalized(msa_zero).astype(BF16), row_w[...])
    masks = [head_mask(h, head_size, channels) for h in range(heads)]
    scale = head_size ** (-0.5)

    loads[6].wait()
    loads[7].wait()
    def by_head(block):
        return jnp.concatenate([block * m for m in masks], 0)

    def split(part):
        query = (part[:, :channels] * scale).astype(BF16)
        key = part[:, channels : 2 * channels].astype(BF16)
        value = part[:, 2 * channels : 3 * channels].astype(BF16)
        scores = dot(by_head(query), key, NT).reshape(heads, query.shape[0], key.shape[0])
        return scores, by_head(value), jax.nn.sigmoid(part[:, 3 * channels :])

    zero_v[...] = msa_zero.reshape(zero_v.shape)
    for s in range(seqs):
        raw_v[s], value_v[s], open_v[s] = split(projected[s * length : (s + 1) * length])
    for load in loads[8:]:
        load.wait()
    tri_t[...] = jnp.transpose(tri_w[:, : 4 * pair_chan].astype(F32), (1, 0)).astype(BF16)
    fill(outer_f, outer_w[...].astype(F32))
    for d in range(width):
        outer_w2[:, d * pair_chan : (d + 1) * pair_chan] = pick(
            outer_f, d, width, width
        ).astype(BF16)

    near, reach = chips // 2 - 1, half * rows
    mine = lax.div(me, half)
    turns = (
        (range(near), mine, pl.multiple_of(mine * reach, reach)),
        (range(near, chips - 1), 1 - mine, pl.multiple_of((1 - mine) * reach, reach)),
    )
    mask_bias = (mask[...].astype(F32) - 1.0) * 10000.0
    row_ones = by_head(jnp.ones((length, channels), BF16))
    lane_parts = channels // 128
    for turn, (steps, which, start) in enumerate(turns):
        gather_relay(0, bias_sem, bias_land, (), steps, 7 * turn)
        gather_finish(7 * turn, bias_land, chips // 2)
        fill(bias_f, landed(bias_land.at[pl.ds(which * half, half)]))
        extra = jnp.stack([pick(bias_f, h, reach, heads) for h in range(heads)], 0) + mask_bias
        gated = []
        for s in range(seqs):
            mixed = attend(raw_v[s, :, pl.ds(start, reach), :] + extra, value_v[s], row_ones)
            gated.append((open_v[s, pl.ds(start, reach), :] * mixed).astype(BF16))
        added = dot(jnp.concatenate(gated, 0), row_o[...])
        blocks = [
            zero_v[s, pl.ds(start, reach), :] + added[s * reach : (s + 1) * reach]
            for s in range(seqs)
        ]
        ordered = interleave(blocks, rows)
        msa_src[pl.ds(which * half, half)] = jnp.concatenate(
            [ordered[:, :, k * 128 : (k + 1) * 128] for k in range(lane_parts)], 1
        ).astype(BF16)
        if turn == 0:
            msa_land[me] = msa_src[me]
        spread(
            1,
            lambda peer: msa_src.at[peer],
            msa_land.at[me],
            own_half if turn == 0 else other_half,
        )

    to_output = selection(
        total * rows,
        lambda o: (
            split_index(o, rows)[1] * total
            + split_index(split_index(o, rows)[0], seqs)[1] * count
            + split_index(o, seqs * rows)[0]
        ),
    )
    taken(msa_land.at[pl.ds(0, count - 1)], recv_sem.at[1])
    fill(msa_f, landed(msa_land))
    step = lane_parts * seqs * rows
    column = jnp.concatenate(
        [
            jnp.concatenate(
                [
                    pick(msa_f, (k * seqs + s) * rows + i, count, step)
                    for i in range(rows)
                    for s in range(seqs)
                ],
                0,
            )
            for k in range(lane_parts)
        ],
        1,
    )
    pack = max(1, 128 // total)
    groups = width // pack
    lanes = pack * total
    column_ones = by_head(jnp.ones((lanes, channels), BF16))
    together = (
        split_index(lax.broadcasted_iota(jnp.int32, (1, lanes, lanes), 1), total)[0]
        == split_index(lax.broadcasted_iota(jnp.int32, (1, lanes, lanes), 2), total)[0]
    )
    two_rows, inputs = [], []
    for start in range(0, rows, pack):
        block = column[start * total : (start + pack) * total]
        projected = dot(layer_normalized(block).astype(BF16), col_w[...])
        scores, value, opened = split(projected)
        if pack > 1:
            scores = jnp.where(together, scores, -1e30)
        gated = (opened * attend(scores, value, column_ones)).astype(BF16)
        msa_two = block + dot(gated, col_o[...])
        outer_input = layer_normalized(msa_two).astype(BF16)
        two_rows.append(msa_two.astype(BF16))
        inputs.append(outer_input)

        right_t = dot(factor_w[width:, :], outer_input, NT)
        slab = jnp.concatenate(pack_lanes(right_t, pack, total), 0).astype(BF16)
        part = (start // pack,)
        right_src[part[0]] = slab
        right_land[me, part[0]] = slab
        forwarded = part[0] < rows // pack // 2
        gather_start(
            2, right_sem, right_src.at[part[0]], right_land, part,
            chips // 2 if forwarded else None,
        )

    left = dot(jnp.concatenate(inputs, 0), factor_w[:width, :], NT).astype(BF16)
    chunk = 8
    for start in range(0, width, chunk):
        product = dot(left, outer_w2[:, start * pair_chan : (start + chunk) * pair_chan])
        for d in range(start, start + chunk):
            at = ((d % groups) * pack + d // groups) * total
            for i in range(rows):
                left_t[at : at + total, i * pair_chan : (i + 1) * pair_chan] = product[
                    i * total : (i + 1) * total,
                    (d - start) * pair_chan : (d - start + 1) * pair_chan,
                ].astype(BF16)

    own = pair_chan // half
    fold = max(1, 128 // reach)
    height = pair_chan // fold
    normed = []
    for turn, (steps, which, start) in enumerate(turns):
        for k in range(rows // pack):
            mirrored = k < rows // pack // 2
            if turn == 0 and mirrored:
                gather_forward(2, right_sem, right_land, (k,))
            left_over = [x for x in steps if not (turn == 1 and mirrored and x == near)]
            gather_relay(2, right_sem, right_land, (k,), left_over, 2 + 4 * turn)
        gather_finish(2 + 4 * turn, right_land, chips // 2)
        fill(right_f, landed(right_land.at[pl.ds(which * half, half)]))
        for k in range(groups):
            right_m[:, k * lanes : (k + 1) * lanes] = pick(right_f, k, reach, groups).astype(BF16)
        update = dot(right_m[...], left_t[...]) * (1.0 / total)
        stacked = []
        for i in range(rows):
            one = pair[i, pl.ds(start, reach), :].astype(F32) + update[
                :, i * pair_chan : (i + 1) * pair_chan
            ]
            pair_one_v[i, pl.ds(start, reach), :] = one
            stacked.append(one)
        normed.append(layer_normalized(jnp.concatenate(stacked, 0)).astype(BF16))
        factors = dot(tri_t[...], normed[turn], NT)
        for side, target in enumerate((tri_left, tri_right)):
            low = 2 * side * pair_chan
            factor = (
                jax.nn.sigmoid(factors[low + pair_chan : low + 2 * pair_chan])
                * factors[low : low + pair_chan]
            )
            wide = fold * reach
            for base in range(rows // fold):
                packed = pack_lanes(factor[:, base * wide : (base + 1) * wide], fold, reach)
                for place in range(fold):
                    at = (base * fold + place) * height
                    fill(tri_f.at[:, pl.ds(at, height), :], packed[place])
            for g in range(half):
                target[turn, g] = pick(tri_f, g, rows * own // fold, half).astype(BF16)
        left_land[which, group] = tri_left[turn, group]
        tri_land[which, me] = tri_right[turn, group]
        spread(
            3,
            lambda peer: tri_right.at[turn, lax.rem(peer, half)],
            tri_land.at[which, me],
            everyone,
        )
        spread(
            4,
            lambda peer: tri_left.at[turn, lax.rem(peer, half)],
            left_land.at[which, group],
            own_half,
        )

    ordered = dot(to_output, jnp.concatenate(two_rows, 0))
    align_out[...] = ordered.reshape(total, rows, channels).astype(BF16)
    for turn in range(2):
        opened = jax.nn.sigmoid(dot(normed[turn], tri_w[:, 4 * pair_chan :]))
        for i in range(rows):
            gate_v[i, pl.ds(turns[turn][2], reach), :] = opened[i * reach : (i + 1) * reach]

    taken(tri_land.at[pl.ds(0, 2), pl.ds(0, count - 1)], recv_sem.at[3])
    taken(left_land.at[pl.ds(0, 2), pl.ds(0, half - 1)], recv_sem.at[4])
    fill(land_f, landed(tri_land))
    fill(left_f, landed(left_land))
    slab_rows = rows * own // fold
    block = half * rows
    lane = lax.broadcasted_iota(jnp.int32, (1, fold * reach), 1)
    folds = [
        jnp.where((lane >= k * reach) & (lane < (k + 1) * reach), 1.0, 0.0).astype(BF16)
        for k in range(fold)
    ]
    for c in range(own // fold):
        step = own // fold
        left_sides = [
            jnp.concatenate(
                [
                    pick(left_f, q * half * slab_rows + i * step + c, half, slab_rows)
                    for i in range(rows)
                ],
                0,
            ).astype(BF16)
            for q in range(2)
        ]
        right_side = jnp.concatenate(
            [pick(land_f, q * count * slab_rows + c, length, step) for q in range(2)], 1
        ).astype(BF16)
        left_side = jnp.concatenate(
            [jnp.concatenate([side * m for side in left_sides], 1) for m in folds], 0
        )
        product = dot(left_side, right_side, NT)
        for k in range(fold):
            fill(
                comb_f.at[:, pl.ds((k * step + c) * block, block), :],
                product[k * block : (k + 1) * block],
            )
    for p in range(half):
        back_src[p] = pick(comb_f, p, own * rows, half).astype(BF16)
    back_land[group] = back_src[group]
    spread(5, lambda peer: back_src.at[lax.rem(peer, half)], back_land.at[group], own_half)

    taken(back_land.at[pl.ds(0, half - 1)], recv_sem.at[5])
    for number, sent in enumerate((bias_land, msa_land, right_land)):
        taken(sent.at[pl.ds(0, count - 1)], send_sem.at[number])
    taken(tri_land.at[pl.ds(0, 2), pl.ds(0, count - 1)], send_sem.at[3])
    taken(left_land.at[pl.ds(0, 2), pl.ds(0, half - 1)], send_sem.at[4])
    taken(back_land.at[pl.ds(0, half - 1)], send_sem.at[5])


def finish_kernel(rows, align, back_land, pair_one, gate, tri_o, align_out, pair_out, back_f, pair_v, sem):
    store_align = pltpu.make_async_copy(align, align_out, sem.at[0])
    store_align.start()
    fill(back_f, landed(back_land))
    owners = back_land.shape[0]
    own = back_land.shape[1] // rows
    for i in range(rows):
        channels = [pick(back_f, c * rows + i, owners, own * rows) for c in range(own)]
        combined = layer_normalized(jnp.concatenate(channels, 0), 0).astype(BF16)
        result = pair_one[i] + gate[i] * dot(combined, tri_o[...], TN)
        pair_v[i] = result.astype(BF16)
    store_pair = pltpu.make_async_copy(pair_v, pair_out, sem.at[1])
    store_pair.start()
    store_align.wait()
    store_pair.wait()


def shards(
    homolog_symbol_ids,
    residue_attend_mask,
    alignment_state,
    pair,
    symbol_lookup_matrix,
    pair_bias_weight,
    row_projection_weight,
    horizontal_readout_matrix,
    column_projection_weight,
    vertical_readout_matrix,
    product_factor_matrices,
    outer_output_weight,
    triangle_input_weight,
    triangle_output_weight,
):
    count = lax.axis_size("res")
    seqs, length, channels = alignment_state.shape
    rows, _, pair_chan = pair.shape
    heads = pair_bias_weight.shape[1]
    width = product_factor_matrices.shape[1] // 2
    total = seqs * count
    half = count // 2
    own = pair_chan // half
    pack = max(1, 128 // total)
    groups, lanes = width // pack, pack * total
    operands = [
        homolog_symbol_ids,
        residue_attend_mask.reshape(1, length),
        alignment_state,
        pair,
        symbol_lookup_matrix,
        pair_bias_weight.T,
        row_projection_weight,
        horizontal_readout_matrix,
        column_projection_weight,
        vertical_readout_matrix,
        product_factor_matrices.T,
        outer_output_weight,
        triangle_input_weight,
    ]
    lane_parts = channels // 128
    vmem = pltpu.VMEM
    parts = rows // pack
    reach = half * rows
    fold = max(1, 128 // reach)
    tri_slab = (rows * own // fold, fold * reach)
    exchanges = [
        vmem((heads * rows, length), BF16),
        vmem((count, heads * rows, length), BF16),
        vmem((count, lane_parts * seqs * rows, 128), BF16),
        vmem((count, lane_parts * seqs * rows, 128), BF16),
        vmem((parts, groups * pack, lanes), BF16),
        vmem((count, parts, groups * pack, lanes), BF16),
        vmem((2, half) + tri_slab, BF16),
        vmem((2, half) + tri_slab, BF16),
        vmem((2, half) + tri_slab, BF16),
        vmem((2, count) + tri_slab, BF16),
        vmem((half, own * rows, length), BF16),
    ]

    def pieces(row_count, lane_count):
        return vmem((lane_count // 128, row_count, 128), F32)

    scratch = (
        [vmem(x.shape, x.dtype) for x in operands]
        + exchanges
        + [
            pieces(half * heads * rows, length),
            pieces(count * lane_parts * seqs * rows, 128),
            pieces(width * width, pair_chan),
            vmem((width, width * pair_chan), BF16),
            vmem((width * total, rows * pair_chan), BF16),
            pieces(reach * groups, lanes),
            vmem((reach, width * total), BF16),
            vmem((4 * pair_chan, pair_chan), BF16),
            pieces(rows * pair_chan // fold, fold * reach),
            pieces(2 * count * tri_slab[0], tri_slab[1]),
            pieces(2 * half * tri_slab[0], tri_slab[1]),
            pieces(half * own * rows, length),
            vmem((seqs, length, channels), F32),
            vmem((seqs, heads, length, length), F32),
            vmem((seqs, heads * length, channels), BF16),
            vmem((seqs, length, channels), F32),
            pltpu.SemaphoreType.DMA((len(operands),)),
            pltpu.SemaphoreType.DMA((6,)),
            pltpu.SemaphoreType.DMA((8,)),
            pltpu.SemaphoreType.DMA((half - 1,)),
            pltpu.SemaphoreType.DMA((parts, half - 1)),
        ]
    )
    sizes = (count, seqs, rows, length, channels, heads, width, pair_chan, total)
    anywhere = pl.BlockSpec(memory_space=pltpu.HBM)
    inside = pl.BlockSpec(memory_space=pltpu.VMEM)
    aligned, back, pair_one, gate = pl.pallas_call(
        functools.partial(block_kernel, sizes),
        out_shape=(
            jax.ShapeDtypeStruct((total, rows, channels), BF16),
            jax.ShapeDtypeStruct((half, own * rows, length), BF16),
            jax.ShapeDtypeStruct(pair.shape, F32),
            jax.ShapeDtypeStruct(pair.shape, F32),
        ),
        in_specs=[anywhere] * len(operands),
        out_specs=(inside,) * 4,
        scratch_shapes=scratch,
        compiler_params=pltpu.CompilerParams(
            collective_id=0, has_side_effects=True, vmem_limit_bytes=VMEM_BYTES
        ),
    )(*[pltpu.with_memory_space_constraint(x, pltpu.HBM) for x in operands])
    return pl.pallas_call(
        functools.partial(finish_kernel, rows),
        out_shape=(
            jax.ShapeDtypeStruct((total, rows, channels), BF16),
            jax.ShapeDtypeStruct(pair.shape, BF16),
        ),
        in_specs=[inside] * 5,
        out_specs=(anywhere, anywhere),
        scratch_shapes=[
            pieces(half * own * rows, length),
            vmem(pair.shape, BF16),
            pltpu.SemaphoreType.DMA((2,)),
        ],
        compiler_params=pltpu.CompilerParams(vmem_limit_bytes=VMEM_BYTES // 4),
    )(aligned, back, pair_one, gate, triangle_output_weight)


def solution(mesh):
    placed = (
        P(("crop", "res"), None),
        P("crop"),
        P(("crop", "res"), None, None),
        P(("crop", "res"), None, None),
        P(),
        P(),
        P(),
        P(),
        P(),
        P(),
        P(),
        P(),
        P(),
        P(),
    )
    return jax.shard_map(
        shards,
        mesh=mesh,
        in_specs=placed,
        out_specs=(P("crop", "res", None), P(("crop", "res"), None, None)),
        check_vma=False,
    )
```

```python
import functools

import jax
import jax.numpy as jnp
from jax import lax
from jax.experimental import pallas as pl
from jax.experimental.pallas import tpu as pltpu
from jax.sharding import PartitionSpec as P

EPSILON = 1e-05
MESH = pl.DeviceIdType.MESH
VMEM_BYTES = 40 * 1024 * 1024
F32 = jnp.float32
BF16 = jnp.bfloat16

NN = (((1,), (0,)), ((), ()))
NT = (((1,), (1,)), ((), ()))
TN = (((0,), (0,)), ((), ()))


def dot(a, b, dims=NN):
    return lax.dot_general(a, b, dims, preferred_element_type=F32)


def layer_normalized(rows, axis=-1):
    average = jnp.mean(rows, axis, keepdims=True)
    centred = rows - average
    spread = jnp.mean(centred * centred, axis, keepdims=True)
    return centred * lax.rsqrt(spread + EPSILON)


def split_index(index, size):
    if size & (size - 1) == 0:
        return lax.shift_right_logical(index, jnp.int32(size.bit_length() - 1)), index & (size - 1)
    return lax.div(index, size), lax.rem(index, size)


def selection(size, source):
    row = lax.broadcasted_iota(jnp.int32, (size, size), 0)
    column = lax.broadcasted_iota(jnp.int32, (size, size), 1)
    return jnp.where(column == source(row), 1.0, 0.0).astype(BF16)


def head_mask(head, head_size, channels):
    lane = lax.broadcasted_iota(jnp.int32, (1, channels), 1)
    inside = (lane >= head * head_size) & (lane < (head + 1) * head_size)
    return jnp.where(inside, 1.0, 0.0).astype(BF16)


def fill(buffer, values):
    for k in range(buffer.shape[0]):
        buffer[k] = values[:, k * 128 : (k + 1) * 128]


def pick(buffer, start, size, stride):
    return jnp.concatenate(
        [buffer[k, pl.ds(start, size, stride=stride), :] for k in range(buffer.shape[0])], 1
    )


def landed(landing):
    blocks = landing[...].astype(F32)
    return blocks.reshape(-1, blocks.shape[-1])


def pack_lanes(block, pack, size):
    if pack == 1:
        return [block]
    height, lanes = block.shape[0] // pack, pack * size
    lane = lax.broadcasted_iota(jnp.int32, (height, lanes), 1)
    packed = []
    for place in range(pack):
        joined = None
        for k in range(pack):
            piece = block[k * height : (k + 1) * height]
            shift = ((k - place) * size) % lanes
            if shift:
                piece = pltpu.roll(piece, shift, 1)
            joined = piece if joined is None else jnp.where(lane >= k * size, piece, joined)
        packed.append(joined)
    return packed


def attend(scores, values, ones):
    powers = jnp.exp(scores - jnp.max(scores, -1, keepdims=True)).astype(BF16)
    side = jnp.concatenate([powers[h] for h in range(powers.shape[0])], 1)
    return dot(side, values) / dot(side, ones)


def interleave(blocks, rows):
    owners, lanes = blocks[0].shape[0] // rows, blocks[0].shape[1]
    if len(blocks) == 2 and rows == 4:
        one, two = [b.reshape(owners // 2, 8, lanes) for b in blocks]
        low = lax.broadcasted_iota(jnp.int32, one.shape, 1) < rows
        even = jnp.where(low, one, pltpu.roll(two, rows, 1))
        odd = jnp.where(low, pltpu.roll(one, rows, 1), two)
        return jnp.stack([even, odd], 1).reshape(owners, 8, lanes)
    return jnp.stack(
        [
            jnp.concatenate([b[p * rows : (p + 1) * rows] for b in blocks], 0)
            for p in range(owners)
        ],
        0,
    )


def block_kernel(
    sizes,
    ids_h, mask_h, align_h, pair_h, table_h, bias_w_h, row_w_h, row_o_h, col_w_h, col_o_h,
    factor_w_h, outer_w_h, tri_w_h,
    align_out, back_land, pair_one_v, gate_v,
    ids, mask, align, pair, table, bias_w, row_w, row_o, col_w, col_o,
    factor_w, outer_w, tri_w,
    bias_src, bias_land, msa_src, msa_land, right_src, right_land, tri_left, left_land,
    tri_right, tri_land, back_src,
    bias_f, msa_f, outer_f, outer_w2, left_t, right_f, right_m, tri_t,
    tri_f, land_f, left_f, comb_f, zero_v, raw_v, value_v, open_v,
    in_sem, send_sem, recv_sem, bias_sem, right_sem,
):
    count, seqs, rows, length, channels, heads, width, pair_chan, total = sizes
    head_size = channels // heads
    me = lax.axis_index("res")
    half = count // 2
    flips = [
        (1 - 2 * lax.rem(lax.div(me, 1 << j), 2)) * (1 << j) for j in range(count.bit_length() - 1)
    ]

    def across(k):
        return me + sum(flips[j] for j in range(len(flips)) if (k >> j) & 1)

    mirror = across(half)
    barrier = pltpu.get_barrier_semaphore()
    for k in reversed(range(1, half + 1)):
        pl.semaphore_signal(barrier, inc=1, device_id={"res": across(k)}, device_id_type=MESH)

    staged = [
        (pair_h, pair), (bias_w_h, bias_w), (align_h, align), (ids_h, ids), (table_h, table),
        (row_w_h, row_w), (mask_h, mask), (row_o_h, row_o), (col_w_h, col_w), (col_o_h, col_o),
        (factor_w_h, factor_w), (outer_w_h, outer_w), (tri_w_h, tri_w),
    ]
    loads = [
        pltpu.make_async_copy(source, target, in_sem.at[k])
        for k, (source, target) in enumerate(staged)
    ]
    for load in loads:
        load.start()

    def remote(source, target, number, received_by, peer):
        pltpu.make_async_remote_copy(
            src_ref=source,
            dst_ref=target,
            send_sem=send_sem.at[number],
            recv_sem=received_by,
            device_id={"res": peer},
            device_id_type=MESH,
        ).start()

    def taken(landing, semaphore):
        pltpu.make_async_copy(landing, landing, semaphore).wait()

    def gather_start(number, mirrored, source, landing, part=()):
        remote(source, landing.at[(me,) + part], number, mirrored, mirror)
        for k in reversed(range(1, half)):
            remote(source, landing.at[(me,) + part], number, recv_sem.at[number], across(k))

    def gather_forward(number, mirrored, landing, handed, part=()):
        block = landing.at[(mirror,) + part]
        taken(block, mirrored)
        for k in reversed(range(1, half)):
            remote(block, block, number, recv_sem.at[handed], across(k))

    group = lax.rem(me, half)

    def spread(number, source, landing, distances):
        for k in reversed(distances):
            peer = across(k)
            remote(source(peer), landing, number, recv_sem.at[number], peer)

    everyone, own_half, other_half = range(1, count), range(1, half), range(half, count)

    loads[0].wait()
    loads[1].wait()
    pieces = []
    for i in range(rows):
        normed = layer_normalized(pair[i].astype(F32)).astype(BF16)
        pieces.append(dot(bias_w[...], normed, NT))
    slab = jnp.concatenate(pieces, 0).astype(BF16)
    bias_src[...] = slab
    bias_land[me] = slab

    for load in loads[2:6]:
        load.wait()
    token = lax.broadcasted_iota(jnp.int32, (table.shape[0], length), 0)
    zero_rows = []
    for s in range(seqs):
        one_hot = jnp.where(ids[pl.ds(s, 1), :] == token, 1.0, 0.0).astype(BF16)
        zero_rows.append(align[s].astype(F32) + dot(one_hot, table[...], TN))
    msa_zero = jnp.concatenate(zero_rows, 0)
    projected = dot(layer_normalized(msa_zero).astype(BF16), row_w[...])
    masks = [head_mask(h, head_size, channels) for h in range(heads)]
    scale = head_size ** (-0.5)

    loads[6].wait()
    loads[7].wait()
    def by_head(block):
        return jnp.concatenate([block * m for m in masks], 0)

    def split(part):
        query = (part[:, :channels] * scale).astype(BF16)
        key = part[:, channels : 2 * channels].astype(BF16)
        value = part[:, 2 * channels : 3 * channels].astype(BF16)
        scores = dot(by_head(query), key, NT).reshape(heads, query.shape[0], key.shape[0])
        return scores, by_head(value), jax.nn.sigmoid(part[:, 3 * channels :])

    zero_v[...] = msa_zero.reshape(zero_v.shape)
    for s in range(seqs):
        raw_v[s], value_v[s], open_v[s] = split(projected[s * length : (s + 1) * length])
    pl.semaphore_wait(barrier, half)
    gather_start(0, bias_sem.at[0], bias_src, bias_land)

    for load in loads[8:]:
        load.wait()
    tri_t[...] = jnp.transpose(tri_w[:, : 4 * pair_chan].astype(F32), (1, 0)).astype(BF16)
    fill(outer_f, outer_w[...].astype(F32))
    for d in range(width):
        outer_w2[:, d * pair_chan : (d + 1) * pair_chan] = pick(
            outer_f, d, width, width
        ).astype(BF16)

    reach = half * rows
    mine = lax.div(me, half)
    turns = (
        (mine, pl.multiple_of(mine * reach, reach)),
        (1 - mine, pl.multiple_of((1 - mine) * reach, reach)),
    )
    mask_bias = (mask[...].astype(F32) - 1.0) * 10000.0
    row_ones = by_head(jnp.ones((length, channels), BF16))
    lane_parts = channels // 128
    for turn, (which, start) in enumerate(turns):
        if turn == 0:
            gather_forward(0, bias_sem.at[0], bias_land, 7)
        taken(bias_land.at[pl.ds(0, half - 1)], recv_sem.at[7 * turn])
        fill(bias_f, landed(bias_land.at[pl.ds(which * half, half)]))
        extra = jnp.stack([pick(bias_f, h, reach, heads) for h in range(heads)], 0) + mask_bias
        gated = []
        for s in range(seqs):
            mixed = attend(raw_v[s, :, pl.ds(start, reach), :] + extra, value_v[s], row_ones)
            gated.append((open_v[s, pl.ds(start, reach), :] * mixed).astype(BF16))
        added = dot(jnp.concatenate(gated, 0), row_o[...])
        blocks = [
            zero_v[s, pl.ds(start, reach), :] + added[s * reach : (s + 1) * reach]
            for s in range(seqs)
        ]
        ordered = interleave(blocks, rows)
        msa_src[pl.ds(which * half, half)] = jnp.concatenate(
            [ordered[:, :, k * 128 : (k + 1) * 128] for k in range(lane_parts)], 1
        ).astype(BF16)
        if turn == 0:
            msa_land[me] = msa_src[me]
        spread(
            1,
            lambda peer: msa_src.at[peer],
            msa_land.at[me],
            own_half if turn == 0 else other_half,
        )

    to_output = selection(
        total * rows,
        lambda o: (
            split_index(o, rows)[1] * total
            + split_index(split_index(o, rows)[0], seqs)[1] * count
            + split_index(o, seqs * rows)[0]
        ),
    )
    taken(msa_land.at[pl.ds(0, count - 1)], recv_sem.at[1])
    fill(msa_f, landed(msa_land))
    step = lane_parts * seqs * rows
    column = jnp.concatenate(
        [
            jnp.concatenate(
                [
                    pick(msa_f, (k * seqs + s) * rows + i, count, step)
                    for i in range(rows)
                    for s in range(seqs)
                ],
                0,
            )
            for k in range(lane_parts)
        ],
        1,
    )
    pack = max(1, 128 // total)
    groups = width // pack
    lanes = pack * total
    column_ones = by_head(jnp.ones((lanes, channels), BF16))
    together = (
        split_index(lax.broadcasted_iota(jnp.int32, (1, lanes, lanes), 1), total)[0]
        == split_index(lax.broadcasted_iota(jnp.int32, (1, lanes, lanes), 2), total)[0]
    )
    two_rows, inputs = [], []
    for start in range(0, rows, pack):
        block = column[start * total : (start + pack) * total]
        projected = dot(layer_normalized(block).astype(BF16), col_w[...])
        scores, value, opened = split(projected)
        if pack > 1:
            scores = jnp.where(together, scores, -1e30)
        gated = (opened * attend(scores, value, column_ones)).astype(BF16)
        msa_two = block + dot(gated, col_o[...])
        outer_input = layer_normalized(msa_two).astype(BF16)
        two_rows.append(msa_two.astype(BF16))
        inputs.append(outer_input)

        right_t = dot(factor_w[width:, :], outer_input, NT)
        slab = jnp.concatenate(pack_lanes(right_t, pack, total), 0).astype(BF16)
        part = (start // pack,)
        right_src[part[0]] = slab
        right_land[me, part[0]] = slab
        gather_start(2, right_sem.at[part[0]], right_src.at[part[0]], right_land, part)

    left = dot(jnp.concatenate(inputs, 0), factor_w[:width, :], NT).astype(BF16)
    chunk = 8
    for start in range(0, width, chunk):
        product = dot(left, outer_w2[:, start * pair_chan : (start + chunk) * pair_chan])
        for d in range(start, start + chunk):
            at = ((d % groups) * pack + d // groups) * total
            for i in range(rows):
                left_t[at : at + total, i * pair_chan : (i + 1) * pair_chan] = product[
                    i * total : (i + 1) * total,
                    (d - start) * pair_chan : (d - start + 1) * pair_chan,
                ].astype(BF16)

    own = pair_chan // half
    fold = max(1, 128 // reach)
    height = pair_chan // fold
    normed = []
    for k in range(rows // pack):
        gather_forward(2, right_sem.at[k], right_land, 6, (k,))
    for turn, (which, start) in enumerate(turns):
        taken(right_land.at[pl.ds(0, half - 1)], recv_sem.at[2 + 4 * turn])
        fill(right_f, landed(right_land.at[pl.ds(which * half, half)]))
        for k in range(groups):
            right_m[:, k * lanes : (k + 1) * lanes] = pick(right_f, k, reach, groups).astype(BF16)
        update = dot(right_m[...], left_t[...]) * (1.0 / total)
        stacked = []
        for i in range(rows):
            one = pair[i, pl.ds(start, reach), :].astype(F32) + update[
                :, i * pair_chan : (i + 1) * pair_chan
            ]
            pair_one_v[i, pl.ds(start, reach), :] = one
            stacked.append(one)
        normed.append(layer_normalized(jnp.concatenate(stacked, 0)).astype(BF16))
        for side, target in ((1, tri_right), (0, tri_left)):
            low = 2 * side * pair_chan
            factors = dot(tri_t[low : low + 2 * pair_chan, :], normed[turn], NT)
            factor = jax.nn.sigmoid(factors[pair_chan:]) * factors[:pair_chan]
            wide = fold * reach
            for base in range(rows // fold):
                packed = pack_lanes(factor[:, base * wide : (base + 1) * wide], fold, reach)
                for place in range(fold):
                    at = (base * fold + place) * height
                    fill(tri_f.at[side, :, pl.ds(at, height), :], packed[place])
            for g in range(half):
                target[turn, g] = pick(
                    tri_f.at[side], g, rows * own // fold, half
                ).astype(BF16)
            if side == 1:
                spread(
                    3,
                    lambda peer: tri_right.at[turn, lax.rem(peer, half)],
                    tri_land.at[which, me],
                    everyone,
                )
            else:
                spread(
                    4,
                    lambda peer: tri_left.at[turn, lax.rem(peer, half)],
                    left_land.at[which, group],
                    own_half,
                )
        left_land[which, group] = tri_left[turn, group]
        tri_land[which, me] = tri_right[turn, group]

    ordered = dot(to_output, jnp.concatenate(two_rows, 0))
    align_out[...] = ordered.reshape(total, rows, channels).astype(BF16)
    for turn in range(2):
        opened = jax.nn.sigmoid(dot(normed[turn], tri_w[:, 4 * pair_chan :]))
        for i in range(rows):
            gate_v[i, pl.ds(turns[turn][1], reach), :] = opened[i * reach : (i + 1) * reach]

    taken(tri_land.at[pl.ds(0, 2), pl.ds(0, count - 1)], recv_sem.at[3])
    taken(left_land.at[pl.ds(0, 2), pl.ds(0, half - 1)], recv_sem.at[4])
    fill(land_f, landed(tri_land))
    fill(left_f, landed(left_land))
    slab_rows = rows * own // fold
    block = half * rows
    lane = lax.broadcasted_iota(jnp.int32, (1, fold * reach), 1)
    folds = [
        jnp.where((lane >= k * reach) & (lane < (k + 1) * reach), 1.0, 0.0).astype(BF16)
        for k in range(fold)
    ]
    for c in range(own // fold):
        step = own // fold
        left_sides = [
            jnp.concatenate(
                [
                    pick(left_f, q * half * slab_rows + i * step + c, half, slab_rows)
                    for i in range(rows)
                ],
                0,
            ).astype(BF16)
            for q in range(2)
        ]
        right_side = jnp.concatenate(
            [pick(land_f, q * count * slab_rows + c, length, step) for q in range(2)], 1
        ).astype(BF16)
        left_side = jnp.concatenate(
            [jnp.concatenate([side * m for side in left_sides], 1) for m in folds], 0
        )
        product = dot(left_side, right_side, NT)
        for k in range(fold):
            fill(
                comb_f.at[:, pl.ds((k * step + c) * block, block), :],
                product[k * block : (k + 1) * block],
            )
    for p in range(half):
        back_src[p] = pick(comb_f, p, own * rows, half).astype(BF16)
    back_land[group] = back_src[group]
    spread(5, lambda peer: back_src.at[lax.rem(peer, half)], back_land.at[group], own_half)

    taken(back_land.at[pl.ds(0, half - 1)], recv_sem.at[5])
    for number, sent in enumerate((bias_land, msa_land, right_land)):
        taken(sent.at[pl.ds(0, count - 1)], send_sem.at[number])
    taken(tri_land.at[pl.ds(0, 2), pl.ds(0, count - 1)], send_sem.at[3])
    taken(left_land.at[pl.ds(0, 2), pl.ds(0, half - 1)], send_sem.at[4])
    taken(back_land.at[pl.ds(0, half - 1)], send_sem.at[5])


def finish_kernel(rows, align, back_land, pair_one, gate, tri_o, align_out, pair_out, back_f, pair_v, sem):
    store_align = pltpu.make_async_copy(align, align_out, sem.at[0])
    store_align.start()
    fill(back_f, landed(back_land))
    owners = back_land.shape[0]
    own = back_land.shape[1] // rows
    stores = []
    for i in range(rows):
        channels = [pick(back_f, c * rows + i, owners, own * rows) for c in range(own)]
        combined = layer_normalized(jnp.concatenate(channels, 0), 0).astype(BF16)
        result = pair_one[i] + gate[i] * dot(combined, tri_o[...], TN)
        pair_v[i] = result.astype(BF16)
        stores.append(pltpu.make_async_copy(pair_v.at[i], pair_out.at[i], sem.at[1 + i]))
        stores[i].start()
    store_align.wait()
    for store in stores:
        store.wait()


def shards(
    homolog_symbol_ids,
    residue_attend_mask,
    alignment_state,
    pair,
    symbol_lookup_matrix,
    pair_bias_weight,
    row_projection_weight,
    horizontal_readout_matrix,
    column_projection_weight,
    vertical_readout_matrix,
    product_factor_matrices,
    outer_output_weight,
    triangle_input_weight,
    triangle_output_weight,
):
    count = lax.axis_size("res")
    seqs, length, channels = alignment_state.shape
    rows, _, pair_chan = pair.shape
    heads = pair_bias_weight.shape[1]
    width = product_factor_matrices.shape[1] // 2
    total = seqs * count
    half = count // 2
    own = pair_chan // half
    pack = max(1, 128 // total)
    groups, lanes = width // pack, pack * total
    operands = [
        homolog_symbol_ids,
        residue_attend_mask.reshape(1, length),
        alignment_state,
        pair,
        symbol_lookup_matrix,
        pair_bias_weight.T,
        row_projection_weight,
        horizontal_readout_matrix,
        column_projection_weight,
        vertical_readout_matrix,
        product_factor_matrices.T,
        outer_output_weight,
        triangle_input_weight,
    ]
    lane_parts = channels // 128
    vmem = pltpu.VMEM
    parts = rows // pack
    reach = half * rows
    fold = max(1, 128 // reach)
    tri_slab = (rows * own // fold, fold * reach)
    exchanges = [
        vmem((heads * rows, length), BF16),
        vmem((count, heads * rows, length), BF16),
        vmem((count, lane_parts * seqs * rows, 128), BF16),
        vmem((count, lane_parts * seqs * rows, 128), BF16),
        vmem((parts, groups * pack, lanes), BF16),
        vmem((count, parts, groups * pack, lanes), BF16),
        vmem((2, half) + tri_slab, BF16),
        vmem((2, half) + tri_slab, BF16),
        vmem((2, half) + tri_slab, BF16),
        vmem((2, count) + tri_slab, BF16),
        vmem((half, own * rows, length), BF16),
    ]

    def pieces(row_count, lane_count):
        return vmem((lane_count // 128, row_count, 128), F32)

    scratch = (
        [vmem(x.shape, x.dtype) for x in operands]
        + exchanges
        + [
            pieces(half * heads * rows, length),
            pieces(count * lane_parts * seqs * rows, 128),
            pieces(width * width, pair_chan),
            vmem((width, width * pair_chan), BF16),
            vmem((width * total, rows * pair_chan), BF16),
            pieces(reach * groups, lanes),
            vmem((reach, width * total), BF16),
            vmem((4 * pair_chan, pair_chan), BF16),
            vmem((2, fold * reach // 128, rows * pair_chan // fold, 128), F32),
            pieces(2 * count * tri_slab[0], tri_slab[1]),
            pieces(2 * half * tri_slab[0], tri_slab[1]),
            pieces(half * own * rows, length),
            vmem((seqs, length, channels), F32),
            vmem((seqs, heads, length, length), F32),
            vmem((seqs, heads * length, channels), BF16),
            vmem((seqs, length, channels), F32),
            pltpu.SemaphoreType.DMA((len(operands),)),
            pltpu.SemaphoreType.DMA((6,)),
            pltpu.SemaphoreType.DMA((8,)),
            pltpu.SemaphoreType.DMA((1,)),
            pltpu.SemaphoreType.DMA((parts,)),
        ]
    )
    sizes = (count, seqs, rows, length, channels, heads, width, pair_chan, total)
    anywhere = pl.BlockSpec(memory_space=pltpu.HBM)
    inside = pl.BlockSpec(memory_space=pltpu.VMEM)
    aligned, back, pair_one, gate = pl.pallas_call(
        functools.partial(block_kernel, sizes),
        out_shape=(
            jax.ShapeDtypeStruct((total, rows, channels), BF16),
            jax.ShapeDtypeStruct((half, own * rows, length), BF16),
            jax.ShapeDtypeStruct(pair.shape, F32),
            jax.ShapeDtypeStruct(pair.shape, F32),
        ),
        in_specs=[anywhere] * len(operands),
        out_specs=(inside,) * 4,
        scratch_shapes=scratch,
        compiler_params=pltpu.CompilerParams(
            collective_id=0, has_side_effects=True, vmem_limit_bytes=VMEM_BYTES
        ),
    )(*[pltpu.with_memory_space_constraint(x, pltpu.HBM) for x in operands])
    return pl.pallas_call(
        functools.partial(finish_kernel, rows),
        out_shape=(
            jax.ShapeDtypeStruct((total, rows, channels), BF16),
            jax.ShapeDtypeStruct(pair.shape, BF16),
        ),
        in_specs=[inside] * 5,
        out_specs=(anywhere, anywhere),
        scratch_shapes=[
            pieces(half * own * rows, length),
            vmem(pair.shape, BF16),
            pltpu.SemaphoreType.DMA((1 + rows,)),
        ],
        compiler_params=pltpu.CompilerParams(vmem_limit_bytes=VMEM_BYTES // 4),
    )(aligned, back, pair_one, gate, triangle_output_weight)


def solution(mesh):
    placed = (
        P(("crop", "res"), None),
        P("crop"),
        P(("crop", "res"), None, None),
        P(("crop", "res"), None, None),
        P(),
        P(),
        P(),
        P(),
        P(),
        P(),
        P(),
        P(),
        P(),
        P(),
    )
    return jax.shard_map(
        shards,
        mesh=mesh,
        in_specs=placed,
        out_specs=(P("crop", "res", None), P(("crop", "res"), None, None)),
        check_vma=False,
    )
```

```python
import functools

import jax
import jax.numpy as jnp
from jax import lax
from jax.experimental import pallas as pl
from jax.experimental.pallas import tpu as pltpu
from jax.sharding import PartitionSpec as P

EPSILON = 1e-05
MESH = pl.DeviceIdType.MESH
VMEM_BYTES = 40 * 1024 * 1024
F32 = jnp.float32
BF16 = jnp.bfloat16

NN = (((1,), (0,)), ((), ()))
NT = (((1,), (1,)), ((), ()))
TN = (((0,), (0,)), ((), ()))


def dot(a, b, dims=NN):
    return lax.dot_general(a, b, dims, preferred_element_type=F32)


def layer_normalized(rows, axis=-1):
    average = jnp.mean(rows, axis, keepdims=True)
    centred = rows - average
    spread = jnp.mean(centred * centred, axis, keepdims=True)
    return centred * lax.rsqrt(spread + EPSILON)


def split_index(index, size):
    if size & (size - 1) == 0:
        return lax.shift_right_logical(index, jnp.int32(size.bit_length() - 1)), index & (size - 1)
    return lax.div(index, size), lax.rem(index, size)


def selection(size, source):
    row = lax.broadcasted_iota(jnp.int32, (size, size), 0)
    column = lax.broadcasted_iota(jnp.int32, (size, size), 1)
    return jnp.where(column == source(row), 1.0, 0.0).astype(BF16)


def head_mask(head, head_size, channels):
    lane = lax.broadcasted_iota(jnp.int32, (1, channels), 1)
    inside = (lane >= head * head_size) & (lane < (head + 1) * head_size)
    return jnp.where(inside, 1.0, 0.0).astype(BF16)


def fill(buffer, values):
    for k in range(buffer.shape[0]):
        buffer[k] = values[:, k * 128 : (k + 1) * 128]


def pick(buffer, start, size, stride):
    return jnp.concatenate(
        [buffer[k, pl.ds(start, size, stride=stride), :] for k in range(buffer.shape[0])], 1
    )


def landed(landing):
    blocks = landing[...].astype(F32)
    return blocks.reshape(-1, blocks.shape[-1])


def pack_lanes(block, pack, size):
    if pack == 1:
        return [block]
    height, lanes = block.shape[0] // pack, pack * size
    lane = lax.broadcasted_iota(jnp.int32, (height, lanes), 1)
    packed = []
    for place in range(pack):
        joined = None
        for k in range(pack):
            piece = block[k * height : (k + 1) * height]
            shift = ((k - place) * size) % lanes
            if shift:
                piece = pltpu.roll(piece, shift, 1)
            joined = piece if joined is None else jnp.where(lane >= k * size, piece, joined)
        packed.append(joined)
    return packed


def attend(scores, values, ones):
    powers = jnp.exp(scores - jnp.max(scores, -1, keepdims=True)).astype(BF16)
    side = jnp.concatenate([powers[h] for h in range(powers.shape[0])], 1)
    return dot(side, values) / dot(side, ones)


def interleave(blocks, rows):
    owners, lanes = blocks[0].shape[0] // rows, blocks[0].shape[1]
    if len(blocks) == 2 and rows == 4:
        one, two = [b.reshape(owners // 2, 8, lanes) for b in blocks]
        low = lax.broadcasted_iota(jnp.int32, one.shape, 1) < rows
        even = jnp.where(low, one, pltpu.roll(two, rows, 1))
        odd = jnp.where(low, pltpu.roll(one, rows, 1), two)
        return jnp.stack([even, odd], 1).reshape(owners, 8, lanes)
    return jnp.stack(
        [
            jnp.concatenate([b[p * rows : (p + 1) * rows] for b in blocks], 0)
            for p in range(owners)
        ],
        0,
    )


def block_kernel(
    sizes,
    ids_h, mask_h, align_h, pair_h, table_h, bias_w_h, row_w_h, row_o_h, col_w_h, col_o_h,
    factor_w_h, outer_w_h, tri_w_h,
    align_out, back_land, pair_one_v, gate_v,
    ids, mask, align, pair, table, bias_w, row_w, row_o, col_w, col_o,
    factor_w, outer_w, tri_w,
    bias_src, bias_land, msa_src, msa_land, right_src, right_land, tri_left, left_land,
    tri_right, tri_land, back_src,
    bias_f, msa_f, outer_f, outer_w2, left_t, right_f, right_m, tri_t,
    tri_f, land_f, left_f, comb_f, zero_v, raw_v, value_v, open_v, column_v, project_v,
    in_sem, send_sem, recv_sem, bias_sem, right_sem,
):
    count, seqs, rows, length, channels, heads, width, pair_chan, total = sizes
    head_size = channels // heads
    me = lax.axis_index("res")
    half = count // 2
    flips = [
        (1 - 2 * lax.rem(lax.div(me, 1 << j), 2)) * (1 << j) for j in range(count.bit_length() - 1)
    ]

    def across(k):
        return me + sum(flips[j] for j in range(len(flips)) if (k >> j) & 1)

    mirror = across(half)
    barrier = pltpu.get_barrier_semaphore()
    for k in reversed(range(1, half + 1)):
        pl.semaphore_signal(barrier, inc=1, device_id={"res": across(k)}, device_id_type=MESH)

    staged = [
        (pair_h, pair), (bias_w_h, bias_w), (align_h, align), (ids_h, ids), (table_h, table),
        (row_w_h, row_w), (mask_h, mask), (row_o_h, row_o), (col_w_h, col_w), (col_o_h, col_o),
        (factor_w_h, factor_w), (outer_w_h, outer_w), (tri_w_h, tri_w),
    ]
    loads = [
        pltpu.make_async_copy(source, target, in_sem.at[k])
        for k, (source, target) in enumerate(staged)
    ]
    for load in loads:
        load.start()

    def remote(source, target, number, received_by, peer):
        pltpu.make_async_remote_copy(
            src_ref=source,
            dst_ref=target,
            send_sem=send_sem.at[number],
            recv_sem=received_by,
            device_id={"res": peer},
            device_id_type=MESH,
        ).start()

    def taken(landing, semaphore):
        pltpu.make_async_copy(landing, landing, semaphore).wait()

    def gather_start(number, mirrored, source, landing, part=()):
        remote(source, landing.at[(me,) + part], number, mirrored, mirror)
        for k in reversed(range(1, half)):
            remote(source, landing.at[(me,) + part], number, recv_sem.at[number], across(k))

    def gather_forward(number, mirrored, landing, handed, part=()):
        block = landing.at[(mirror,) + part]
        taken(block, mirrored)
        for k in reversed(range(1, half)):
            remote(block, block, number, recv_sem.at[handed], across(k))

    group = lax.rem(me, half)

    def spread(number, source, landing, distances, handed=None):
        for k in reversed(distances):
            peer = across(k)
            received_by = recv_sem.at[number if handed is None else handed]
            remote(source(peer), landing, number, received_by, peer)

    everyone, own_half, other_half = range(1, count), range(1, half), range(half, count)

    loads[0].wait()
    loads[1].wait()
    pieces = []
    for i in range(rows):
        normed = layer_normalized(pair[i].astype(F32)).astype(BF16)
        pieces.append(dot(bias_w[...], normed, NT))
    slab = jnp.concatenate(pieces, 0).astype(BF16)
    bias_src[...] = slab
    bias_land[me] = slab

    for load in loads[2:6]:
        load.wait()
    token = lax.broadcasted_iota(jnp.int32, (table.shape[0], length), 0)
    zero_rows = []
    for s in range(seqs):
        one_hot = jnp.where(ids[pl.ds(s, 1), :] == token, 1.0, 0.0).astype(BF16)
        zero_rows.append(align[s].astype(F32) + dot(one_hot, table[...], TN))
    msa_zero = jnp.concatenate(zero_rows, 0)
    projected = dot(layer_normalized(msa_zero).astype(BF16), row_w[...])
    masks = [head_mask(h, head_size, channels) for h in range(heads)]
    scale = head_size ** (-0.5)

    loads[6].wait()
    loads[7].wait()
    def by_head(block):
        return jnp.concatenate([block * m for m in masks], 0)

    def split(part):
        query = (part[:, :channels] * scale).astype(BF16)
        key = part[:, channels : 2 * channels].astype(BF16)
        value = part[:, 2 * channels : 3 * channels].astype(BF16)
        scores = dot(by_head(query), key, NT).reshape(heads, query.shape[0], key.shape[0])
        return scores, by_head(value), jax.nn.sigmoid(part[:, 3 * channels :])

    zero_v[...] = msa_zero.reshape(zero_v.shape)
    for s in range(seqs):
        raw_v[s], value_v[s], open_v[s] = split(projected[s * length : (s + 1) * length])
    pl.semaphore_wait(barrier, half)
    gather_start(0, bias_sem.at[0], bias_src, bias_land)

    for load in loads[8:]:
        load.wait()
    tri_t[...] = jnp.transpose(tri_w[:, : 4 * pair_chan].astype(F32), (1, 0)).astype(BF16)
    fill(outer_f, outer_w[...].astype(F32))
    for d in range(width):
        outer_w2[:, d * pair_chan : (d + 1) * pair_chan] = pick(
            outer_f, d, width, width
        ).astype(BF16)

    reach = half * rows
    mine = lax.div(me, half)
    turns = (
        (mine, pl.multiple_of(mine * reach, reach)),
        (1 - mine, pl.multiple_of((1 - mine) * reach, reach)),
    )
    mask_bias = (mask[...].astype(F32) - 1.0) * 10000.0
    row_ones = by_head(jnp.ones((length, channels), BF16))
    lane_parts = channels // 128
    for turn, (which, start) in enumerate(turns):
        if turn == 0:
            gather_forward(0, bias_sem.at[0], bias_land, 7)
        taken(bias_land.at[pl.ds(0, half - 1)], recv_sem.at[7 * turn])
        fill(bias_f, landed(bias_land.at[pl.ds(which * half, half)]))
        extra = jnp.stack([pick(bias_f, h, reach, heads) for h in range(heads)], 0) + mask_bias
        gated = []
        for s in range(seqs):
            mixed = attend(raw_v[s, :, pl.ds(start, reach), :] + extra, value_v[s], row_ones)
            gated.append((open_v[s, pl.ds(start, reach), :] * mixed).astype(BF16))
        added = dot(jnp.concatenate(gated, 0), row_o[...])
        blocks = [
            zero_v[s, pl.ds(start, reach), :] + added[s * reach : (s + 1) * reach]
            for s in range(seqs)
        ]
        ordered = interleave(blocks, rows)
        msa_src[pl.ds(which * half, half)] = jnp.concatenate(
            [ordered[:, :, k * 128 : (k + 1) * 128] for k in range(lane_parts)], 1
        ).astype(BF16)
        if turn == 0:
            msa_land[me] = msa_src[me]
        spread(
            1,
            lambda peer: msa_src.at[peer],
            msa_land.at[me],
            own_half if turn == 0 else other_half,
            1 + 7 * turn,
        )

    share = seqs * half
    to_output = selection(
        total * rows,
        lambda o: (
            split_index(o, rows)[1] * total
            + split_index(o, rows * share)[0] * share
            + split_index(split_index(o, rows)[0], seqs)[1] * half
            + split_index(split_index(o, rows * seqs)[0], half)[1]
        ),
    )
    step = lane_parts * seqs * rows
    for turn, (which, start) in enumerate(turns):
        taken(msa_land.at[pl.ds(0, half - 1 + turn)], recv_sem.at[1 + 7 * turn])
        fill(msa_f, landed(msa_land.at[pl.ds(which * half, half)]))
        column = jnp.concatenate(
            [
                jnp.concatenate(
                    [
                        pick(msa_f, (k * seqs + s) * rows + i, half, step)
                        for i in range(rows)
                        for s in range(seqs)
                    ],
                    0,
                )
                for k in range(lane_parts)
            ],
            1,
        )
        projected = dot(layer_normalized(column).astype(BF16), col_w[...])
        place = pl.ds(pl.multiple_of(which * share, share), share)
        for i in range(rows):
            column_v[i, place, :] = column[i * share : (i + 1) * share]
            project_v[i, place, :] = projected[i * share : (i + 1) * share]
    pack = max(1, 128 // total)
    groups = width // pack
    lanes = pack * total
    column_ones = by_head(jnp.ones((lanes, channels), BF16))
    together = (
        split_index(lax.broadcasted_iota(jnp.int32, (1, lanes, lanes), 1), total)[0]
        == split_index(lax.broadcasted_iota(jnp.int32, (1, lanes, lanes), 2), total)[0]
    )
    two_rows, inputs = [], []
    for start in range(0, rows, pack):
        block = column_v[start : start + pack].reshape(lanes, channels)
        scores, value, opened = split(
            project_v[start : start + pack].reshape(lanes, 4 * channels)
        )
        if pack > 1:
            scores = jnp.where(together, scores, -1e30)
        gated = (opened * attend(scores, value, column_ones)).astype(BF16)
        msa_two = block + dot(gated, col_o[...])
        outer_input = layer_normalized(msa_two).astype(BF16)
        two_rows.append(msa_two.astype(BF16))
        inputs.append(outer_input)

        right_t = dot(factor_w[width:, :], outer_input, NT)
        slab = jnp.concatenate(pack_lanes(right_t, pack, total), 0).astype(BF16)
        part = (start // pack,)
        right_src[part[0]] = slab
        right_land[me, part[0]] = slab
        gather_start(2, right_sem.at[part[0]], right_src.at[part[0]], right_land, part)

    left = dot(jnp.concatenate(inputs, 0), factor_w[:width, :], NT).astype(BF16)
    chunk = 8
    for start in range(0, width, chunk):
        product = dot(left, outer_w2[:, start * pair_chan : (start + chunk) * pair_chan])
        for d in range(start, start + chunk):
            at = ((d % groups) * pack + d // groups) * total
            for i in range(rows):
                left_t[at : at + total, i * pair_chan : (i + 1) * pair_chan] = product[
                    i * total : (i + 1) * total,
                    (d - start) * pair_chan : (d - start + 1) * pair_chan,
                ].astype(BF16)

    own = pair_chan // half
    fold = max(1, 128 // reach)
    height = pair_chan // fold
    normed = []
    for k in range(rows // pack):
        gather_forward(2, right_sem.at[k], right_land, 6, (k,))
    for turn, (which, start) in enumerate(turns):
        taken(right_land.at[pl.ds(0, half - 1)], recv_sem.at[2 + 4 * turn])
        fill(right_f, landed(right_land.at[pl.ds(which * half, half)]))
        for k in range(groups):
            right_m[:, k * lanes : (k + 1) * lanes] = pick(right_f, k, reach, groups).astype(BF16)
        update = dot(right_m[...], left_t[...]) * (1.0 / total)
        stacked = []
        for i in range(rows):
            one = pair[i, pl.ds(start, reach), :].astype(F32) + update[
                :, i * pair_chan : (i + 1) * pair_chan
            ]
            pair_one_v[i, pl.ds(start, reach), :] = one
            stacked.append(one)
        normed.append(layer_normalized(jnp.concatenate(stacked, 0)).astype(BF16))
        for side, target in ((1, tri_right), (0, tri_left)):
            low = 2 * side * pair_chan
            factors = dot(tri_t[low : low + 2 * pair_chan, :], normed[turn], NT)
            factor = jax.nn.sigmoid(factors[pair_chan:]) * factors[:pair_chan]
            wide = fold * reach
            for base in range(rows // fold):
                packed = pack_lanes(factor[:, base * wide : (base + 1) * wide], fold, reach)
                for place in range(fold):
                    at = (base * fold + place) * height
                    fill(tri_f.at[side, :, pl.ds(at, height), :], packed[place])
            for g in range(half):
                target[turn, g] = pick(
                    tri_f.at[side], g, rows * own // fold, half
                ).astype(BF16)
            if side == 1:
                spread(
                    3,
                    lambda peer: tri_right.at[turn, lax.rem(peer, half)],
                    tri_land.at[which, me],
                    everyone,
                )
            else:
                spread(
                    4,
                    lambda peer: tri_left.at[turn, lax.rem(peer, half)],
                    left_land.at[which, group],
                    own_half,
                )
        left_land[which, group] = tri_left[turn, group]
        tri_land[which, me] = tri_right[turn, group]

    ordered = dot(to_output, jnp.concatenate(two_rows, 0))
    align_out[...] = ordered.reshape(total, rows, channels).astype(BF16)
    for turn in range(2):
        opened = jax.nn.sigmoid(dot(normed[turn], tri_w[:, 4 * pair_chan :]))
        for i in range(rows):
            gate_v[i, pl.ds(turns[turn][1], reach), :] = opened[i * reach : (i + 1) * reach]

    taken(tri_land.at[pl.ds(0, 2), pl.ds(0, count - 1)], recv_sem.at[3])
    taken(left_land.at[pl.ds(0, 2), pl.ds(0, half - 1)], recv_sem.at[4])
    fill(land_f, landed(tri_land))
    fill(left_f, landed(left_land))
    slab_rows = rows * own // fold
    block = half * rows
    lane = lax.broadcasted_iota(jnp.int32, (1, fold * reach), 1)
    folds = [
        jnp.where((lane >= k * reach) & (lane < (k + 1) * reach), 1.0, 0.0).astype(BF16)
        for k in range(fold)
    ]
    for c in range(own // fold):
        step = own // fold
        left_sides = [
            jnp.concatenate(
                [
                    pick(left_f, q * half * slab_rows + i * step + c, half, slab_rows)
                    for i in range(rows)
                ],
                0,
            ).astype(BF16)
            for q in range(2)
        ]
        right_side = jnp.concatenate(
            [pick(land_f, q * count * slab_rows + c, length, step) for q in range(2)], 1
        ).astype(BF16)
        left_side = jnp.concatenate(
            [jnp.concatenate([side * m for side in left_sides], 1) for m in folds], 0
        )
        product = dot(left_side, right_side, NT)
        for k in range(fold):
            fill(
                comb_f.at[:, pl.ds((k * step + c) * block, block), :],
                product[k * block : (k + 1) * block],
            )
    for p in range(half):
        back_src[p] = pick(comb_f, p, own * rows, half).astype(BF16)
    back_land[group] = back_src[group]
    spread(5, lambda peer: back_src.at[lax.rem(peer, half)], back_land.at[group], own_half)

    taken(back_land.at[pl.ds(0, half - 1)], recv_sem.at[5])
    for number, sent in enumerate((bias_land, msa_land, right_land)):
        taken(sent.at[pl.ds(0, count - 1)], send_sem.at[number])
    taken(tri_land.at[pl.ds(0, 2), pl.ds(0, count - 1)], send_sem.at[3])
    taken(left_land.at[pl.ds(0, 2), pl.ds(0, half - 1)], send_sem.at[4])
    taken(back_land.at[pl.ds(0, half - 1)], send_sem.at[5])


def finish_kernel(rows, align, back_land, pair_one, gate, tri_o, align_out, pair_out, back_f, pair_v, sem):
    store_align = pltpu.make_async_copy(align, align_out, sem.at[0])
    store_align.start()
    fill(back_f, landed(back_land))
    owners = back_land.shape[0]
    own = back_land.shape[1] // rows
    stores = []
    for i in range(rows):
        channels = [pick(back_f, c * rows + i, owners, own * rows) for c in range(own)]
        combined = layer_normalized(jnp.concatenate(channels, 0), 0).astype(BF16)
        result = pair_one[i] + gate[i] * dot(combined, tri_o[...], TN)
        pair_v[i] = result.astype(BF16)
        stores.append(pltpu.make_async_copy(pair_v.at[i], pair_out.at[i], sem.at[1 + i]))
        stores[i].start()
    store_align.wait()
    for store in stores:
        store.wait()


def shards(
    homolog_symbol_ids,
    residue_attend_mask,
    alignment_state,
    pair,
    symbol_lookup_matrix,
    pair_bias_weight,
    row_projection_weight,
    horizontal_readout_matrix,
    column_projection_weight,
    vertical_readout_matrix,
    product_factor_matrices,
    outer_output_weight,
    triangle_input_weight,
    triangle_output_weight,
):
    count = lax.axis_size("res")
    seqs, length, channels = alignment_state.shape
    rows, _, pair_chan = pair.shape
    heads = pair_bias_weight.shape[1]
    width = product_factor_matrices.shape[1] // 2
    total = seqs * count
    half = count // 2
    own = pair_chan // half
    pack = max(1, 128 // total)
    groups, lanes = width // pack, pack * total
    operands = [
        homolog_symbol_ids,
        residue_attend_mask.reshape(1, length),
        alignment_state,
        pair,
        symbol_lookup_matrix,
        pair_bias_weight.T,
        row_projection_weight,
        horizontal_readout_matrix,
        column_projection_weight,
        vertical_readout_matrix,
        product_factor_matrices.T,
        outer_output_weight,
        triangle_input_weight,
    ]
    lane_parts = channels // 128
    vmem = pltpu.VMEM
    parts = rows // pack
    reach = half * rows
    fold = max(1, 128 // reach)
    tri_slab = (rows * own // fold, fold * reach)
    exchanges = [
        vmem((heads * rows, length), BF16),
        vmem((count, heads * rows, length), BF16),
        vmem((count, lane_parts * seqs * rows, 128), BF16),
        vmem((count, lane_parts * seqs * rows, 128), BF16),
        vmem((parts, groups * pack, lanes), BF16),
        vmem((count, parts, groups * pack, lanes), BF16),
        vmem((2, half) + tri_slab, BF16),
        vmem((2, half) + tri_slab, BF16),
        vmem((2, half) + tri_slab, BF16),
        vmem((2, count) + tri_slab, BF16),
        vmem((half, own * rows, length), BF16),
    ]

    def pieces(row_count, lane_count):
        return vmem((lane_count // 128, row_count, 128), F32)

    scratch = (
        [vmem(x.shape, x.dtype) for x in operands]
        + exchanges
        + [
            pieces(half * heads * rows, length),
            pieces(half * lane_parts * seqs * rows, 128),
            pieces(width * width, pair_chan),
            vmem((width, width * pair_chan), BF16),
            vmem((width * total, rows * pair_chan), BF16),
            pieces(reach * groups, lanes),
            vmem((reach, width * total), BF16),
            vmem((4 * pair_chan, pair_chan), BF16),
            vmem((2, fold * reach // 128, rows * pair_chan // fold, 128), F32),
            pieces(2 * count * tri_slab[0], tri_slab[1]),
            pieces(2 * half * tri_slab[0], tri_slab[1]),
            pieces(half * own * rows, length),
            vmem((seqs, length, channels), F32),
            vmem((seqs, heads, length, length), F32),
            vmem((seqs, heads * length, channels), BF16),
            vmem((seqs, length, channels), F32),
            vmem((rows, total, channels), F32),
            vmem((rows, total, 4 * channels), F32),
            pltpu.SemaphoreType.DMA((len(operands),)),
            pltpu.SemaphoreType.DMA((6,)),
            pltpu.SemaphoreType.DMA((9,)),
            pltpu.SemaphoreType.DMA((1,)),
            pltpu.SemaphoreType.DMA((parts,)),
        ]
    )
    sizes = (count, seqs, rows, length, channels, heads, width, pair_chan, total)
    anywhere = pl.BlockSpec(memory_space=pltpu.HBM)
    inside = pl.BlockSpec(memory_space=pltpu.VMEM)
    aligned, back, pair_one, gate = pl.pallas_call(
        functools.partial(block_kernel, sizes),
        out_shape=(
            jax.ShapeDtypeStruct((total, rows, channels), BF16),
            jax.ShapeDtypeStruct((half, own * rows, length), BF16),
            jax.ShapeDtypeStruct(pair.shape, F32),
            jax.ShapeDtypeStruct(pair.shape, F32),
        ),
        in_specs=[anywhere] * len(operands),
        out_specs=(inside,) * 4,
        scratch_shapes=scratch,
        compiler_params=pltpu.CompilerParams(
            collective_id=0, has_side_effects=True, vmem_limit_bytes=VMEM_BYTES
        ),
    )(*[pltpu.with_memory_space_constraint(x, pltpu.HBM) for x in operands])
    return pl.pallas_call(
        functools.partial(finish_kernel, rows),
        out_shape=(
            jax.ShapeDtypeStruct((total, rows, channels), BF16),
            jax.ShapeDtypeStruct(pair.shape, BF16),
        ),
        in_specs=[inside] * 5,
        out_specs=(anywhere, anywhere),
        scratch_shapes=[
            pieces(half * own * rows, length),
            vmem(pair.shape, BF16),
            pltpu.SemaphoreType.DMA((1 + rows,)),
        ],
        compiler_params=pltpu.CompilerParams(vmem_limit_bytes=VMEM_BYTES // 4),
    )(aligned, back, pair_one, gate, triangle_output_weight)


def solution(mesh):
    placed = (
        P(("crop", "res"), None),
        P("crop"),
        P(("crop", "res"), None, None),
        P(("crop", "res"), None, None),
        P(),
        P(),
        P(),
        P(),
        P(),
        P(),
        P(),
        P(),
        P(),
        P(),
    )
    return jax.shard_map(
        shards,
        mesh=mesh,
        in_specs=placed,
        out_specs=(P("crop", "res", None), P(("crop", "res"), None, None)),
        check_vma=False,
    )
```

```python
import functools

import jax
import jax.numpy as jnp
from jax import lax
from jax.experimental import pallas as pl
from jax.experimental.pallas import tpu as pltpu
from jax.sharding import PartitionSpec as P

EPSILON = 1e-05
MESH = pl.DeviceIdType.MESH
VMEM_BYTES = 40 * 1024 * 1024
F32 = jnp.float32
BF16 = jnp.bfloat16

NN = (((1,), (0,)), ((), ()))
NT = (((1,), (1,)), ((), ()))
TN = (((0,), (0,)), ((), ()))


def dot(a, b, dims=NN):
    return lax.dot_general(a, b, dims, preferred_element_type=F32)


def layer_normalized(rows, axis=-1):
    average = jnp.mean(rows, axis, keepdims=True)
    centred = rows - average
    spread = jnp.mean(centred * centred, axis, keepdims=True)
    return centred * lax.rsqrt(spread + EPSILON)


def split_index(index, size):
    if size & (size - 1) == 0:
        return lax.shift_right_logical(index, jnp.int32(size.bit_length() - 1)), index & (size - 1)
    return lax.div(index, size), lax.rem(index, size)


def selection(size, source):
    row = lax.broadcasted_iota(jnp.int32, (size, size), 0)
    column = lax.broadcasted_iota(jnp.int32, (size, size), 1)
    return jnp.where(column == source(row), 1.0, 0.0).astype(BF16)


def head_mask(head, head_size, channels):
    lane = lax.broadcasted_iota(jnp.int32, (1, channels), 1)
    inside = (lane >= head * head_size) & (lane < (head + 1) * head_size)
    return jnp.where(inside, 1.0, 0.0).astype(BF16)


def fill(buffer, values):
    for k in range(buffer.shape[0]):
        buffer[k] = values[:, k * 128 : (k + 1) * 128]


def pick(buffer, start, size, stride):
    return jnp.concatenate(
        [buffer[k, pl.ds(start, size, stride=stride), :] for k in range(buffer.shape[0])], 1
    )


def landed(landing):
    blocks = landing[...].astype(F32)
    return blocks.reshape(-1, blocks.shape[-1])


def pack_lanes(block, pack, size):
    if pack == 1:
        return [block]
    height, lanes = block.shape[0] // pack, pack * size
    lane = lax.broadcasted_iota(jnp.int32, (height, lanes), 1)
    packed = []
    for place in range(pack):
        joined = None
        for k in range(pack):
            piece = block[k * height : (k + 1) * height]
            shift = ((k - place) * size) % lanes
            if shift:
                piece = pltpu.roll(piece, shift, 1)
            joined = piece if joined is None else jnp.where(lane >= k * size, piece, joined)
        packed.append(joined)
    return packed


def attend(scores, values, ones):
    powers = jnp.exp(scores - jnp.max(scores, -1, keepdims=True)).astype(BF16)
    side = jnp.concatenate([powers[h] for h in range(powers.shape[0])], 1)
    return dot(side, values) / dot(side, ones)


def interleave(blocks, rows):
    owners, lanes = blocks[0].shape[0] // rows, blocks[0].shape[1]
    if len(blocks) == 2 and rows == 4:
        one, two = [b.reshape(owners // 2, 8, lanes) for b in blocks]
        low = lax.broadcasted_iota(jnp.int32, one.shape, 1) < rows
        even = jnp.where(low, one, pltpu.roll(two, rows, 1))
        odd = jnp.where(low, pltpu.roll(one, rows, 1), two)
        return jnp.stack([even, odd], 1).reshape(owners, 8, lanes)
    return jnp.stack(
        [
            jnp.concatenate([b[p * rows : (p + 1) * rows] for b in blocks], 0)
            for p in range(owners)
        ],
        0,
    )


def block_kernel(
    sizes,
    ids_h, mask_h, align_h, pair_h, table_h, bias_w_h, row_w_h, row_o_h, col_w_h, col_o_h,
    factor_w_h, outer_w_h, tri_w_h,
    align_out, back_land, pair_one_v, gate_v,
    ids, mask, align, pair, table, bias_w, row_w, row_o, col_w, col_o,
    factor_w, outer_w, tri_w,
    bias_src, bias_land, msa_src, msa_land, right_src, right_land, tri_left, left_land,
    tri_right, tri_land, back_src,
    bias_f, msa_f, outer_f, outer_w2, left_t, right_f, right_m, tri_t,
    tri_f, land_f, left_f, comb_f, zero_v, raw_v, value_v, open_v, column_v, project_v,
    in_sem, send_sem, recv_sem, bias_sem, right_sem,
):
    count, seqs, rows, length, channels, heads, width, pair_chan, total = sizes
    head_size = channels // heads
    me = lax.axis_index("res")
    half = count // 2
    flips = [
        (1 - 2 * lax.rem(lax.div(me, 1 << j), 2)) * (1 << j) for j in range(count.bit_length() - 1)
    ]

    def across(k):
        return me + sum(flips[j] for j in range(len(flips)) if (k >> j) & 1)

    mirror = across(half)
    barrier = pltpu.get_barrier_semaphore()
    for k in reversed(range(1, half + 1)):
        pl.semaphore_signal(barrier, inc=1, device_id={"res": across(k)}, device_id_type=MESH)

    staged = [
        (pair_h, pair), (bias_w_h, bias_w), (align_h, align), (ids_h, ids), (table_h, table),
        (row_w_h, row_w), (mask_h, mask), (row_o_h, row_o), (col_w_h, col_w), (col_o_h, col_o),
        (factor_w_h, factor_w), (outer_w_h, outer_w), (tri_w_h, tri_w),
    ]
    loads = [
        pltpu.make_async_copy(source, target, in_sem.at[k])
        for k, (source, target) in enumerate(staged)
    ]
    for load in loads:
        load.start()

    def remote(source, target, number, received_by, peer):
        pltpu.make_async_remote_copy(
            src_ref=source,
            dst_ref=target,
            send_sem=send_sem.at[number],
            recv_sem=received_by,
            device_id={"res": peer},
            device_id_type=MESH,
        ).start()

    def taken(landing, semaphore):
        pltpu.make_async_copy(landing, landing, semaphore).wait()

    def gather_start(number, mirrored, source, landing, part=()):
        remote(source, landing.at[(me,) + part], number, mirrored, mirror)
        for k in reversed(range(1, half)):
            remote(source, landing.at[(me,) + part], number, recv_sem.at[number], across(k))

    def gather_forward(number, mirrored, landing, handed, part=()):
        block = landing.at[(mirror,) + part]
        taken(block, mirrored)
        for k in reversed(range(1, half)):
            remote(block, block, number, recv_sem.at[handed], across(k))

    group = lax.rem(me, half)

    def spread(number, source, landing, distances, handed=None):
        for k in reversed(distances):
            peer = across(k)
            received_by = recv_sem.at[number if handed is None else handed]
            remote(source(peer), landing, number, received_by, peer)

    everyone, own_half, other_half = range(1, count), range(1, half), range(half, count)

    loads[0].wait()
    loads[1].wait()
    pieces = []
    for i in range(rows):
        normed = layer_normalized(pair[i].astype(F32)).astype(BF16)
        pieces.append(dot(bias_w[...], normed, NT))
    slab = jnp.concatenate(pieces, 0).astype(BF16)
    bias_src[...] = slab
    bias_land[me] = slab

    pl.semaphore_wait(barrier, half)
    gather_start(0, bias_sem.at[0], bias_src, bias_land)

    for load in loads[2:6]:
        load.wait()
    token = lax.broadcasted_iota(jnp.int32, (table.shape[0], length), 0)
    zero_rows = []
    for s in range(seqs):
        one_hot = jnp.where(ids[pl.ds(s, 1), :] == token, 1.0, 0.0).astype(BF16)
        zero_rows.append(align[s].astype(F32) + dot(one_hot, table[...], TN))
    msa_zero = jnp.concatenate(zero_rows, 0)
    projected = dot(layer_normalized(msa_zero).astype(BF16), row_w[...])
    masks = [head_mask(h, head_size, channels) for h in range(heads)]
    scale = head_size ** (-0.5)

    loads[6].wait()
    loads[7].wait()
    def by_head(block):
        return jnp.concatenate([block * m for m in masks], 0)

    def split(part):
        query = (part[:, :channels] * scale).astype(BF16)
        key = part[:, channels : 2 * channels].astype(BF16)
        value = part[:, 2 * channels : 3 * channels].astype(BF16)
        scores = dot(by_head(query), key, NT).reshape(heads, query.shape[0], key.shape[0])
        return scores, by_head(value), jax.nn.sigmoid(part[:, 3 * channels :])

    zero_v[...] = msa_zero.reshape(zero_v.shape)
    for s in range(seqs):
        raw_v[s], value_v[s], open_v[s] = split(projected[s * length : (s + 1) * length])
    for load in loads[8:]:
        load.wait()
    tri_t[...] = jnp.transpose(tri_w[:, : 4 * pair_chan].astype(F32), (1, 0)).astype(BF16)
    fill(outer_f, outer_w[...].astype(F32))
    for d in range(width):
        outer_w2[:, d * pair_chan : (d + 1) * pair_chan] = pick(
            outer_f, d, width, width
        ).astype(BF16)

    reach = half * rows
    mine = lax.div(me, half)
    turns = (
        (mine, pl.multiple_of(mine * reach, reach)),
        (1 - mine, pl.multiple_of((1 - mine) * reach, reach)),
    )
    mask_bias = (mask[...].astype(F32) - 1.0) * 10000.0
    row_ones = by_head(jnp.ones((length, channels), BF16))
    lane_parts = channels // 128
    for turn, (which, start) in enumerate(turns):
        if turn == 0:
            gather_forward(0, bias_sem.at[0], bias_land, 7)
        taken(bias_land.at[pl.ds(0, half - 1)], recv_sem.at[7 * turn])
        fill(bias_f, landed(bias_land.at[pl.ds(which * half, half)]))
        extra = jnp.stack([pick(bias_f, h, reach, heads) for h in range(heads)], 0) + mask_bias
        gated = []
        for s in range(seqs):
            mixed = attend(raw_v[s, :, pl.ds(start, reach), :] + extra, value_v[s], row_ones)
            gated.append((open_v[s, pl.ds(start, reach), :] * mixed).astype(BF16))
        added = dot(jnp.concatenate(gated, 0), row_o[...])
        blocks = [
            zero_v[s, pl.ds(start, reach), :] + added[s * reach : (s + 1) * reach]
            for s in range(seqs)
        ]
        ordered = interleave(blocks, rows)
        msa_src[pl.ds(which * half, half)] = jnp.concatenate(
            [ordered[:, :, k * 128 : (k + 1) * 128] for k in range(lane_parts)], 1
        ).astype(BF16)
        if turn == 0:
            msa_land[me] = msa_src[me]
        spread(
            1,
            lambda peer: msa_src.at[peer],
            msa_land.at[me],
            own_half if turn == 0 else other_half,
            1 + 7 * turn,
        )

    share = seqs * half
    to_output = selection(
        total * rows,
        lambda o: (
            split_index(o, rows)[1] * total
            + split_index(o, rows * share)[0] * share
            + split_index(split_index(o, rows)[0], seqs)[1] * half
            + split_index(split_index(o, rows * seqs)[0], half)[1]
        ),
    )
    step = lane_parts * seqs * rows
    for turn, (which, start) in enumerate(turns):
        taken(msa_land.at[pl.ds(0, half - 1 + turn)], recv_sem.at[1 + 7 * turn])
        fill(msa_f, landed(msa_land.at[pl.ds(which * half, half)]))
        column = jnp.concatenate(
            [
                jnp.concatenate(
                    [
                        pick(msa_f, (k * seqs + s) * rows + i, half, step)
                        for i in range(rows)
                        for s in range(seqs)
                    ],
                    0,
                )
                for k in range(lane_parts)
            ],
            1,
        )
        projected = dot(layer_normalized(column).astype(BF16), col_w[...])
        place = pl.ds(pl.multiple_of(which * share, share), share)
        for i in range(rows):
            column_v[i, place, :] = column[i * share : (i + 1) * share]
            project_v[i, place, :] = projected[i * share : (i + 1) * share]
    pack = max(1, 128 // total)
    groups = width // pack
    lanes = pack * total
    column_ones = by_head(jnp.ones((lanes, channels), BF16))
    together = (
        split_index(lax.broadcasted_iota(jnp.int32, (1, lanes, lanes), 1), total)[0]
        == split_index(lax.broadcasted_iota(jnp.int32, (1, lanes, lanes), 2), total)[0]
    )
    two_rows, inputs = [], []
    for start in range(0, rows, pack):
        block = column_v[start : start + pack].reshape(lanes, channels)
        scores, value, opened = split(
            project_v[start : start + pack].reshape(lanes, 4 * channels)
        )
        if pack > 1:
            scores = jnp.where(together, scores, -1e30)
        gated = (opened * attend(scores, value, column_ones)).astype(BF16)
        msa_two = block + dot(gated, col_o[...])
        outer_input = layer_normalized(msa_two).astype(BF16)
        two_rows.append(msa_two.astype(BF16))
        inputs.append(outer_input)

        right_t = dot(factor_w[width:, :], outer_input, NT)
        slab = jnp.concatenate(pack_lanes(right_t, pack, total), 0).astype(BF16)
        part = (start // pack,)
        right_src[part[0]] = slab
        right_land[me, part[0]] = slab
        gather_start(2, right_sem.at[part[0]], right_src.at[part[0]], right_land, part)

    left = dot(jnp.concatenate(inputs, 0), factor_w[:width, :], NT).astype(BF16)
    chunk = 8
    for start in range(0, width, chunk):
        product = dot(left, outer_w2[:, start * pair_chan : (start + chunk) * pair_chan])
        for d in range(start, start + chunk):
            at = ((d % groups) * pack + d // groups) * total
            for i in range(rows):
                left_t[at : at + total, i * pair_chan : (i + 1) * pair_chan] = product[
                    i * total : (i + 1) * total,
                    (d - start) * pair_chan : (d - start + 1) * pair_chan,
                ].astype(BF16)

    own = pair_chan // half
    fold = max(1, 128 // reach)
    height = pair_chan // fold
    normed = []
    for k in range(rows // pack):
        gather_forward(2, right_sem.at[k], right_land, 6, (k,))
    for turn, (which, start) in enumerate(turns):
        taken(right_land.at[pl.ds(0, half - 1)], recv_sem.at[2 + 4 * turn])
        fill(right_f, landed(right_land.at[pl.ds(which * half, half)]))
        for k in range(groups):
            right_m[:, k * lanes : (k + 1) * lanes] = pick(right_f, k, reach, groups).astype(BF16)
        update = dot(right_m[...], left_t[...]) * (1.0 / total)
        stacked = []
        for i in range(rows):
            one = pair[i, pl.ds(start, reach), :].astype(F32) + update[
                :, i * pair_chan : (i + 1) * pair_chan
            ]
            pair_one_v[i, pl.ds(start, reach), :] = one
            stacked.append(one)
        normed.append(layer_normalized(jnp.concatenate(stacked, 0)).astype(BF16))
        for side, target in ((1, tri_right), (0, tri_left)):
            low = 2 * side * pair_chan
            factors = dot(tri_t[low : low + 2 * pair_chan, :], normed[turn], NT)
            factor = jax.nn.sigmoid(factors[pair_chan:]) * factors[:pair_chan]
            wide = fold * reach
            for base in range(rows // fold):
                packed = pack_lanes(factor[:, base * wide : (base + 1) * wide], fold, reach)
                for place in range(fold):
                    at = (base * fold + place) * height
                    fill(tri_f.at[side, :, pl.ds(at, height), :], packed[place])
            for g in range(half):
                target[turn, g] = pick(
                    tri_f.at[side], g, rows * own // fold, half
                ).astype(BF16)
            if side == 1:
                spread(
                    3,
                    lambda peer: tri_right.at[turn, lax.rem(peer, half)],
                    tri_land.at[which, me],
                    everyone,
                )
            else:
                spread(
                    4,
                    lambda peer: tri_left.at[turn, lax.rem(peer, half)],
                    left_land.at[which, group],
                    own_half,
                )
        left_land[which, group] = tri_left[turn, group]
        tri_land[which, me] = tri_right[turn, group]

    ordered = dot(to_output, jnp.concatenate(two_rows, 0))
    align_out[...] = ordered.reshape(total, rows, channels).astype(BF16)
    for turn in range(2):
        opened = jax.nn.sigmoid(dot(normed[turn], tri_w[:, 4 * pair_chan :]))
        for i in range(rows):
            gate_v[i, pl.ds(turns[turn][1], reach), :] = opened[i * reach : (i + 1) * reach]

    taken(tri_land.at[pl.ds(0, 2), pl.ds(0, count - 1)], recv_sem.at[3])
    taken(left_land.at[pl.ds(0, 2), pl.ds(0, half - 1)], recv_sem.at[4])
    fill(land_f, landed(tri_land))
    fill(left_f, landed(left_land))
    slab_rows = rows * own // fold
    block = half * rows
    lane = lax.broadcasted_iota(jnp.int32, (1, fold * reach), 1)
    folds = [
        jnp.where((lane >= k * reach) & (lane < (k + 1) * reach), 1.0, 0.0).astype(BF16)
        for k in range(fold)
    ]
    for c in range(own // fold):
        step = own // fold
        left_sides = [
            jnp.concatenate(
                [
                    pick(left_f, q * half * slab_rows + i * step + c, half, slab_rows)
                    for i in range(rows)
                ],
                0,
            ).astype(BF16)
            for q in range(2)
        ]
        right_side = jnp.concatenate(
            [pick(land_f, q * count * slab_rows + c, length, step) for q in range(2)], 1
        ).astype(BF16)
        left_side = jnp.concatenate(
            [jnp.concatenate([side * m for side in left_sides], 1) for m in folds], 0
        )
        product = dot(left_side, right_side, NT)
        for k in range(fold):
            fill(
                comb_f.at[:, pl.ds((k * step + c) * block, block), :],
                product[k * block : (k + 1) * block],
            )
    for p in range(half):
        back_src[p] = pick(comb_f, p, own * rows, half).astype(BF16)
    back_land[group] = back_src[group]
    spread(5, lambda peer: back_src.at[lax.rem(peer, half)], back_land.at[group], own_half)

    taken(back_land.at[pl.ds(0, half - 1)], recv_sem.at[5])
    for number, sent in enumerate((bias_land, msa_land, right_land)):
        taken(sent.at[pl.ds(0, count - 1)], send_sem.at[number])
    taken(tri_land.at[pl.ds(0, 2), pl.ds(0, count - 1)], send_sem.at[3])
    taken(left_land.at[pl.ds(0, 2), pl.ds(0, half - 1)], send_sem.at[4])
    taken(back_land.at[pl.ds(0, half - 1)], send_sem.at[5])


def finish_kernel(rows, align, back_land, pair_one, gate, tri_o, align_out, pair_out, back_f, pair_v, sem):
    store_align = pltpu.make_async_copy(align, align_out, sem.at[0])
    store_align.start()
    fill(back_f, landed(back_land))
    owners = back_land.shape[0]
    own = back_land.shape[1] // rows
    stores = []
    for i in range(rows):
        channels = [pick(back_f, c * rows + i, owners, own * rows) for c in range(own)]
        combined = layer_normalized(jnp.concatenate(channels, 0), 0).astype(BF16)
        result = pair_one[i] + gate[i] * dot(combined, tri_o[...], TN)
        pair_v[i] = result.astype(BF16)
        stores.append(pltpu.make_async_copy(pair_v.at[i], pair_out.at[i], sem.at[1 + i]))
        stores[i].start()
    store_align.wait()
    for store in stores:
        store.wait()


def shards(
    homolog_symbol_ids,
    residue_attend_mask,
    alignment_state,
    pair,
    symbol_lookup_matrix,
    pair_bias_weight,
    row_projection_weight,
    horizontal_readout_matrix,
    column_projection_weight,
    vertical_readout_matrix,
    product_factor_matrices,
    outer_output_weight,
    triangle_input_weight,
    triangle_output_weight,
):
    count = lax.axis_size("res")
    seqs, length, channels = alignment_state.shape
    rows, _, pair_chan = pair.shape
    heads = pair_bias_weight.shape[1]
    width = product_factor_matrices.shape[1] // 2
    total = seqs * count
    half = count // 2
    own = pair_chan // half
    pack = max(1, 128 // total)
    groups, lanes = width // pack, pack * total
    operands = [
        homolog_symbol_ids,
        residue_attend_mask.reshape(1, length),
        alignment_state,
        pair,
        symbol_lookup_matrix,
        pair_bias_weight.T,
        row_projection_weight,
        horizontal_readout_matrix,
        column_projection_weight,
        vertical_readout_matrix,
        product_factor_matrices.T,
        outer_output_weight,
        triangle_input_weight,
    ]
    lane_parts = channels // 128
    vmem = pltpu.VMEM
    parts = rows // pack
    reach = half * rows
    fold = max(1, 128 // reach)
    tri_slab = (rows * own // fold, fold * reach)
    exchanges = [
        vmem((heads * rows, length), BF16),
        vmem((count, heads * rows, length), BF16),
        vmem((count, lane_parts * seqs * rows, 128), BF16),
        vmem((count, lane_parts * seqs * rows, 128), BF16),
        vmem((parts, groups * pack, lanes), BF16),
        vmem((count, parts, groups * pack, lanes), BF16),
        vmem((2, half) + tri_slab, BF16),
        vmem((2, half) + tri_slab, BF16),
        vmem((2, half) + tri_slab, BF16),
        vmem((2, count) + tri_slab, BF16),
        vmem((half, own * rows, length), BF16),
    ]

    def pieces(row_count, lane_count):
        return vmem((lane_count // 128, row_count, 128), F32)

    scratch = (
        [vmem(x.shape, x.dtype) for x in operands]
        + exchanges
        + [
            pieces(half * heads * rows, length),
            pieces(half * lane_parts * seqs * rows, 128),
            pieces(width * width, pair_chan),
            vmem((width, width * pair_chan), BF16),
            vmem((width * total, rows * pair_chan), BF16),
            pieces(reach * groups, lanes),
            vmem((reach, width * total), BF16),
            vmem((4 * pair_chan, pair_chan), BF16),
            vmem((2, fold * reach // 128, rows * pair_chan // fold, 128), F32),
            pieces(2 * count * tri_slab[0], tri_slab[1]),
            pieces(2 * half * tri_slab[0], tri_slab[1]),
            pieces(half * own * rows, length),
            vmem((seqs, length, channels), F32),
            vmem((seqs, heads, length, length), F32),
            vmem((seqs, heads * length, channels), BF16),
            vmem((seqs, length, channels), F32),
            vmem((rows, total, channels), F32),
            vmem((rows, total, 4 * channels), F32),
            pltpu.SemaphoreType.DMA((len(operands),)),
            pltpu.SemaphoreType.DMA((6,)),
            pltpu.SemaphoreType.DMA((9,)),
            pltpu.SemaphoreType.DMA((1,)),
            pltpu.SemaphoreType.DMA((parts,)),
        ]
    )
    sizes = (count, seqs, rows, length, channels, heads, width, pair_chan, total)
    anywhere = pl.BlockSpec(memory_space=pltpu.HBM)
    inside = pl.BlockSpec(memory_space=pltpu.VMEM)
    aligned, back, pair_one, gate = pl.pallas_call(
        functools.partial(block_kernel, sizes),
        out_shape=(
            jax.ShapeDtypeStruct((total, rows, channels), BF16),
            jax.ShapeDtypeStruct((half, own * rows, length), BF16),
            jax.ShapeDtypeStruct(pair.shape, F32),
            jax.ShapeDtypeStruct(pair.shape, F32),
        ),
        in_specs=[anywhere] * len(operands),
        out_specs=(inside,) * 4,
        scratch_shapes=scratch,
        compiler_params=pltpu.CompilerParams(
            collective_id=0, has_side_effects=True, vmem_limit_bytes=VMEM_BYTES
        ),
    )(*[pltpu.with_memory_space_constraint(x, pltpu.HBM) for x in operands])
    return pl.pallas_call(
        functools.partial(finish_kernel, rows),
        out_shape=(
            jax.ShapeDtypeStruct((total, rows, channels), BF16),
            jax.ShapeDtypeStruct(pair.shape, BF16),
        ),
        in_specs=[inside] * 5,
        out_specs=(anywhere, anywhere),
        scratch_shapes=[
            pieces(half * own * rows, length),
            vmem(pair.shape, BF16),
            pltpu.SemaphoreType.DMA((1 + rows,)),
        ],
        compiler_params=pltpu.CompilerParams(vmem_limit_bytes=VMEM_BYTES // 4),
    )(aligned, back, pair_one, gate, triangle_output_weight)


def solution(mesh):
    placed = (
        P(("crop", "res"), None),
        P("crop"),
        P(("crop", "res"), None, None),
        P(("crop", "res"), None, None),
        P(),
        P(),
        P(),
        P(),
        P(),
        P(),
        P(),
        P(),
        P(),
        P(),
    )
    return jax.shard_map(
        shards,
        mesh=mesh,
        in_specs=placed,
        out_specs=(P("crop", "res", None), P(("crop", "res"), None, None)),
        check_vma=False,
    )
```

```python
import functools

import jax
import jax.numpy as jnp
from jax import lax
from jax.experimental import pallas as pl
from jax.experimental.pallas import tpu as pltpu
from jax.sharding import PartitionSpec as P

EPSILON = 1e-05
MESH = pl.DeviceIdType.MESH
VMEM_BYTES = 40 * 1024 * 1024
F32 = jnp.float32
BF16 = jnp.bfloat16

NN = (((1,), (0,)), ((), ()))
NT = (((1,), (1,)), ((), ()))
TN = (((0,), (0,)), ((), ()))


def dot(a, b, dims=NN):
    return lax.dot_general(a, b, dims, preferred_element_type=F32)


def layer_normalized(rows, axis=-1):
    average = jnp.mean(rows, axis, keepdims=True)
    centred = rows - average
    spread = jnp.mean(centred * centred, axis, keepdims=True)
    return centred * lax.rsqrt(spread + EPSILON)


def split_index(index, size):
    if size & (size - 1) == 0:
        return lax.shift_right_logical(index, jnp.int32(size.bit_length() - 1)), index & (size - 1)
    return lax.div(index, size), lax.rem(index, size)


def selection(size, source):
    row = lax.broadcasted_iota(jnp.int32, (size, size), 0)
    column = lax.broadcasted_iota(jnp.int32, (size, size), 1)
    return jnp.where(column == source(row), 1.0, 0.0).astype(BF16)


def head_mask(head, head_size, channels):
    lane = lax.broadcasted_iota(jnp.int32, (1, channels), 1)
    inside = (lane >= head * head_size) & (lane < (head + 1) * head_size)
    return jnp.where(inside, 1.0, 0.0).astype(BF16)


def fill(buffer, values):
    for k in range(buffer.shape[0]):
        buffer[k] = values[:, k * 128 : (k + 1) * 128]


def pick(buffer, start, size, stride):
    return jnp.concatenate(
        [buffer[k, pl.ds(start, size, stride=stride), :] for k in range(buffer.shape[0])], 1
    )


def landed(landing):
    blocks = landing[...].astype(F32)
    return blocks.reshape(-1, blocks.shape[-1])


def pack_lanes(block, pack, size):
    if pack == 1:
        return [block]
    height, lanes = block.shape[0] // pack, pack * size
    lane = lax.broadcasted_iota(jnp.int32, (height, lanes), 1)
    packed = []
    for place in range(pack):
        joined = None
        for k in range(pack):
            piece = block[k * height : (k + 1) * height]
            shift = ((k - place) * size) % lanes
            if shift:
                piece = pltpu.roll(piece, shift, 1)
            joined = piece if joined is None else jnp.where(lane >= k * size, piece, joined)
        packed.append(joined)
    return packed


def attend(scores, values, ones):
    sides = []
    for block in scores:
        powers = jnp.exp(block - jnp.max(block, -1, keepdims=True)).astype(BF16)
        sides.append(jnp.concatenate([powers[h] for h in range(powers.shape[0])], 1))
    mixed = jnp.concatenate([dot(side, value) for side, value in zip(sides, values)], 0)
    return mixed / dot(jnp.concatenate(sides, 0), ones)


def interleave(blocks, rows):
    owners, lanes = blocks[0].shape[0] // rows, blocks[0].shape[1]
    if len(blocks) == 2 and rows == 4:
        one, two = [b.reshape(owners // 2, 8, lanes) for b in blocks]
        low = lax.broadcasted_iota(jnp.int32, one.shape, 1) < rows
        even = jnp.where(low, one, pltpu.roll(two, rows, 1))
        odd = jnp.where(low, pltpu.roll(one, rows, 1), two)
        return jnp.stack([even, odd], 1).reshape(owners, 8, lanes)
    return jnp.stack(
        [
            jnp.concatenate([b[p * rows : (p + 1) * rows] for b in blocks], 0)
            for p in range(owners)
        ],
        0,
    )


def block_kernel(
    sizes,
    ids_h, mask_h, align_h, pair_h, table_h, bias_w_h, row_w_h, row_o_h, col_w_h, col_o_h,
    factor_w_h, outer_w_h, tri_w_h,
    align_out, back_land, pair_one_v, gate_v,
    ids, mask, align, pair, table, bias_w, row_w, row_o, col_w, col_o,
    factor_w, outer_w, tri_w,
    bias_src, bias_land, msa_src, msa_land, right_src, right_land, tri_left, left_land,
    tri_right, tri_land, back_src,
    bias_f, msa_f, outer_f, outer_w2, left_t, right_f, right_m, tri_t,
    tri_f, land_f, left_f, comb_f, zero_v, raw_v, value_v, open_v, column_v, project_v,
    in_sem, send_sem, recv_sem, bias_sem, right_sem,
):
    count, seqs, rows, length, channels, heads, width, pair_chan, total = sizes
    head_size = channels // heads
    me = lax.axis_index("res")
    half = count // 2
    flips = [
        (1 - 2 * lax.rem(lax.div(me, 1 << j), 2)) * (1 << j) for j in range(count.bit_length() - 1)
    ]

    def across(k):
        return me + sum(flips[j] for j in range(len(flips)) if (k >> j) & 1)

    mirror = across(half)
    barrier = pltpu.get_barrier_semaphore()
    for k in reversed(range(1, half + 1)):
        pl.semaphore_signal(barrier, inc=1, device_id={"res": across(k)}, device_id_type=MESH)

    staged = [
        (pair_h, pair), (bias_w_h, bias_w), (align_h, align), (ids_h, ids), (table_h, table),
        (row_w_h, row_w), (mask_h, mask), (row_o_h, row_o), (col_w_h, col_w), (col_o_h, col_o),
        (factor_w_h, factor_w), (outer_w_h, outer_w), (tri_w_h, tri_w),
    ]
    loads = [
        pltpu.make_async_copy(source, target, in_sem.at[k])
        for k, (source, target) in enumerate(staged)
    ]
    for load in loads:
        load.start()

    def remote(source, target, number, received_by, peer):
        pltpu.make_async_remote_copy(
            src_ref=source,
            dst_ref=target,
            send_sem=send_sem.at[number],
            recv_sem=received_by,
            device_id={"res": peer},
            device_id_type=MESH,
        ).start()

    def taken(landing, semaphore):
        pltpu.make_async_copy(landing, landing, semaphore).wait()

    def gather_start(number, mirrored, source, landing, part=()):
        remote(source, landing.at[(me,) + part], number, mirrored, mirror)
        for k in reversed(range(1, half)):
            remote(source, landing.at[(me,) + part], number, recv_sem.at[number], across(k))

    def gather_forward(number, mirrored, landing, handed, part=()):
        block = landing.at[(mirror,) + part]
        taken(block, mirrored)
        for k in reversed(range(1, half)):
            remote(block, block, number, recv_sem.at[handed], across(k))

    group = lax.rem(me, half)

    def spread(number, source, landing, distances, handed=None):
        for k in reversed(distances):
            peer = across(k)
            received_by = recv_sem.at[number if handed is None else handed]
            remote(source(peer), landing, number, received_by, peer)

    everyone, own_half, other_half = range(1, count), range(1, half), range(half, count)

    loads[0].wait()
    loads[1].wait()
    pieces = []
    for i in range(rows):
        normed = layer_normalized(pair[i].astype(F32)).astype(BF16)
        pieces.append(dot(bias_w[...], normed, NT))
    slab = jnp.concatenate(pieces, 0).astype(BF16)
    bias_src[...] = slab
    bias_land[me] = slab

    pl.semaphore_wait(barrier, half)
    gather_start(0, bias_sem.at[0], bias_src, bias_land)

    for load in loads[2:6]:
        load.wait()
    token = lax.broadcasted_iota(jnp.int32, (table.shape[0], length), 0)
    zero_rows = []
    for s in range(seqs):
        one_hot = jnp.where(ids[pl.ds(s, 1), :] == token, 1.0, 0.0).astype(BF16)
        zero_rows.append(align[s].astype(F32) + dot(one_hot, table[...], TN))
    msa_zero = jnp.concatenate(zero_rows, 0)
    projected = dot(layer_normalized(msa_zero).astype(BF16), row_w[...])
    masks = [head_mask(h, head_size, channels) for h in range(heads)]
    scale = head_size ** (-0.5)

    loads[6].wait()
    loads[7].wait()
    def by_head(block):
        return jnp.concatenate([block * m for m in masks], 0)

    def split(part):
        query = (part[:, :channels] * scale).astype(BF16)
        key = part[:, channels : 2 * channels].astype(BF16)
        value = part[:, 2 * channels : 3 * channels].astype(BF16)
        scores = dot(by_head(query), key, NT).reshape(heads, query.shape[0], key.shape[0])
        return scores, by_head(value), jax.nn.sigmoid(part[:, 3 * channels :])

    zero_v[...] = msa_zero.reshape(zero_v.shape)
    for s in range(seqs):
        raw_v[s], value_v[s], open_v[s] = split(projected[s * length : (s + 1) * length])
    for load in loads[8:]:
        load.wait()
    tri_t[...] = jnp.transpose(tri_w[:, : 4 * pair_chan].astype(F32), (1, 0)).astype(BF16)
    fill(outer_f, outer_w[...].astype(F32))
    for d in range(width):
        outer_w2[:, d * pair_chan : (d + 1) * pair_chan] = pick(
            outer_f, d, width, width
        ).astype(BF16)

    reach = half * rows
    mine = lax.div(me, half)
    turns = (
        (mine, pl.multiple_of(mine * reach, reach)),
        (1 - mine, pl.multiple_of((1 - mine) * reach, reach)),
    )
    mask_bias = (mask[...].astype(F32) - 1.0) * 10000.0
    row_ones = by_head(jnp.ones((length, channels), BF16))
    lane_parts = channels // 128
    for turn, (which, start) in enumerate(turns):
        if turn == 0:
            gather_forward(0, bias_sem.at[0], bias_land, 7)
        taken(bias_land.at[pl.ds(0, half - 1)], recv_sem.at[7 * turn])
        fill(bias_f, landed(bias_land.at[pl.ds(which * half, half)]))
        extra = jnp.stack([pick(bias_f, h, reach, heads) for h in range(heads)], 0) + mask_bias
        mixed = attend(
            [raw_v[s, :, pl.ds(start, reach), :] + extra for s in range(seqs)],
            [value_v[s] for s in range(seqs)],
            row_ones,
        )
        opened = open_v[:, pl.ds(start, reach), :].reshape(mixed.shape)
        added = dot((opened * mixed).astype(BF16), row_o[...])
        blocks = [
            zero_v[s, pl.ds(start, reach), :] + added[s * reach : (s + 1) * reach]
            for s in range(seqs)
        ]
        ordered = interleave(blocks, rows)
        msa_src[pl.ds(which * half, half)] = jnp.concatenate(
            [ordered[:, :, k * 128 : (k + 1) * 128] for k in range(lane_parts)], 1
        ).astype(BF16)
        if turn == 0:
            msa_land[me] = msa_src[me]
        spread(
            1,
            lambda peer: msa_src.at[peer],
            msa_land.at[me],
            own_half if turn == 0 else other_half,
            1 + 7 * turn,
        )

    share = seqs * half
    to_output = selection(
        total * rows,
        lambda o: (
            split_index(o, rows)[1] * total
            + split_index(o, rows * share)[0] * share
            + split_index(split_index(o, rows)[0], seqs)[1] * half
            + split_index(split_index(o, rows * seqs)[0], half)[1]
        ),
    )
    step = lane_parts * seqs * rows
    for turn, (which, start) in enumerate(turns):
        taken(msa_land.at[pl.ds(0, half - 1 + turn)], recv_sem.at[1 + 7 * turn])
        fill(msa_f, landed(msa_land.at[pl.ds(which * half, half)]))
        column = jnp.concatenate(
            [
                jnp.concatenate(
                    [
                        pick(msa_f, (k * seqs + s) * rows + i, half, step)
                        for i in range(rows)
                        for s in range(seqs)
                    ],
                    0,
                )
                for k in range(lane_parts)
            ],
            1,
        )
        projected = dot(layer_normalized(column).astype(BF16), col_w[...])
        place = pl.ds(pl.multiple_of(which * share, share), share)
        for i in range(rows):
            column_v[i, place, :] = column[i * share : (i + 1) * share]
            project_v[i, place, :] = projected[i * share : (i + 1) * share]
    pack = max(1, 128 // total)
    groups = width // pack
    lanes = pack * total
    column_ones = by_head(jnp.ones((lanes, channels), BF16))
    together = (
        split_index(lax.broadcasted_iota(jnp.int32, (1, lanes, lanes), 1), total)[0]
        == split_index(lax.broadcasted_iota(jnp.int32, (1, lanes, lanes), 2), total)[0]
    )
    two_rows, inputs = [], []
    for start in range(0, rows, pack):
        block = column_v[start : start + pack].reshape(lanes, channels)
        scores, value, opened = split(
            project_v[start : start + pack].reshape(lanes, 4 * channels)
        )
        if pack > 1:
            scores = jnp.where(together, scores, -1e30)
        gated = (opened * attend([scores], [value], column_ones)).astype(BF16)
        msa_two = block + dot(gated, col_o[...])
        outer_input = layer_normalized(msa_two).astype(BF16)
        two_rows.append(msa_two.astype(BF16))
        inputs.append(outer_input)

        right_t = dot(factor_w[width:, :], outer_input, NT)
        slab = jnp.concatenate(pack_lanes(right_t, pack, total), 0).astype(BF16)
        part = (start // pack,)
        right_src[part[0]] = slab
        right_land[me, part[0]] = slab
        gather_start(2, right_sem.at[part[0]], right_src.at[part[0]], right_land, part)

    left = dot(jnp.concatenate(inputs, 0), factor_w[:width, :], NT).astype(BF16)
    chunk = 8
    for start in range(0, width, chunk):
        product = dot(left, outer_w2[:, start * pair_chan : (start + chunk) * pair_chan])
        for d in range(start, start + chunk):
            at = ((d % groups) * pack + d // groups) * total
            for i in range(rows):
                left_t[at : at + total, i * pair_chan : (i + 1) * pair_chan] = product[
                    i * total : (i + 1) * total,
                    (d - start) * pair_chan : (d - start + 1) * pair_chan,
                ].astype(BF16)

    own = pair_chan // half
    fold = max(1, 128 // reach)
    height = pair_chan // fold
    normed = []
    for k in range(rows // pack):
        gather_forward(2, right_sem.at[k], right_land, 6, (k,))
    for turn, (which, start) in enumerate(turns):
        taken(right_land.at[pl.ds(0, half - 1)], recv_sem.at[2 + 4 * turn])
        fill(right_f, landed(right_land.at[pl.ds(which * half, half)]))
        for k in range(groups):
            right_m[:, k * lanes : (k + 1) * lanes] = pick(right_f, k, reach, groups).astype(BF16)
        update = dot(right_m[...], left_t[...]) * (1.0 / total)
        stacked = []
        for i in range(rows):
            one = pair[i, pl.ds(start, reach), :].astype(F32) + update[
                :, i * pair_chan : (i + 1) * pair_chan
            ]
            pair_one_v[i, pl.ds(start, reach), :] = one
            stacked.append(one)
        normed.append(layer_normalized(jnp.concatenate(stacked, 0)).astype(BF16))
        for side, target in ((1, tri_right), (0, tri_left)):
            low = 2 * side * pair_chan
            factors = dot(tri_t[low : low + 2 * pair_chan, :], normed[turn], NT)
            factor = jax.nn.sigmoid(factors[pair_chan:]) * factors[:pair_chan]
            wide = fold * reach
            for base in range(rows // fold):
                packed = pack_lanes(factor[:, base * wide : (base + 1) * wide], fold, reach)
                for place in range(fold):
                    at = (base * fold + place) * height
                    fill(tri_f.at[side, :, pl.ds(at, height), :], packed[place])
            for g in range(half):
                target[turn, g] = pick(
                    tri_f.at[side], g, rows * own // fold, half
                ).astype(BF16)
            if side == 1:
                spread(
                    3,
                    lambda peer: tri_right.at[turn, lax.rem(peer, half)],
                    tri_land.at[which, me],
                    everyone,
                )
            else:
                spread(
                    4,
                    lambda peer: tri_left.at[turn, lax.rem(peer, half)],
                    left_land.at[which, group],
                    own_half,
                )
        left_land[which, group] = tri_left[turn, group]
        tri_land[which, me] = tri_right[turn, group]

    ordered = dot(to_output, jnp.concatenate(two_rows, 0))
    align_out[...] = ordered.reshape(total, rows, channels).astype(BF16)
    for turn in range(2):
        opened = jax.nn.sigmoid(dot(normed[turn], tri_w[:, 4 * pair_chan :]))
        for i in range(rows):
            gate_v[i, pl.ds(turns[turn][1], reach), :] = opened[i * reach : (i + 1) * reach]

    taken(tri_land.at[pl.ds(0, 2), pl.ds(0, count - 1)], recv_sem.at[3])
    taken(left_land.at[pl.ds(0, 2), pl.ds(0, half - 1)], recv_sem.at[4])
    fill(land_f, landed(tri_land))
    fill(left_f, landed(left_land))
    slab_rows = rows * own // fold
    block = half * rows
    lane = lax.broadcasted_iota(jnp.int32, (1, fold * reach), 1)
    folds = [
        jnp.where((lane >= k * reach) & (lane < (k + 1) * reach), 1.0, 0.0).astype(BF16)
        for k in range(fold)
    ]
    for c in range(own // fold):
        step = own // fold
        left_sides = [
            jnp.concatenate(
                [
                    pick(left_f, q * half * slab_rows + i * step + c, half, slab_rows)
                    for i in range(rows)
                ],
                0,
            ).astype(BF16)
            for q in range(2)
        ]
        right_side = jnp.concatenate(
            [pick(land_f, q * count * slab_rows + c, length, step) for q in range(2)], 1
        ).astype(BF16)
        left_side = jnp.concatenate(
            [jnp.concatenate([side * m for side in left_sides], 1) for m in folds], 0
        )
        product = dot(left_side, right_side, NT)
        for k in range(fold):
            fill(
                comb_f.at[:, pl.ds((k * step + c) * block, block), :],
                product[k * block : (k + 1) * block],
            )
    for p in range(half):
        back_src[p] = pick(comb_f, p, own * rows, half).astype(BF16)
    back_land[group] = back_src[group]
    spread(5, lambda peer: back_src.at[lax.rem(peer, half)], back_land.at[group], own_half)

    taken(back_land.at[pl.ds(0, half - 1)], recv_sem.at[5])
    for number, sent in enumerate((bias_land, msa_land, right_land)):
        taken(sent.at[pl.ds(0, count - 1)], send_sem.at[number])
    taken(tri_land.at[pl.ds(0, 2), pl.ds(0, count - 1)], send_sem.at[3])
    taken(left_land.at[pl.ds(0, 2), pl.ds(0, half - 1)], send_sem.at[4])
    taken(back_land.at[pl.ds(0, half - 1)], send_sem.at[5])


def finish_kernel(rows, align, back_land, pair_one, gate, tri_o, align_out, pair_out, back_f, pair_v, sem):
    store_align = pltpu.make_async_copy(align, align_out, sem.at[0])
    store_align.start()
    fill(back_f, landed(back_land))
    owners = back_land.shape[0]
    own = back_land.shape[1] // rows
    combined = jnp.concatenate(
        [
            jnp.concatenate(
                [pick(back_f, c * rows + i, owners, own * rows) for c in range(own)], 0
            )
            for i in range(rows)
        ],
        1,
    )
    added = dot(layer_normalized(combined, 0).astype(BF16), tri_o[...], TN)
    pair_v[...] = (pair_one[...] + gate[...] * added.reshape(gate.shape)).astype(BF16)
    store_pair = pltpu.make_async_copy(pair_v, pair_out, sem.at[1])
    store_pair.start()
    store_align.wait()
    store_pair.wait()


def shards(
    homolog_symbol_ids,
    residue_attend_mask,
    alignment_state,
    pair,
    symbol_lookup_matrix,
    pair_bias_weight,
    row_projection_weight,
    horizontal_readout_matrix,
    column_projection_weight,
    vertical_readout_matrix,
    product_factor_matrices,
    outer_output_weight,
    triangle_input_weight,
    triangle_output_weight,
):
    count = lax.axis_size("res")
    seqs, length, channels = alignment_state.shape
    rows, _, pair_chan = pair.shape
    heads = pair_bias_weight.shape[1]
    width = product_factor_matrices.shape[1] // 2
    total = seqs * count
    half = count // 2
    own = pair_chan // half
    pack = max(1, 128 // total)
    groups, lanes = width // pack, pack * total
    operands = [
        homolog_symbol_ids,
        residue_attend_mask.reshape(1, length),
        alignment_state,
        pair,
        symbol_lookup_matrix,
        pair_bias_weight.T,
        row_projection_weight,
        horizontal_readout_matrix,
        column_projection_weight,
        vertical_readout_matrix,
        product_factor_matrices.T,
        outer_output_weight,
        triangle_input_weight,
    ]
    lane_parts = channels // 128
    vmem = pltpu.VMEM
    parts = rows // pack
    reach = half * rows
    fold = max(1, 128 // reach)
    tri_slab = (rows * own // fold, fold * reach)
    exchanges = [
        vmem((heads * rows, length), BF16),
        vmem((count, heads * rows, length), BF16),
        vmem((count, lane_parts * seqs * rows, 128), BF16),
        vmem((count, lane_parts * seqs * rows, 128), BF16),
        vmem((parts, groups * pack, lanes), BF16),
        vmem((count, parts, groups * pack, lanes), BF16),
        vmem((2, half) + tri_slab, BF16),
        vmem((2, half) + tri_slab, BF16),
        vmem((2, half) + tri_slab, BF16),
        vmem((2, count) + tri_slab, BF16),
        vmem((half, own * rows, length), BF16),
    ]

    def pieces(row_count, lane_count):
        return vmem((lane_count // 128, row_count, 128), F32)

    scratch = (
        [vmem(x.shape, x.dtype) for x in operands]
        + exchanges
        + [
            pieces(half * heads * rows, length),
            pieces(half * lane_parts * seqs * rows, 128),
            pieces(width * width, pair_chan),
            vmem((width, width * pair_chan), BF16),
            vmem((width * total, rows * pair_chan), BF16),
            pieces(reach * groups, lanes),
            vmem((reach, width * total), BF16),
            vmem((4 * pair_chan, pair_chan), BF16),
            vmem((2, fold * reach // 128, rows * pair_chan // fold, 128), F32),
            pieces(2 * count * tri_slab[0], tri_slab[1]),
            pieces(2 * half * tri_slab[0], tri_slab[1]),
            pieces(half * own * rows, length),
            vmem((seqs, length, channels), F32),
            vmem((seqs, heads, length, length), F32),
            vmem((seqs, heads * length, channels), BF16),
            vmem((seqs, length, channels), F32),
            vmem((rows, total, channels), F32),
            vmem((rows, total, 4 * channels), F32),
            pltpu.SemaphoreType.DMA((len(operands),)),
            pltpu.SemaphoreType.DMA((6,)),
            pltpu.SemaphoreType.DMA((9,)),
            pltpu.SemaphoreType.DMA((1,)),
            pltpu.SemaphoreType.DMA((parts,)),
        ]
    )
    sizes = (count, seqs, rows, length, channels, heads, width, pair_chan, total)
    anywhere = pl.BlockSpec(memory_space=pltpu.HBM)
    inside = pl.BlockSpec(memory_space=pltpu.VMEM)
    aligned, back, pair_one, gate = pl.pallas_call(
        functools.partial(block_kernel, sizes),
        out_shape=(
            jax.ShapeDtypeStruct((total, rows, channels), BF16),
            jax.ShapeDtypeStruct((half, own * rows, length), BF16),
            jax.ShapeDtypeStruct(pair.shape, F32),
            jax.ShapeDtypeStruct(pair.shape, F32),
        ),
        in_specs=[anywhere] * len(operands),
        out_specs=(inside,) * 4,
        scratch_shapes=scratch,
        compiler_params=pltpu.CompilerParams(
            collective_id=0, has_side_effects=True, vmem_limit_bytes=VMEM_BYTES
        ),
    )(*[pltpu.with_memory_space_constraint(x, pltpu.HBM) for x in operands])
    return pl.pallas_call(
        functools.partial(finish_kernel, rows),
        out_shape=(
            jax.ShapeDtypeStruct((total, rows, channels), BF16),
            jax.ShapeDtypeStruct(pair.shape, BF16),
        ),
        in_specs=[inside] * 5,
        out_specs=(anywhere, anywhere),
        scratch_shapes=[
            pieces(half * own * rows, length),
            vmem(pair.shape, BF16),
            pltpu.SemaphoreType.DMA((2,)),
        ],
        compiler_params=pltpu.CompilerParams(vmem_limit_bytes=VMEM_BYTES // 4),
    )(aligned, back, pair_one, gate, triangle_output_weight)


def solution(mesh):
    placed = (
        P(("crop", "res"), None),
        P("crop"),
        P(("crop", "res"), None, None),
        P(("crop", "res"), None, None),
        P(),
        P(),
        P(),
        P(),
        P(),
        P(),
        P(),
        P(),
        P(),
        P(),
    )
    return jax.shard_map(
        shards,
        mesh=mesh,
        in_specs=placed,
        out_specs=(P("crop", "res", None), P(("crop", "res"), None, None)),
        check_vma=False,
    )
```
